32 devices in a mesh: fsdp: 16 (over z, y, core), tp: 2 (over x).
Axes of the slice: x: 2, y: 2, z: 4, core: 2. Of those that a mesh axis runs over, the one named last changes fastest.
Arguments:
- frames: bfloat16 [16, 1504, 1280], P('fsdp', 'tp'), may hold values from -6 to 6
- out_grad: bfloat16 [16, 1504, 1280], P('fsdp', 'tp'), may hold values from -6 to 6
- clip_lengths: int32 [16], replicated, may hold values from 1 to 1504, 18048 in all
- clip_order: int32 [16], replicated, may hold values from 0 to 15, each once
- w_query: bfloat16 [1280, 1280], P('fsdp', 'tp'), may hold values from -0.25 to 0.25
- w_key: bfloat16 [1280, 1280], P('fsdp', 'tp'), may hold values from -0.25 to 0.25
- w_value: bfloat16 [1280, 1280], P('fsdp', 'tp'), may hold values from -0.15625 to 0.15625
- b_query: bfloat16 [1280], P(('tp', 'fsdp')), may hold values from -3 to 3
- b_value: bfloat16 [1280], P(('tp', 'fsdp')), may hold values from -0.1796875 to 0.1796875
- w_out: bfloat16 [1280, 1280], P('tp', 'fsdp'), may hold values from -1.75 to 1.75
- b_out: bfloat16 [1280], P(('fsdp', 'tp')), may hold values from -3 to 3
- w_expand: bfloat16 [1280, 5120], P('fsdp', 'tp'), may hold values from -0.15625 to 0.15625
- b_expand: bfloat16 [5120], P(('tp', 'fsdp')), may hold values from -3 to 3
- w_reduce: bfloat16 [5120, 1280], P('tp', 'fsdp'), may hold values from -0.078125 to 0.078125
- b_reduce: bfloat16 [1280], P(('fsdp', 'tp')), may hold values from -3 to 3
- first_gain: bfloat16 [1280], P(('fsdp', 'tp')), may hold values from 0.099609375 to 1.8984375
- first_shift: bfloat16 [1280], P(('fsdp', 'tp')), may hold values from -2 to 2
- second_gain: bfloat16 [1280], P(('fsdp', 'tp')), may hold values from 0.099609375 to 1.8984375
- second_shift: bfloat16 [1280], P(('fsdp', 'tp')), may hold values from -2 to 2
Outputs:
- out_frames: bfloat16 [16, 1504, 1280], P('fsdp', 'tp')
- frames_grad: bfloat16 [16, 1504, 1280], P('fsdp', 'tp')
- w_query_grad: float32 [1280, 1280], P('fsdp', 'tp')
- w_key_grad: float32 [1280, 1280], P('fsdp', 'tp')
- w_value_grad: float32 [1280, 1280], P('fsdp', 'tp')
- b_query_grad: float32 [1280], P(('tp', 'fsdp'))
- b_value_grad: float32 [1280], P(('tp', 'fsdp'))
- w_out_grad: float32 [1280, 1280], P('tp', 'fsdp')
- b_out_grad: float32 [1280], P(('fsdp', 'tp'))
- w_expand_grad: float32 [1280, 5120], P('fsdp', 'tp')
- b_expand_grad: float32 [5120], P(('tp', 'fsdp'))
- w_reduce_grad: float32 [5120, 1280], P('tp', 'fsdp')
- b_reduce_grad: float32 [1280], P(('fsdp', 'tp'))
- first_gain_grad: float32 [1280], P(('fsdp', 'tp'))
- first_shift_grad: float32 [1280], P(('fsdp', 'tp'))
- second_gain_grad: float32 [1280], P(('fsdp', 'tp'))
- second_shift_grad: float32 [1280], P(('fsdp', 'tp'))
The draws below stay inside these ranges and needn't reach their ends.
Inputs may be any that keep to these rules, and one draw needn't show every extreme that they name: `clip_lengths`: frames of each clip that keys may come from; they sum to 18048. `clip_order`: each clip stands in exactly one slot.
All inputs are finite; a program needn't handle non-finite values.
Results may differ from the reference program's by a relative error of at most 0.02.
Values may be sent and summed in bfloat16 or wider, within the bound.
No kernel may reach another device: no remote copies, remote signals or barrier semaphores. Data moves between devices by JAX's collectives and lax.ppermute only.
A program may use at most 448 MiB of HBM per device.

```python
import math
import jax
import jax.numpy as jnp
import numpy as np
from jax import lax

D = 1280
HEADS = 16
HD = 80
FF = 5120
SEQ = 1504
CLIPS = 16


def with_spikes(values, own_key, source, target, shards_of, factor):
    def block_of(position):
        return (jnp.arange(values.shape[position]) // (values.shape[position] // shards_of)).reshape((-1,) + (1,) * (values.ndim - 1 - position))

    one_side = jax.random.permutation(own_key, shards_of)[block_of(target)]
    far = (block_of(target) + shards_of // 2) % shards_of
    return jnp.where((block_of(source) == one_side) | (block_of(source) == far), factor * values, values)


def shard_levels(rng, dims, pieces, smallest, largest):
    level = 1.0
    for dim, parts in pieces:
        draws = jax.random.uniform(jax.random.fold_in(jax.random.fold_in(rng, 6), dim), (parts,), jnp.float32, smallest / len(pieces), largest / len(pieces))
        level = level * jnp.repeat(jnp.exp(draws), dims[dim] // parts).reshape((-1,) + (1,) * (len(dims) - 1 - dim))
    return level


def length_profile(count, total, most, lean):
    weights = [(1 << 20) // math.isqrt(grade ** lean) + 1 for grade in range(2, count + 1)]
    rest, counts = total - most - (count - 1), [1] * (count - 1)
    while rest > 0:
        candidates = [i for i in range(count - 1) if counts[i] < most]
        mass, budget = sum([weights[i] for i in candidates]), rest
        for i in candidates:
            extra = min(most - counts[i], max(1, budget * weights[i] // mass), rest)
            counts[i] = counts[i] + extra
            rest = rest - extra
    return np.array([most] + counts)


def uneven(stream_key, number_of, total, reach, lean):
    if number_of == 2:
        one = jax.random.randint(stream_key, (), max(1, total - reach), min(reach, total - 1) + 1)
        return jnp.stack([one, total - one])
    tallies = jnp.asarray(length_profile(number_of, total, reach, lean), jnp.int32)
    twos = (number_of - 1) // 2
    source_of, sink = tallies[1:1 + 2 * twos:2], tallies[2:2 + 2 * twos:2]
    slack = jnp.minimum(source_of - 1, reach - sink)
    shifted = jax.random.randint(jax.random.fold_in(stream_key, 1), (twos,), 0, 1 << 20) % (slack + 1)
    tallies = tallies.at[1:1 + 2 * twos:2].set(source_of - shifted).at[2:2 + 2 * twos:2].set(sink + shifted)
    return tallies[jax.random.permutation(jax.random.fold_in(stream_key, 2), number_of)]


def scatter_about(rng, dims, deviation, reach, split=(), held_as=jnp.bfloat16):
    level = shard_levels(rng, dims, split, -0.22, 0.18) if split else 1.0
    drawn = jax.random.normal(rng, dims, jnp.float32) * deviation * level
    return jnp.minimum(jnp.maximum(drawn, -reach), reach).astype(held_as)


def bell_draw_with(stream_key, extent, width, limit, shards, heavy, kind=jnp.bfloat16):
    values = width * jax.random.normal(stream_key, extent, jnp.float32)
    if shards:
        values = values * shard_levels(stream_key, extent, shards, -0.22, 0.18)
    return jnp.clip(with_spikes(values, jax.random.fold_in(stream_key, 3), *heavy), -limit, limit).astype(kind)


def setup_inputs(seed: int = 0) -> dict:
    seeds = jax.random.split(jax.random.key(seed), 20)
    return {
        "frames": scatter_about(seeds[0], (CLIPS, SEQ, D), 1.0, 6.0, ((0, 16), (1, 2))),
        "out_grad": bell_draw_with(seeds[1], (CLIPS, SEQ, D), 1.0, 6.0, ((0, 16), (1, 2)), (0, 2, 16, 2.0)),
        "clip_lengths": uneven(seeds[2], CLIPS, CLIPS * SEQ * 3 // 4, SEQ, 2).astype(jnp.int32),
        "clip_order": jax.random.permutation(seeds[3], CLIPS).astype(jnp.int32),
        "w_query": scatter_about(seeds[4], (D, D), (D // 2) ** -0.5, 0.25, ((0, 16), (1, 2))),
        "w_key": scatter_about(seeds[5], (D, D), (D // 2) ** -0.5, 0.25, ((0, 16), (1, 2))),
        "w_value": scatter_about(seeds[6], (D, D), D ** -0.5, 0.15625, ((0, 16), (1, 2))),
        "b_query": scatter_about(seeds[7], (D,), 0.5, 3.0, ((0, 32),)),
        "b_value": scatter_about(seeds[8], (D,), 0.03, 0.1796875, ((0, 32),)),
        "w_out": scatter_about(seeds[9], (D, D), (max(1, D * 16 // SEQ)) ** -0.5, 1.75, ((0, 2), (1, 16))),
        "b_out": scatter_about(seeds[10], (D,), 0.5, 3.0, ((0, 32),)),
        "w_expand": scatter_about(seeds[11], (D, FF), D ** -0.5, 0.15625, ((0, 16), (1, 2))),
        "b_expand": scatter_about(seeds[12], (FF,), 0.5, 3.0, ((0, 32),)),
        "w_reduce": scatter_about(seeds[13], (FF, D), FF ** -0.5, 0.078125, ((0, 2), (1, 16))),
        "b_reduce": scatter_about(seeds[14], (D,), 0.5, 3.0, ((0, 32),)),
        "first_gain": jnp.clip(1.0 + 0.18 * jax.random.normal(seeds[15], (D,), jnp.float32), 0.099609375, 1.8984375).astype(jnp.bfloat16),
        "first_shift": scatter_about(seeds[16], (D,), 0.3, 2.0, ((0, 32),)),
        "second_gain": jnp.clip(1.0 + 0.18 * jax.random.normal(seeds[17], (D,), jnp.float32), 0.099609375, 1.8984375).astype(jnp.bfloat16),
        "second_shift": scatter_about(seeds[18], (D,), 0.3, 2.0, ((0, 32),)),
    }


PRECISE = lax.Precision.HIGHEST
EPSILON = 1e-05
MASKED = -1000000000.0

@jax.custom_vjp
def low(v):
    return lax.optimization_barrier(v.astype(jnp.bfloat16)).astype(jnp.float32)

@jax.custom_vjp
def low_back(v):
    return v

def low_keep(v):
    return (low(v), None)

def low_pass(kept, grad):
    return (grad,)

def back_keep(v):
    return (v, None)

def back_low(kept, grad):
    return (low(grad),)
low.defvjp(low_keep, low_pass)
low_back.defvjp(back_keep, back_low)

def layer_norm(features, norm_gain, norm_shift):
    row_mean = lax.optimization_barrier(jnp.mean(features, axis=-1, keepdims=True))
    centred = features - row_mean
    row_var = lax.optimization_barrier(jnp.mean(centred * centred, axis=-1, keepdims=True))
    return centred * lax.rsqrt(row_var + EPSILON) * norm_gain + norm_shift

def matmul(left, right):
    return jnp.dot(left, right, precision=PRECISE)

def forward(frames_row, length, w_query, w_key, w_value, b_query, b_value, w_out, b_out, w_expand, b_expand, w_reduce, b_reduce, first_gain, first_shift, second_gain, second_shift):
    seq_len = frames_row.shape[0]
    first_rows = low(layer_norm(frames_row, first_gain, first_shift))
    queries = low(low_back((matmul(first_rows, w_query) + b_query) * HD ** (-0.5)))
    keys = low(low_back(matmul(first_rows, w_key)))
    values = low(low_back(matmul(first_rows, w_value) + b_value))
    query_heads = queries.reshape(seq_len, HEADS, HD)
    key_heads = keys.reshape(seq_len, HEADS, HD)
    value_heads = values.reshape(seq_len, HEADS, HD)
    scores = low_back(jnp.einsum('qhe,khe->hqk', query_heads, key_heads, precision=PRECISE))
    allowed = jnp.arange(seq_len) < length
    scores = jnp.where(allowed[None, None, :], scores, MASKED)
    weights = low(jax.nn.softmax(scores, axis=-1))
    context = low(low_back(jnp.einsum('hqk,khe->qhe', weights, value_heads, precision=PRECISE)))
    context = context.reshape(seq_len, HEADS * HD)
    middle = frames_row + low_back(matmul(context, w_out) + b_out)
    second_rows = low(layer_norm(middle, second_gain, second_shift))
    expanded = low_back(matmul(second_rows, w_expand) + b_expand)
    hidden = low(jax.nn.gelu(expanded, approximate=False))
    return middle + low_back(matmul(hidden, w_reduce) + b_reduce)

def reference(frames, out_grad, clip_lengths, clip_order, w_query, w_key, w_value, b_query, b_value, w_out, b_out, w_expand, b_expand, w_reduce, b_reduce, first_gain, first_shift, second_gain, second_shift):
    params = tuple((tensor.astype(jnp.float32) for tensor in (w_query, w_key, w_value, b_query, b_value, w_out, b_out, w_expand, b_expand, w_reduce, b_reduce, first_gain, first_shift, second_gain, second_shift)))
    slot_lengths = clip_lengths[clip_order].astype(jnp.int32)

    def one_clip(totals, inputs):
        frames_row, grad_row, length = inputs

        def run_layer(frames_in, *weight_list):
            return forward(frames_in, length, *weight_list)
        result, pullback = jax.vjp(run_layer, frames_row.astype(jnp.float32), *params)
        gradients = pullback(grad_row.astype(jnp.float32))
        totals = tuple((running + update for running, update in zip(totals, gradients[1:])))
        return (totals, (result.astype(jnp.bfloat16), gradients[0].astype(jnp.bfloat16)))
    initial = tuple((jnp.zeros_like(tensor) for tensor in params))
    totals, outputs = lax.scan(one_clip, initial, (frames, out_grad, slot_lengths))
    out_frames, frames_grad = outputs
    return (out_frames, frames_grad, totals[0], totals[1], totals[2], totals[3], totals[4], totals[5], totals[6], totals[7], totals[8], totals[9], totals[10], totals[11], totals[12], totals[13], totals[14])
```

```python
import functools

import jax
import jax.numpy as jnp
from jax import lax
from jax.experimental import pallas as pl
from jax.experimental.pallas import tpu as pltpu
from jax.sharding import PartitionSpec as P

HD = 80


EPSILON = 1e-05
MASKED = -1000000000.0
HIDDEN = -1e30


def layer_norm(features, norm_gain, norm_shift):
    row_mean = jnp.mean(features, axis=-1, keepdims=True)
    centred = features - row_mean
    row_var = jnp.mean(centred * centred, axis=-1, keepdims=True)
    inverse = lax.rsqrt(row_var + EPSILON)
    normed = centred * inverse
    return (normed * norm_gain + norm_shift, normed, inverse)


def norm_back(upstream, normed, inverse, norm_gain):
    tilted = upstream * norm_gain
    return inverse * (
        tilted
        - jnp.mean(tilted, axis=-1, keepdims=True)
        - normed * jnp.mean(tilted * normed, axis=-1, keepdims=True)
    )


def gelu_exact(inputs):
    return jax.nn.gelu(inputs, approximate=False)


def masked_scores(queries, key_rows, length):
    scores = jnp.einsum("qhe,khe->hqk", queries, key_rows, preferred_element_type=jnp.float32)
    allowed = jnp.arange(scores.shape[-1]) < length
    return jnp.where(allowed[None, None, :], scores, MASKED)


def attend(inputs):
    queries, key_rows, value_rows, length = inputs
    scores = masked_scores(queries, key_rows, length)
    row_top = jnp.max(scores, axis=-1, keepdims=True)
    raised = jnp.exp(scores - row_top)
    row_sum = jnp.sum(raised, axis=-1, keepdims=True)
    weights = (raised / row_sum).astype(jnp.bfloat16)
    context = jnp.einsum("hqk,khe->qhe", weights, value_rows, preferred_element_type=jnp.float32)
    return (context.astype(jnp.bfloat16), row_top[..., 0] + jnp.log(row_sum[..., 0]))


def attend_back(inputs):
    queries, key_rows, value_rows, length, log_total, context_grad = inputs
    scores = masked_scores(queries, key_rows, length)
    probs = jnp.exp(scores - log_total[..., None])
    weights = probs.astype(jnp.bfloat16)
    value_grad = jnp.einsum(
        "hqk,qhe->khe", weights, context_grad, preferred_element_type=jnp.float32
    )
    weight_grad = jnp.einsum(
        "qhe,khe->hqk", context_grad, value_rows, preferred_element_type=jnp.float32
    )
    row_inner = jnp.sum(weight_grad * probs, axis=-1, keepdims=True)
    score_grad = (probs * (weight_grad - row_inner)).astype(jnp.bfloat16)
    query_grad = jnp.einsum(
        "hqk,khe->qhe", score_grad, key_rows, preferred_element_type=jnp.float32
    )
    key_grad = jnp.einsum("hqk,qhe->khe", score_grad, queries, preferred_element_type=jnp.float32)
    return (
        query_grad.astype(jnp.bfloat16),
        key_grad.astype(jnp.bfloat16),
        value_grad.astype(jnp.bfloat16),
    )


def gather_inward(w_query, w_key, w_value, b_query, b_value, w_expand, b_expand):
    return (
        lax.all_gather(w_query, "fsdp", axis=0, tiled=True),
        lax.all_gather(w_key, "fsdp", axis=0, tiled=True),
        lax.all_gather(w_value, "fsdp", axis=0, tiled=True),
        lax.all_gather(b_query, "fsdp", axis=0, tiled=True),
        lax.all_gather(b_value, "fsdp", axis=0, tiled=True),
        lax.all_gather(w_expand, "fsdp", axis=0, tiled=True),
        lax.all_gather(b_expand, "fsdp", axis=0, tiled=True),
    )


def gather_outward(w_out, w_reduce):
    return (
        lax.all_gather(w_out, "fsdp", axis=1, tiled=True),
        lax.all_gather(w_reduce, "fsdp", axis=1, tiled=True),
    )


def per_device(
    frames,
    out_grad,
    clip_lengths,
    clip_order,
    w_query,
    w_key,
    w_value,
    b_query,
    b_value,
    w_out,
    b_out,
    w_expand,
    b_expand,
    w_reduce,
    b_reduce,
    first_gain,
    first_shift,
    second_gain,
    second_shift,
):
    per_group = frames.shape[0]
    clip_count = clip_order.shape[0]
    slot_ids = lax.axis_index("fsdp") * per_group + jnp.arange(per_group, dtype=jnp.int32)
    every_clip = jnp.arange(clip_count, dtype=jnp.int32)
    clip_ids = jnp.sum(
        jnp.where(every_clip[None, :] == slot_ids[:, None], clip_order[None, :], 0), axis=1
    )
    lengths = jnp.sum(
        jnp.where(every_clip[None, :] == clip_ids[:, None], clip_lengths[None, :], 0), axis=1
    )
    norm_params = (
        lax.all_gather(first_gain, ("fsdp", "tp"), axis=0, tiled=True),
        lax.all_gather(first_shift, ("fsdp", "tp"), axis=0, tiled=True),
        lax.all_gather(second_gain, ("fsdp", "tp"), axis=0, tiled=True),
        lax.all_gather(second_shift, ("fsdp", "tp"), axis=0, tiled=True),
        lax.all_gather(b_out, ("fsdp", "tp"), axis=0, tiled=True),
        lax.all_gather(b_reduce, ("fsdp", "tp"), axis=0, tiled=True),
    )
    gain_one, shift_one, gain_two, shift_two, out_bias, reduce_bias = [
        tensor.astype(jnp.float32) for tensor in norm_params
    ]
    wq_all, wk_all, wv_all, bq_all, bv_all, we_all, be_all = gather_inward(
        w_query, w_key, w_value, b_query, b_value, w_expand, b_expand
    )
    wo_all, wr_all = gather_outward(w_out, w_reduce)
    q_factor = HD ** (-0.5)
    frames_wide = frames.astype(jnp.float32)
    norm_one, normed_one, inverse_one = layer_norm(frames_wide, gain_one, shift_one)
    first_rows = lax.all_gather(norm_one.astype(jnp.bfloat16), "tp", axis=1, tiled=True)
    seq_len = first_rows.shape[1]
    queries = (
        (
            jnp.einsum("csd,de->cse", first_rows, wq_all, preferred_element_type=jnp.float32)
            + bq_all.astype(jnp.float32)
        )
        * q_factor
    ).astype(jnp.bfloat16)
    keys = jnp.einsum("csd,de->cse", first_rows, wk_all, preferred_element_type=jnp.float32).astype(
        jnp.bfloat16
    )
    values = (
        jnp.einsum("csd,de->cse", first_rows, wv_all, preferred_element_type=jnp.float32)
        + bv_all.astype(jnp.float32)
    ).astype(jnp.bfloat16)
    head_shape = (per_group, seq_len, -1, HD)
    query_heads = queries.reshape(head_shape)
    key_heads = keys.reshape(head_shape)
    value_heads = values.reshape(head_shape)
    context, log_total = lax.map(attend, (query_heads, key_heads, value_heads, lengths))
    context_flat = context.reshape(per_group, seq_len, -1)
    attn_terms = jnp.einsum("cse,ed->csd", context_flat, wo_all, preferred_element_type=jnp.float32)
    attn_part = lax.psum_scatter(
        attn_terms.astype(jnp.bfloat16), "tp", scatter_dimension=1, tiled=True
    ).astype(jnp.float32)
    middle = frames_wide + attn_part + out_bias
    norm_two, normed_two, inverse_two = layer_norm(middle, gain_two, shift_two)
    second_rows = lax.all_gather(norm_two.astype(jnp.bfloat16), "tp", axis=1, tiled=True)
    expanded = jnp.einsum(
        "csd,df->csf", second_rows, we_all, preferred_element_type=jnp.float32
    ) + be_all.astype(jnp.float32)
    activated, gelu_pull = jax.vjp(gelu_exact, expanded)
    hidden = activated.astype(jnp.bfloat16)
    mlp_terms = jnp.einsum("csf,fd->csd", hidden, wr_all, preferred_element_type=jnp.float32)
    out_frames = (
        middle
        + lax.psum_scatter(
            mlp_terms.astype(jnp.bfloat16), "tp", scatter_dimension=1, tiled=True
        ).astype(jnp.float32)
        + reduce_bias
    ).astype(jnp.bfloat16)
    wq_all, wk_all, wv_all, bq_all, bv_all, we_all, be_all = gather_inward(
        w_query, w_key, w_value, b_query, b_value, w_expand, b_expand
    )
    wo_all, wr_all = gather_outward(w_out, w_reduce)
    grad_wide = out_grad.astype(jnp.float32)
    grad_rows = lax.all_gather(out_grad, "tp", axis=1, tiled=True)
    w_reduce_grad = jnp.einsum("csf,csd->fd", hidden, grad_rows, preferred_element_type=jnp.float32)
    hidden_grad = jnp.einsum("csd,fd->csf", grad_rows, wr_all, preferred_element_type=jnp.float32)
    expanded_grad = gelu_pull(hidden_grad)[0].astype(jnp.bfloat16)
    b_expand_grad = jnp.sum(expanded_grad.astype(jnp.float32), axis=(0, 1))
    w_expand_grad = jnp.einsum(
        "csd,csf->df", second_rows, expanded_grad, preferred_element_type=jnp.float32
    )
    second_terms = jnp.einsum(
        "csf,df->csd", expanded_grad, we_all, preferred_element_type=jnp.float32
    )
    second_grad = lax.psum_scatter(
        second_terms.astype(jnp.bfloat16), "tp", scatter_dimension=1, tiled=True
    ).astype(jnp.float32)
    second_gain_grad = jnp.sum(second_grad * normed_two, axis=(0, 1))
    second_shift_grad = jnp.sum(second_grad, axis=(0, 1))
    middle_grad = grad_wide + norm_back(second_grad, normed_two, inverse_two, gain_two)
    branch_grad = middle_grad.astype(jnp.bfloat16)
    b_out_grad = jnp.sum(branch_grad.astype(jnp.float32), axis=(0, 1))
    b_reduce_grad = jnp.sum(grad_wide, axis=(0, 1))
    branch_rows = lax.all_gather(branch_grad, "tp", axis=1, tiled=True)
    w_out_grad = jnp.einsum(
        "cse,csd->ed", context_flat, branch_rows, preferred_element_type=jnp.float32
    )
    context_grad = jnp.einsum(
        "csd,ed->cse", branch_rows, wo_all, preferred_element_type=jnp.float32
    ).astype(jnp.bfloat16)
    query_grad, key_grad, value_grad = lax.map(
        attend_back,
        (query_heads, key_heads, value_heads, lengths, log_total, context_grad.reshape(head_shape)),
    )
    query_grad = query_grad.reshape(per_group, seq_len, -1)
    key_grad = key_grad.reshape(per_group, seq_len, -1)
    value_grad = value_grad.reshape(per_group, seq_len, -1)
    w_query_grad = (
        jnp.einsum("csd,cse->de", first_rows, query_grad, preferred_element_type=jnp.float32)
        * q_factor
    )
    b_query_grad = jnp.sum(query_grad.astype(jnp.float32), axis=(0, 1)) * q_factor
    w_key_grad = jnp.einsum("csd,cse->de", first_rows, key_grad, preferred_element_type=jnp.float32)
    w_value_grad = jnp.einsum(
        "csd,cse->de", first_rows, value_grad, preferred_element_type=jnp.float32
    )
    b_value_grad = jnp.sum(value_grad.astype(jnp.float32), axis=(0, 1))
    first_terms = (
        jnp.einsum("cse,de->csd", query_grad, wq_all, preferred_element_type=jnp.float32) * q_factor
        + jnp.einsum("cse,de->csd", key_grad, wk_all, preferred_element_type=jnp.float32)
        + jnp.einsum("cse,de->csd", value_grad, wv_all, preferred_element_type=jnp.float32)
    )
    first_grad = lax.psum_scatter(
        first_terms.astype(jnp.bfloat16), "tp", scatter_dimension=1, tiled=True
    ).astype(jnp.float32)
    first_gain_grad = jnp.sum(first_grad * normed_one, axis=(0, 1))
    first_shift_grad = jnp.sum(first_grad, axis=(0, 1))
    frames_grad = (middle_grad + norm_back(first_grad, normed_one, inverse_one, gain_one)).astype(
        jnp.bfloat16
    )
    inward_grads = (
        lax.psum_scatter(
            w_query_grad.astype(jnp.bfloat16), "fsdp", scatter_dimension=0, tiled=True
        ).astype(jnp.float32),
        lax.psum_scatter(
            w_key_grad.astype(jnp.bfloat16), "fsdp", scatter_dimension=0, tiled=True
        ).astype(jnp.float32),
        lax.psum_scatter(
            w_value_grad.astype(jnp.bfloat16), "fsdp", scatter_dimension=0, tiled=True
        ).astype(jnp.float32),
        lax.psum_scatter(
            b_query_grad.astype(jnp.bfloat16), "fsdp", scatter_dimension=0, tiled=True
        ).astype(jnp.float32),
        lax.psum_scatter(
            b_value_grad.astype(jnp.bfloat16), "fsdp", scatter_dimension=0, tiled=True
        ).astype(jnp.float32),
        lax.psum_scatter(
            w_expand_grad.astype(jnp.bfloat16), "fsdp", scatter_dimension=0, tiled=True
        ).astype(jnp.float32),
        lax.psum_scatter(
            b_expand_grad.astype(jnp.bfloat16), "fsdp", scatter_dimension=0, tiled=True
        ).astype(jnp.float32),
    )
    outward_grads = (
        lax.psum_scatter(
            w_out_grad.astype(jnp.bfloat16), "fsdp", scatter_dimension=1, tiled=True
        ).astype(jnp.float32),
        lax.psum_scatter(
            w_reduce_grad.astype(jnp.bfloat16), "fsdp", scatter_dimension=1, tiled=True
        ).astype(jnp.float32),
    )
    small_grads = (
        lax.psum_scatter(first_gain_grad, ("fsdp", "tp"), scatter_dimension=0, tiled=True),
        lax.psum_scatter(first_shift_grad, ("fsdp", "tp"), scatter_dimension=0, tiled=True),
        lax.psum_scatter(second_gain_grad, ("fsdp", "tp"), scatter_dimension=0, tiled=True),
        lax.psum_scatter(second_shift_grad, ("fsdp", "tp"), scatter_dimension=0, tiled=True),
        lax.psum_scatter(b_out_grad, ("fsdp", "tp"), scatter_dimension=0, tiled=True),
        lax.psum_scatter(b_reduce_grad, ("fsdp", "tp"), scatter_dimension=0, tiled=True),
    )
    return (
        out_frames,
        frames_grad,
        inward_grads[0],
        inward_grads[1],
        inward_grads[2],
        inward_grads[3],
        inward_grads[4],
        outward_grads[0],
        small_grads[4],
        inward_grads[5],
        inward_grads[6],
        outward_grads[1],
        small_grads[5],
        small_grads[0],
        small_grads[1],
        small_grads[2],
        small_grads[3],
    )


VMEM_LIMIT = 60 << 20
PAD = 128


def kernel_params():
    return pltpu.CompilerParams(vmem_limit_bytes=VMEM_LIMIT)


def cost(flops, moved):
    return pl.CostEstimate(flops=int(flops), bytes_accessed=int(moved), transcendentals=0)


def row_pieces(rows, size):
    return [(start, min(size, rows - start)) for start in range(0, rows, size)]


def whole(shape, fixed=None):
    index = fixed if fixed is not None else (0,) * len(shape)
    return pl.BlockSpec(shape, lambda *_: index)


def normalise(rows):
    row_mean = jnp.mean(rows, axis=-1, keepdims=True)
    centred = rows - row_mean
    inverse = lax.rsqrt(jnp.mean(centred * centred, axis=-1, keepdims=True) + EPSILON)
    return centred * inverse, inverse


def dot_nn(left, right):
    return jnp.dot(left, right, preferred_element_type=jnp.float32)


def dot_nt(left, right):
    return lax.dot_general(left, right, (((1,), (1,)), ((), ())), preferred_element_type=jnp.float32)


def dot_tn(left, right):
    return lax.dot_general(left, right, (((0,), (0,)), ((), ())), preferred_element_type=jnp.float32)


def project_kernel(
    heads, scal_ref, frames_ref, gain_ref, shift_ref, weight_ref, bq_ref, bv_ref,
    first_ref, q_ref, k_ref, v_ref,
):
    rows, width = frames_ref.shape
    cols = heads * HD
    length, start = scal_ref[0], scal_ref[1]
    q_factor = HD ** (-0.5)
    pieces = row_pieces(rows, 256)

    def norm(piece):
        normed, _ = normalise(frames_ref[piece[0] : piece[0] + piece[1], :].astype(jnp.float32))
        first = (normed * gain_ref[...] + shift_ref[...]).astype(jnp.bfloat16)
        first_ref[piece[0] : piece[0] + piece[1], :] = first
        return first

    def split(block, offset, filler, lane):
        if offset + PAD <= block.shape[1]:
            part = block[:, offset : offset + PAD]
        else:
            back = block.shape[1] - PAD
            part = pltpu.roll(block[:, back:], PAD - (offset - back), 1)
        return jnp.where(lane < HD, part, filler).astype(jnp.bfloat16)

    def finish(piece, out):
        lane = lax.broadcasted_iota(jnp.int32, (piece[1], PAD), 1)
        position = lax.broadcasted_iota(jnp.int32, (piece[1], PAD), 0) + (start + piece[0])
        one = jnp.where(lane == HD, 1.0, 0.0)
        hide = jnp.where((lane == HD) & (position >= length), HIDDEN, 0.0)
        queries = (out[:, :cols] + bq_ref[...]) * q_factor
        keys = out[:, cols : 2 * cols]
        values = out[:, 2 * cols :] + bv_ref[...]
        for head in range(heads):
            where = (head, slice(piece[0], piece[0] + piece[1]), slice(None))
            q_ref[where] = split(queries, head * HD, one, lane)
            k_ref[where] = split(keys, head * HD, hide, lane)
            v_ref[where] = split(values, head * HD, 0.0, lane)

    first = norm(pieces[0])
    for number, piece in enumerate(pieces):
        out = dot_nn(first, weight_ref[...])
        if number + 1 < len(pieces):
            first = norm(pieces[number + 1])
        finish(piece, out)


def project(scalars, frames, gain, shift, weights, bias_q, bias_v, heads):
    rows, width = frames.shape
    cols = heads * HD
    head_out = jax.ShapeDtypeStruct((heads, rows, PAD), jnp.bfloat16)
    return pl.pallas_call(
        functools.partial(project_kernel, heads),
        out_shape=(jax.ShapeDtypeStruct((rows, width), jnp.bfloat16), head_out, head_out, head_out),
        grid_spec=pltpu.PrefetchScalarGridSpec(
            num_scalar_prefetch=1,
            grid=(1,),
            in_specs=[
                whole((rows, width)), whole((1, width)), whole((1, width)),
                whole((width, 3 * cols)), whole((1, cols)), whole((1, cols)),
            ],
            out_specs=(whole((rows, width)),) + (whole((heads, rows, PAD)),) * 3,
        ),
        compiler_params=kernel_params(),
        cost_estimate=cost(2 * rows * width * 3 * cols, 4 * rows * width + 6 * width * cols),
        name="project",
    )(scalars, frames, gain, shift, weights, bias_q, bias_v)


def attend_kernel(q_ref, ko_ref, kt_ref, vo_ref, vt_ref, out_ref, log_ref):
    per_step, rows, _ = q_ref.shape
    half = -(-rows // 256) * 128
    pieces = [(head, start, size) for head in range(per_step) for start, size in row_pieces(rows, half)]
    keys = [jnp.concatenate([ko_ref[h], kt_ref[h]], axis=0) for h in range(per_step)]
    values = [jnp.concatenate([vo_ref[h], vt_ref[h]], axis=0).T[:HD] for h in range(per_step)]

    def scores(piece):
        head, start, size = piece
        return dot_nt(keys[head], q_ref[head, start : start + size, :])

    def finish(piece, score):
        head, start, size = piece
        top = jnp.max(score, axis=0, keepdims=True)
        raised = jnp.exp(score - top)
        total = jnp.sum(raised, axis=0, keepdims=True)
        context = dot_nn(values[head], raised.astype(jnp.bfloat16)) / total
        out_ref[head, :, start : start + size] = context.astype(jnp.bfloat16)
        log_ref[head, :, start : start + size] = top + jnp.log(total)

    current = scores(pieces[0])
    for number, piece in enumerate(pieces):
        coming = scores(pieces[number + 1]) if number + 1 < len(pieces) else None
        finish(piece, current)
        current = coming


def attend_rows(queries, keys_own, keys_far, values_own, values_far):
    heads, rows, _ = queries.shape
    per_step = 2 if heads % 2 == 0 else 1
    spec = pl.BlockSpec((per_step, rows, PAD), lambda h: (h, 0, 0))
    return pl.pallas_call(
        attend_kernel,
        out_shape=(
            jax.ShapeDtypeStruct((heads, HD, rows), jnp.bfloat16),
            jax.ShapeDtypeStruct((heads, 1, rows), jnp.float32),
        ),
        grid=(heads // per_step,),
        in_specs=[spec] * 5,
        out_specs=(
            pl.BlockSpec((per_step, HD, rows), lambda h: (h, 0, 0)),
            pl.BlockSpec((per_step, 1, rows), lambda h: (h, 0, 0)),
        ),
        compiler_params=kernel_params(),
        cost_estimate=cost(heads * 2 * rows * 2 * rows * 2 * 400, heads * rows * PAD * 12),
        name="attend",
    )(queries, keys_own, keys_far, values_own, values_far)


def attend_back_kernel(
    qo_ref, qt_ref, ko_ref, kt_ref, vo_ref, vt_ref, go_ref, gt_ref, lo_ref, lt_ref,
    dqo_ref, dqt_ref, dko_ref, dkt_ref, dvo_ref, dvt_ref,
):
    rows = qo_ref.shape[1]
    keys = jnp.concatenate([ko_ref[0], kt_ref[0]], axis=0)
    values = jnp.concatenate([vo_ref[0], vt_ref[0]], axis=0)
    keys_turned = keys.T[:HD]
    pieces = [(side, start, size) for side in range(2) for start, size in row_pieces(rows, 256)]
    sides = ((qo_ref, go_ref, lo_ref, dqo_ref), (qt_ref, gt_ref, lt_ref, dqt_ref))

    def query(piece):
        side, start, size = piece
        return sides[side][0][0, start : start + size, :]

    def upstream(piece):
        side, start, size = piece
        return sides[side][1][0, :, start : start + size]

    def begin(piece):
        score = dot_nt(keys, query(piece))
        padded = jnp.concatenate(
            [upstream(piece), jnp.zeros((PAD - HD, piece[2]), jnp.bfloat16)], axis=0
        )
        return score, dot_nn(values, padded)

    def middle(piece, score, weight_grad):
        side, start, size = piece
        probs = jnp.exp(score - sides[side][2][0, :, start : start + size])
        tilted = probs * weight_grad
        inner = jnp.sum(tilted, axis=0, keepdims=True)
        return probs.astype(jnp.bfloat16), (tilted - probs * inner).astype(jnp.bfloat16)

    total_k = total_v = None
    current = begin(pieces[0])
    for number, piece in enumerate(pieces):
        coming = begin(pieces[number + 1]) if number + 1 < len(pieces) else None
        weights, score_grad = middle(piece, *current)
        value_part = dot_nt(weights, upstream(piece))
        key_part = dot_nn(score_grad, query(piece))
        query_grad = dot_nn(keys_turned, score_grad)
        side, start, size = piece
        sides[side][3][0, start : start + size, :HD] = query_grad.T.astype(jnp.bfloat16)
        total_v = value_part if total_v is None else total_v + value_part
        total_k = key_part if total_k is None else total_k + key_part
        current = coming
    dko_ref[0] = total_k[:rows].astype(jnp.bfloat16)
    dkt_ref[0] = total_k[rows:].astype(jnp.bfloat16)
    dvo_ref[0, :, :HD] = total_v[:rows].astype(jnp.bfloat16)
    dvt_ref[0, :, :HD] = total_v[rows:].astype(jnp.bfloat16)


def attend_back_rows(queries, keys, values, upstream, logs):
    heads, rows, _ = queries[0].shape
    spec = pl.BlockSpec((1, rows, PAD), lambda h: (h, 0, 0))
    turned = pl.BlockSpec((1, HD, rows), lambda h: (h, 0, 0))
    line = pl.BlockSpec((1, 1, rows), lambda h: (h, 0, 0))
    return pl.pallas_call(
        attend_back_kernel,
        out_shape=(jax.ShapeDtypeStruct((heads, rows, PAD), jnp.bfloat16),) * 6,
        grid=(heads,),
        in_specs=[spec] * 6 + [turned] * 2 + [line] * 2,
        out_specs=(spec,) * 6,
        compiler_params=kernel_params(),
        cost_estimate=cost(heads * 4 * rows * rows * 2 * 900, heads * rows * PAD * 24),
        name="attend_back",
    )(*queries, *keys, *values, *upstream, *logs)


def merge_kernel(
    co_ref, ct_ref, weight_ref, frames_ref, bias_ref, gain_ref, shift_ref, middle_ref, second_ref
):
    rows = frames_ref.shape[0]
    cols = co_ref.shape[0]
    own, far = co_ref[...].T, ct_ref[...].T
    pieces = row_pieces(rows, 256)

    def branch(piece):
        take = slice(piece[0], piece[0] + piece[1])
        return dot_nt(own[take], weight_ref[:, :cols]) + dot_nt(far[take], weight_ref[:, cols:])

    def finish(piece, part):
        take = slice(piece[0], piece[0] + piece[1])
        middle = frames_ref[take, :].astype(jnp.float32) + part + bias_ref[...]
        middle_ref[take, :] = middle
        normed, _ = normalise(middle)
        second_ref[take, :] = (normed * gain_ref[...] + shift_ref[...]).astype(jnp.bfloat16)

    current = branch(pieces[0])
    for number, piece in enumerate(pieces):
        coming = branch(pieces[number + 1]) if number + 1 < len(pieces) else None
        finish(piece, current)
        current = coming


def merge_heads(context_own, context_far, pack, slot, frames, bias, gain, shift):
    rows, width = frames.shape
    cols = context_own.shape[0]
    return pl.pallas_call(
        merge_kernel,
        out_shape=(
            jax.ShapeDtypeStruct((rows, width), jnp.float32),
            jax.ShapeDtypeStruct((rows, width), jnp.bfloat16),
        ),
        grid=(1,),
        in_specs=[
            whole((cols, rows)), whole((cols, rows)), whole((width, 2 * cols), (0, slot)),
            whole((rows, width)), whole((1, width)), whole((1, width)), whole((1, width)),
        ],
        out_specs=(whole((rows, width)),) * 2,
        compiler_params=kernel_params(),
        cost_estimate=cost(4 * rows * width * cols, 10 * rows * width + 4 * width * cols),
        name="merge_heads",
    )(context_own, context_far, pack, frames, bias, gain, shift)


def feed_kernel(
    second_ref, grad_ref, expand_ref, reduce_ref, bias_ref,
    hidden_ref, back_ref, bsum_ref, out_ref, terms_ref, out_acc, terms_acc,
):
    step = pl.program_id(0)
    rows = second_ref.shape[0]
    pieces = row_pieces(rows, 376 if rows % 376 == 0 else 256)
    expand, reduce = expand_ref[...], reduce_ref[...]

    def begin(piece):
        take = slice(piece[0], piece[0] + piece[1])
        return dot_nn(second_ref[take, :], expand), dot_nn(grad_ref[take, :], reduce)

    @pl.when(step == 0)
    def _():
        out_acc[...] = jnp.zeros_like(out_acc)
        terms_acc[...] = jnp.zeros_like(terms_acc)

    sums = None
    current = begin(pieces[0])
    for number, piece in enumerate(pieces):
        coming = begin(pieces[number + 1]) if number + 1 < len(pieces) else None
        take = slice(piece[0], piece[0] + piece[1])
        raw, upstream = current
        raw = raw + bias_ref[...]
        below = 0.5 + 0.5 * lax.erf(raw * 0.7071067811865476)
        density = jnp.exp(raw * raw * -0.5) * 0.3989422804014327
        hidden = (raw * below).astype(jnp.bfloat16)
        back = (upstream * (below + raw * density)).astype(jnp.bfloat16)
        hidden_ref[take, :] = hidden
        back_ref[take, :] = back
        part = jnp.sum(back.astype(jnp.float32), axis=0, keepdims=True)
        sums = part if sums is None else sums + part
        terms_acc[take, :] += dot_nt(back, expand)
        out_acc[take, :] += dot_nt(hidden, reduce)
        current = coming
    bsum_ref[...] = sums

    @pl.when(step == pl.num_programs(0) - 1)
    def _():
        out_ref[...] = out_acc[...].astype(jnp.bfloat16)
        terms_ref[...] = terms_acc[...].astype(jnp.bfloat16)


def feed(second, grads, expand_pack, reduce_pack, bias, units):
    rows, width = second.shape
    block = 512 if units % 512 == 0 else units
    wide = pl.BlockSpec((rows, block), lambda j: (0, j))
    weight = pl.BlockSpec((width, block), lambda j: (0, j))
    line = pl.BlockSpec((1, block), lambda j: (0, j))
    return pl.pallas_call(
        feed_kernel,
        out_shape=(
            jax.ShapeDtypeStruct((rows, units), jnp.bfloat16),
            jax.ShapeDtypeStruct((rows, units), jnp.bfloat16),
            jax.ShapeDtypeStruct((1, units), jnp.float32),
            jax.ShapeDtypeStruct((rows, width), jnp.bfloat16),
            jax.ShapeDtypeStruct((rows, width), jnp.bfloat16),
        ),
        grid=(units // block,),
        in_specs=[whole((rows, width)), whole((rows, width)), weight, weight, line],
        out_specs=(wide, wide, line, whole((rows, width)), whole((rows, width))),
        scratch_shapes=[pltpu.VMEM((rows, width), jnp.float32)] * 2,
        compiler_params=kernel_params(),
        cost_estimate=cost(8 * rows * width * units, 8 * rows * (units + width) + 4 * width * units),
        name="feed",
    )(second, grads, expand_pack, reduce_pack, bias)


def weight_grad_kernel(count, scale_cols, scale, *refs):
    lefts, rights, out_ref = refs[:count], refs[count : 2 * count], refs[2 * count]
    total = None
    for left, right in zip(lefts, rights):
        part = dot_tn(left[...], right[...])
        total = part if total is None else total + part
    if scale_cols:
        block = out_ref.shape[1]
        total = total * jnp.where(pl.program_id(0) * block < scale_cols, scale, 1.0)
    out_ref[...] = total.astype(jnp.bfloat16)


def weight_grad(lefts, rights, block, scale_cols=0, scale=1.0):
    width, units = lefts[0].shape[1], rights[0].shape[1]
    rows = sum(left.shape[0] for left in lefts)
    return pl.pallas_call(
        functools.partial(weight_grad_kernel, len(lefts), scale_cols, scale),
        out_shape=jax.ShapeDtypeStruct((width, units), jnp.bfloat16),
        grid=(units // block,),
        in_specs=[whole(left.shape) for left in lefts]
        + [pl.BlockSpec((right.shape[0], block), lambda j: (0, j)) for right in rights],
        out_specs=pl.BlockSpec((width, block), lambda j: (0, j)),
        compiler_params=kernel_params(),
        cost_estimate=cost(2 * rows * width * units, 2 * (rows * (width + units) + width * units)),
        name="weight_grad",
    )(*lefts, *rights)


def branch_kernel(
    own_ref, far_ref, middle_ref, grad_ref, gain_ref, weight_ref,
    mgrad_ref, branch_ref, go_ref, gt_ref, sums_ref,
):
    rows, width = middle_ref.shape
    cols = go_ref.shape[0]
    pieces = row_pieces(rows, 256)

    def step_back(piece):
        take = slice(piece[0], piece[0] + piece[1])
        second_grad = own_ref[take, :].astype(jnp.float32) + far_ref[take, :].astype(jnp.float32)
        normed, inverse = normalise(middle_ref[take, :])
        wide = grad_ref[take, :].astype(jnp.float32)
        moved = second_grad * normed
        tilted = second_grad * gain_ref[...]
        mgrad = wide + inverse * (
            tilted
            - jnp.mean(tilted, axis=-1, keepdims=True)
            - normed * jnp.mean(tilted * normed, axis=-1, keepdims=True)
        )
        branch = mgrad.astype(jnp.bfloat16)
        mgrad_ref[take, :] = mgrad
        branch_ref[take, :] = branch
        sums = [
            jnp.sum(moved, axis=0, keepdims=True),
            jnp.sum(second_grad, axis=0, keepdims=True),
            jnp.sum(branch.astype(jnp.float32), axis=0, keepdims=True),
            jnp.sum(wide, axis=0, keepdims=True),
        ]
        return branch, sums

    def finish(piece, branch):
        take = slice(piece[0], piece[0] + piece[1])
        out = dot_nn(branch, weight_ref[...]).astype(jnp.bfloat16).T
        go_ref[:, take] = out[:cols]
        gt_ref[:, take] = out[cols:]

    totals = None
    branch, sums = step_back(pieces[0])
    totals = sums
    for number, piece in enumerate(pieces):
        now = branch
        if number + 1 < len(pieces):
            branch, sums = step_back(pieces[number + 1])
            totals = [a + b for a, b in zip(totals, sums)]
        finish(piece, now)
    for index, line in enumerate(totals):
        sums_ref[index : index + 1, :] = line


def branch_back(own, far, middle, grads, gain, pack, slot, cols):
    rows, width = middle.shape
    full = whole((rows, width))
    return pl.pallas_call(
        branch_kernel,
        out_shape=(
            jax.ShapeDtypeStruct((rows, width), jnp.float32),
            jax.ShapeDtypeStruct((rows, width), jnp.bfloat16),
            jax.ShapeDtypeStruct((cols, rows), jnp.bfloat16),
            jax.ShapeDtypeStruct((cols, rows), jnp.bfloat16),
            jax.ShapeDtypeStruct((4, width), jnp.float32),
        ),
        grid=(1,),
        in_specs=[full, full, full, full, whole((1, width)), whole((width, 2 * cols), (0, slot))],
        out_specs=(full, full, whole((cols, rows)), whole((cols, rows)), whole((4, width))),
        compiler_params=kernel_params(),
        cost_estimate=cost(4 * rows * width * cols, 18 * rows * width),
        name="branch_back",
    )(own, far, middle, grads, gain, pack)


def out_grad_kernel(branch_ref, co_ref, ct_ref, out_ref):
    cols = co_ref.shape[0]
    branch = branch_ref[...]
    out_ref[:, :cols] = dot_tn(branch, co_ref[...].T).astype(jnp.bfloat16)
    out_ref[:, cols:] = dot_tn(branch, ct_ref[...].T).astype(jnp.bfloat16)


def out_weight_grad(branch, context_own, context_far):
    rows, width = branch.shape
    cols = context_own.shape[0]
    return pl.pallas_call(
        out_grad_kernel,
        out_shape=jax.ShapeDtypeStruct((width, 2 * cols), jnp.bfloat16),
        grid=(1,),
        in_specs=[whole((rows, width)), whole((cols, rows)), whole((cols, rows))],
        out_specs=whole((width, 2 * cols)),
        compiler_params=kernel_params(),
        cost_estimate=cost(4 * rows * width * cols, 4 * rows * width + 4 * width * cols),
        name="out_weight_grad",
    )(branch, context_own, context_far)


def first_kernel(
    heads, dq_ref, dk_ref, dv_ref, weight_ref, frames_ref, pack_ref, terms_ref, sums_ref, bias_ref
):
    rows, width = frames_ref.shape
    cols = heads * HD
    q_factor = HD ** (-0.5)
    pieces = row_pieces(rows, 256)
    for part, ref in enumerate((dq_ref, dk_ref, dv_ref)):
        for head in range(heads):
            offset = part * cols + head * HD
            pack_ref[:, offset : offset + HD] = ref[head, :, :HD]

    def begin(piece):
        take = slice(piece[0], piece[0] + piece[1])
        return dot_nt(pack_ref[take, :cols], weight_ref[:, :cols]) * q_factor + dot_nt(
            pack_ref[take, cols:], weight_ref[:, cols:]
        )

    totals = None
    current = begin(pieces[0])
    for number, piece in enumerate(pieces):
        coming = begin(pieces[number + 1]) if number + 1 < len(pieces) else None
        take = slice(piece[0], piece[0] + piece[1])
        terms_ref[take, :] = current.astype(jnp.bfloat16)
        normed, _ = normalise(frames_ref[take, :].astype(jnp.float32))
        sums = [
            jnp.sum(current * normed, axis=0, keepdims=True),
            jnp.sum(current, axis=0, keepdims=True),
            jnp.sum(pack_ref[take, :].astype(jnp.float32), axis=0, keepdims=True),
        ]
        totals = sums if totals is None else [a + b for a, b in zip(totals, sums)]
        current = coming
    sums_ref[0:1, :] = totals[0]
    sums_ref[1:2, :] = totals[1]
    bias_ref[...] = totals[2]


def first_back(dq, dk, dv, weights, frames):
    heads, rows, _ = dq.shape
    width = frames.shape[1]
    cols = heads * HD
    return pl.pallas_call(
        functools.partial(first_kernel, heads),
        out_shape=(
            jax.ShapeDtypeStruct((rows, 3 * cols), jnp.bfloat16),
            jax.ShapeDtypeStruct((rows, width), jnp.bfloat16),
            jax.ShapeDtypeStruct((2, width), jnp.float32),
            jax.ShapeDtypeStruct((1, 3 * cols), jnp.float32),
        ),
        grid=(1,),
        in_specs=[whole(dq.shape)] * 3 + [whole((width, 3 * cols)), whole((rows, width))],
        out_specs=(
            whole((rows, 3 * cols)), whole((rows, width)), whole((2, width)), whole((1, 3 * cols))
        ),
        compiler_params=kernel_params(),
        cost_estimate=cost(6 * rows * width * cols, 6 * heads * rows * PAD + 6 * width * cols),
        name="first_back",
    )(dq, dk, dv, weights, frames)


def frames_kernel(frames_ref, own_ref, far_ref, mgrad_ref, gain_ref, out_ref):
    normed, inverse = normalise(frames_ref[...].astype(jnp.float32))
    tilted = (own_ref[...].astype(jnp.float32) + far_ref[...].astype(jnp.float32)) * gain_ref[...]
    out_ref[...] = (
        mgrad_ref[...]
        + inverse
        * (
            tilted
            - jnp.mean(tilted, axis=-1, keepdims=True)
            - normed * jnp.mean(tilted * normed, axis=-1, keepdims=True)
        )
    ).astype(jnp.bfloat16)


def frames_back(frames, own, far, mgrad, gain):
    rows, width = frames.shape
    block = 376 if rows % 376 == 0 else rows
    spec = pl.BlockSpec((block, width), lambda i: (i, 0))
    return pl.pallas_call(
        frames_kernel,
        out_shape=jax.ShapeDtypeStruct((rows, width), jnp.bfloat16),
        grid=(rows // block,),
        in_specs=[spec] * 4 + [whole((1, width))],
        out_specs=spec,
        compiler_params=kernel_params(),
        cost_estimate=cost(20 * rows * width, 12 * rows * width),
        name="frames_back",
    )(frames, own, far, mgrad, gain)


def swap_tp(piece):
    return lax.ppermute(piece, "tp", [(0, 1), (1, 0)])


def gather_steps(vector, fsdp):
    index = lax.axis_index("fsdp")
    other = swap_tp(vector)
    side = lax.axis_index("tp")
    held = jnp.where(side == 0, jnp.stack([vector, other]), jnp.stack([other, vector]))
    bit = 1
    while bit < fsdp:
        other = lax.ppermute(held, "fsdp", [(i, i ^ bit) for i in range(fsdp)])
        low = (index & bit) == 0
        held = jnp.where(low, jnp.concatenate([held, other]), jnp.concatenate([other, held]))
        bit *= 2
    return held


def scatter_steps(held, fsdp):
    index = lax.axis_index("fsdp")
    bit = fsdp // 2
    while bit >= 1:
        low = (index & bit) == 0
        first, second = held[:bit], held[bit:]
        send = jnp.where(low, second, first)
        held = jnp.where(low, first, second) + lax.ppermute(
            send, "fsdp", [(i, i ^ bit) for i in range(fsdp)]
        )
        bit //= 2
    return held[0]


def per_device_pair(
    frames, out_grad, clip_lengths, clip_order, w_query, w_key, w_value, b_query, b_value,
    w_out, b_out, w_expand, b_expand, w_reduce, b_reduce,
    first_gain, first_shift, second_gain, second_shift, *, fsdp,
):
    side = lax.axis_index("tp")
    slot = lax.axis_index("fsdp")
    clip_count = clip_order.shape[0]
    every_clip = jnp.arange(clip_count, dtype=jnp.int32)
    clip_id = jnp.sum(jnp.where(every_clip == slot, clip_order, 0))
    length = jnp.sum(jnp.where(every_clip == clip_id, clip_lengths, 0))
    frames, out_grad = frames[0], out_grad[0]
    rows, width = frames.shape
    cols = w_query.shape[1]
    heads = cols // HD
    units = w_expand.shape[1]
    q_factor = HD ** (-0.5)
    scal_own = jnp.stack([length, side * rows]).astype(jnp.int32)
    scal_far = jnp.stack([length, (1 - side) * rows]).astype(jnp.int32)

    qkv = lax.all_gather(
        jnp.concatenate([w_query, w_key, w_value], axis=1), "fsdp", axis=0, tiled=True
    )
    frames_far = swap_tp(frames)
    wide_six = [first_gain, first_shift, second_gain, second_shift, b_out, b_reduce]
    small = gather_steps(jnp.concatenate(wide_six + [b_query, b_value, b_expand]), fsdp)
    lot = first_gain.shape[0]
    whole_six = small[:, : 6 * lot].astype(jnp.float32).reshape(2 * fsdp, 6, lot)
    whole_six = whole_six.transpose(1, 0, 2).reshape(6, 1, width)
    gain_one, shift_one, gain_two, shift_two, out_bias, reduce_bias = [whole_six[i] for i in range(6)]
    mine = lax.dynamic_index_in_dim(
        small[:, 6 * lot :].astype(jnp.float32).reshape(fsdp, 2, -1), side, axis=1, keepdims=False
    )
    part = b_query.shape[0]
    bias_q = mine[:, :part].reshape(1, -1)
    bias_v = mine[:, part : 2 * part].reshape(1, -1)
    bias_e = mine[:, 2 * part :].reshape(1, -1)
    out_turned = w_out.T
    out_other = swap_tp(out_turned)
    pack_two = lax.all_gather(
        jnp.concatenate([w_expand, out_turned, out_other], axis=1), "fsdp", axis=0, tiled=True
    )
    out_slot = units // (2 * cols)
    reduce_all = lax.all_gather(w_reduce.T, "fsdp", axis=0, tiled=True)
    grads_far = swap_tp(out_grad)

    first_own, q_own, k_own, v_own = project(
        scal_own, frames, gain_one, shift_one, qkv, bias_q, bias_v, heads
    )
    first_far, q_far, k_far, v_far = project(
        scal_far, frames_far, gain_one, shift_one, qkv, bias_q, bias_v, heads
    )
    context_send, log_far = attend_rows(q_far, k_own, k_far, v_own, v_far)
    context_far = swap_tp(context_send.reshape(cols, rows))
    context_own, log_own = attend_rows(q_own, k_own, k_far, v_own, v_far)
    context_own = context_own.reshape(cols, rows)
    middle, second_own = merge_heads(
        context_own, context_far, pack_two, out_slot, frames, out_bias, gain_two, shift_two
    )

    second_far = swap_tp(second_own)
    hid_own, back_own, bsum_own, out_own, terms_own = feed(
        second_own, out_grad, pack_two, reduce_all, bias_e, units
    )
    hid_far, back_far, bsum_far, out_send, terms_send = feed(
        second_far, grads_far, pack_two, reduce_all, bias_e, units
    )
    terms_far = swap_tp(terms_send)
    out_far = swap_tp(out_send)
    block = 512 if units % 512 == 0 else units
    d_reduce = weight_grad([out_grad, grads_far], [hid_own, hid_far], block)
    d_expand = weight_grad([second_own, second_far], [back_own, back_far], block)
    out_frames = (
        middle + out_own.astype(jnp.float32) + out_far.astype(jnp.float32) + reduce_bias
    ).astype(jnp.bfloat16)
    mgrad, branch, up_own, up_send, sums_two = branch_back(
        terms_own, terms_far, middle, out_grad, gain_two, pack_two, out_slot, cols
    )
    up_far = swap_tp(up_send)
    d_out = out_weight_grad(branch, context_own, context_far)

    turned = (heads, HD, rows)
    dq_own, dq_far, dk_own, dk_far, dv_own, dv_far = attend_back_rows(
        (q_own, q_far), (k_own, k_far), (v_own, v_far),
        (up_own.reshape(turned), up_far.reshape(turned)), (log_own, log_far),
    )
    pack_far, first_send, sums_far, bias_far = first_back(dq_far, dk_far, dv_far, qkv, frames_far)
    first_recv = swap_tp(first_send)
    pack_own, first_keep, sums_own, bias_own = first_back(dq_own, dk_own, dv_own, qkv, frames)
    d_qkv = weight_grad([first_own, first_far], [pack_own, pack_far], cols, cols, q_factor)
    frames_grad = frames_back(frames, first_keep, first_recv, mgrad, gain_one)

    def scatter(grad):
        return lax.psum_scatter(grad, "fsdp", scatter_dimension=0, tiled=True).astype(jnp.float32)

    g_reduce, g_expand, g_qkv = scatter(d_reduce), scatter(d_expand), scatter(d_qkv)
    g_out = lax.psum_scatter(d_out, "fsdp", scatter_dimension=0, tiled=True)
    sums_one = sums_own + sums_far
    bias_sum = bias_own + bias_far
    wide_sums = jnp.concatenate([sums_one, sums_two])
    wide_sums = wide_sums.reshape(6, fsdp, 2, lot).transpose(1, 2, 0, 3).reshape(fsdp, 12 * lot)
    tall = jnp.concatenate(
        [
            wide_sums,
            (bias_sum[:, :cols] * q_factor).reshape(fsdp, -1),
            bias_sum[:, 2 * cols :].reshape(fsdp, -1),
            (bsum_own + bsum_far).reshape(fsdp, -1),
        ],
        axis=1,
    )
    small_sum = scatter_steps(tall, fsdp)
    six = small_sum[: 12 * lot].reshape(2, 6 * lot)
    keep = lax.dynamic_index_in_dim(six, side, 0, keepdims=False)
    send = lax.dynamic_index_in_dim(six, 1 - side, 0, keepdims=False)
    six = (keep + swap_tp(send)).reshape(6, lot)
    rest = small_sum[12 * lot :]
    g_bq, g_bv, g_be = rest[:part], rest[part : 2 * part], rest[2 * part :]
    g_out_sum = g_out[:, :cols].astype(jnp.float32) + swap_tp(g_out[:, cols:]).astype(jnp.float32)
    return (
        out_frames[None],
        frames_grad[None],
        g_qkv[:, :cols],
        g_qkv[:, cols : 2 * cols],
        g_qkv[:, 2 * cols :],
        g_bq,
        g_bv,
        g_out_sum.T,
        six[4],
        g_expand,
        g_be,
        g_reduce.T,
        six[5],
        six[0],
        six[1],
        six[2],
        six[3],
    )


def solution(mesh):
    fsdp = mesh.shape["fsdp"]
    if mesh.shape["tp"] == 2 and fsdp & (fsdp - 1) == 0:

        def body(*args):
            return per_device_pair(*args, fsdp=fsdp) if args[0].shape[0] == 1 else per_device(*args)
    else:
        body = per_device
    return jax.shard_map(
        body,
        mesh=mesh,
        in_specs=(
            P("fsdp", "tp", None),
            P("fsdp", "tp", None),
            P(),
            P(),
            P("fsdp", "tp"),
            P("fsdp", "tp"),
            P("fsdp", "tp"),
            P(("tp", "fsdp")),
            P(("tp", "fsdp")),
            P("tp", "fsdp"),
            P(("fsdp", "tp")),
            P("fsdp", "tp"),
            P(("tp", "fsdp")),
            P("tp", "fsdp"),
            P(("fsdp", "tp")),
            P(("fsdp", "tp")),
            P(("fsdp", "tp")),
            P(("fsdp", "tp")),
            P(("fsdp", "tp")),
        ),
        out_specs=(
            P("fsdp", "tp", None),
            P("fsdp", "tp", None),
            P("fsdp", "tp"),
            P("fsdp", "tp"),
            P("fsdp", "tp"),
            P(("tp", "fsdp")),
            P(("tp", "fsdp")),
            P("tp", "fsdp"),
            P(("fsdp", "tp")),
            P("fsdp", "tp"),
            P(("tp", "fsdp")),
            P("tp", "fsdp"),
            P(("fsdp", "tp")),
            P(("fsdp", "tp")),
            P(("fsdp", "tp")),
            P(("fsdp", "tp")),
            P(("fsdp", "tp")),
        ),
        check_vma=False,
    )
```

```python
import functools

import jax
import jax.numpy as jnp
from jax import lax
from jax.experimental import pallas as pl
from jax.experimental.pallas import tpu as pltpu
from jax.sharding import PartitionSpec as P

HD = 80


EPSILON = 1e-05
MASKED = -1000000000.0
HIDDEN = -1e30


def layer_norm(features, norm_gain, norm_shift):
    row_mean = jnp.mean(features, axis=-1, keepdims=True)
    centred = features - row_mean
    row_var = jnp.mean(centred * centred, axis=-1, keepdims=True)
    inverse = lax.rsqrt(row_var + EPSILON)
    normed = centred * inverse
    return (normed * norm_gain + norm_shift, normed, inverse)


def norm_back(upstream, normed, inverse, norm_gain):
    tilted = upstream * norm_gain
    return inverse * (
        tilted
        - jnp.mean(tilted, axis=-1, keepdims=True)
        - normed * jnp.mean(tilted * normed, axis=-1, keepdims=True)
    )


def gelu_exact(inputs):
    return jax.nn.gelu(inputs, approximate=False)


def masked_scores(queries, key_rows, length):
    scores = jnp.einsum("qhe,khe->hqk", queries, key_rows, preferred_element_type=jnp.float32)
    allowed = jnp.arange(scores.shape[-1]) < length
    return jnp.where(allowed[None, None, :], scores, MASKED)


def attend(inputs):
    queries, key_rows, value_rows, length = inputs
    scores = masked_scores(queries, key_rows, length)
    row_top = jnp.max(scores, axis=-1, keepdims=True)
    raised = jnp.exp(scores - row_top)
    row_sum = jnp.sum(raised, axis=-1, keepdims=True)
    weights = (raised / row_sum).astype(jnp.bfloat16)
    context = jnp.einsum("hqk,khe->qhe", weights, value_rows, preferred_element_type=jnp.float32)
    return (context.astype(jnp.bfloat16), row_top[..., 0] + jnp.log(row_sum[..., 0]))


def attend_back(inputs):
    queries, key_rows, value_rows, length, log_total, context_grad = inputs
    scores = masked_scores(queries, key_rows, length)
    probs = jnp.exp(scores - log_total[..., None])
    weights = probs.astype(jnp.bfloat16)
    value_grad = jnp.einsum(
        "hqk,qhe->khe", weights, context_grad, preferred_element_type=jnp.float32
    )
    weight_grad = jnp.einsum(
        "qhe,khe->hqk", context_grad, value_rows, preferred_element_type=jnp.float32
    )
    row_inner = jnp.sum(weight_grad * probs, axis=-1, keepdims=True)
    score_grad = (probs * (weight_grad - row_inner)).astype(jnp.bfloat16)
    query_grad = jnp.einsum(
        "hqk,khe->qhe", score_grad, key_rows, preferred_element_type=jnp.float32
    )
    key_grad = jnp.einsum("hqk,qhe->khe", score_grad, queries, preferred_element_type=jnp.float32)
    return (
        query_grad.astype(jnp.bfloat16),
        key_grad.astype(jnp.bfloat16),
        value_grad.astype(jnp.bfloat16),
    )


def gather_inward(w_query, w_key, w_value, b_query, b_value, w_expand, b_expand):
    return (
        lax.all_gather(w_query, "fsdp", axis=0, tiled=True),
        lax.all_gather(w_key, "fsdp", axis=0, tiled=True),
        lax.all_gather(w_value, "fsdp", axis=0, tiled=True),
        lax.all_gather(b_query, "fsdp", axis=0, tiled=True),
        lax.all_gather(b_value, "fsdp", axis=0, tiled=True),
        lax.all_gather(w_expand, "fsdp", axis=0, tiled=True),
        lax.all_gather(b_expand, "fsdp", axis=0, tiled=True),
    )


def gather_outward(w_out, w_reduce):
    return (
        lax.all_gather(w_out, "fsdp", axis=1, tiled=True),
        lax.all_gather(w_reduce, "fsdp", axis=1, tiled=True),
    )


def per_device(
    frames,
    out_grad,
    clip_lengths,
    clip_order,
    w_query,
    w_key,
    w_value,
    b_query,
    b_value,
    w_out,
    b_out,
    w_expand,
    b_expand,
    w_reduce,
    b_reduce,
    first_gain,
    first_shift,
    second_gain,
    second_shift,
):
    per_group = frames.shape[0]
    clip_count = clip_order.shape[0]
    slot_ids = lax.axis_index("fsdp") * per_group + jnp.arange(per_group, dtype=jnp.int32)
    every_clip = jnp.arange(clip_count, dtype=jnp.int32)
    clip_ids = jnp.sum(
        jnp.where(every_clip[None, :] == slot_ids[:, None], clip_order[None, :], 0), axis=1
    )
    lengths = jnp.sum(
        jnp.where(every_clip[None, :] == clip_ids[:, None], clip_lengths[None, :], 0), axis=1
    )
    norm_params = (
        lax.all_gather(first_gain, ("fsdp", "tp"), axis=0, tiled=True),
        lax.all_gather(first_shift, ("fsdp", "tp"), axis=0, tiled=True),
        lax.all_gather(second_gain, ("fsdp", "tp"), axis=0, tiled=True),
        lax.all_gather(second_shift, ("fsdp", "tp"), axis=0, tiled=True),
        lax.all_gather(b_out, ("fsdp", "tp"), axis=0, tiled=True),
        lax.all_gather(b_reduce, ("fsdp", "tp"), axis=0, tiled=True),
    )
    gain_one, shift_one, gain_two, shift_two, out_bias, reduce_bias = [
        tensor.astype(jnp.float32) for tensor in norm_params
    ]
    wq_all, wk_all, wv_all, bq_all, bv_all, we_all, be_all = gather_inward(
        w_query, w_key, w_value, b_query, b_value, w_expand, b_expand
    )
    wo_all, wr_all = gather_outward(w_out, w_reduce)
    q_factor = HD ** (-0.5)
    frames_wide = frames.astype(jnp.float32)
    norm_one, normed_one, inverse_one = layer_norm(frames_wide, gain_one, shift_one)
    first_rows = lax.all_gather(norm_one.astype(jnp.bfloat16), "tp", axis=1, tiled=True)
    seq_len = first_rows.shape[1]
    queries = (
        (
            jnp.einsum("csd,de->cse", first_rows, wq_all, preferred_element_type=jnp.float32)
            + bq_all.astype(jnp.float32)
        )
        * q_factor
    ).astype(jnp.bfloat16)
    keys = jnp.einsum("csd,de->cse", first_rows, wk_all, preferred_element_type=jnp.float32).astype(
        jnp.bfloat16
    )
    values = (
        jnp.einsum("csd,de->cse", first_rows, wv_all, preferred_element_type=jnp.float32)
        + bv_all.astype(jnp.float32)
    ).astype(jnp.bfloat16)
    head_shape = (per_group, seq_len, -1, HD)
    query_heads = queries.reshape(head_shape)
    key_heads = keys.reshape(head_shape)
    value_heads = values.reshape(head_shape)
    context, log_total = lax.map(attend, (query_heads, key_heads, value_heads, lengths))
    context_flat = context.reshape(per_group, seq_len, -1)
    attn_terms = jnp.einsum("cse,ed->csd", context_flat, wo_all, preferred_element_type=jnp.float32)
    attn_part = lax.psum_scatter(
        attn_terms.astype(jnp.bfloat16), "tp", scatter_dimension=1, tiled=True
    ).astype(jnp.float32)
    middle = frames_wide + attn_part + out_bias
    norm_two, normed_two, inverse_two = layer_norm(middle, gain_two, shift_two)
    second_rows = lax.all_gather(norm_two.astype(jnp.bfloat16), "tp", axis=1, tiled=True)
    expanded = jnp.einsum(
        "csd,df->csf", second_rows, we_all, preferred_element_type=jnp.float32
    ) + be_all.astype(jnp.float32)
    activated, gelu_pull = jax.vjp(gelu_exact, expanded)
    hidden = activated.astype(jnp.bfloat16)
    mlp_terms = jnp.einsum("csf,fd->csd", hidden, wr_all, preferred_element_type=jnp.float32)
    out_frames = (
        middle
        + lax.psum_scatter(
            mlp_terms.astype(jnp.bfloat16), "tp", scatter_dimension=1, tiled=True
        ).astype(jnp.float32)
        + reduce_bias
    ).astype(jnp.bfloat16)
    wq_all, wk_all, wv_all, bq_all, bv_all, we_all, be_all = gather_inward(
        w_query, w_key, w_value, b_query, b_value, w_expand, b_expand
    )
    wo_all, wr_all = gather_outward(w_out, w_reduce)
    grad_wide = out_grad.astype(jnp.float32)
    grad_rows = lax.all_gather(out_grad, "tp", axis=1, tiled=True)
    w_reduce_grad = jnp.einsum("csf,csd->fd", hidden, grad_rows, preferred_element_type=jnp.float32)
    hidden_grad = jnp.einsum("csd,fd->csf", grad_rows, wr_all, preferred_element_type=jnp.float32)
    expanded_grad = gelu_pull(hidden_grad)[0].astype(jnp.bfloat16)
    b_expand_grad = jnp.sum(expanded_grad.astype(jnp.float32), axis=(0, 1))
    w_expand_grad = jnp.einsum(
        "csd,csf->df", second_rows, expanded_grad, preferred_element_type=jnp.float32
    )
    second_terms = jnp.einsum(
        "csf,df->csd", expanded_grad, we_all, preferred_element_type=jnp.float32
    )
    second_grad = lax.psum_scatter(
        second_terms.astype(jnp.bfloat16), "tp", scatter_dimension=1, tiled=True
    ).astype(jnp.float32)
    second_gain_grad = jnp.sum(second_grad * normed_two, axis=(0, 1))
    second_shift_grad = jnp.sum(second_grad, axis=(0, 1))
    middle_grad = grad_wide + norm_back(second_grad, normed_two, inverse_two, gain_two)
    branch_grad = middle_grad.astype(jnp.bfloat16)
    b_out_grad = jnp.sum(branch_grad.astype(jnp.float32), axis=(0, 1))
    b_reduce_grad = jnp.sum(grad_wide, axis=(0, 1))
    branch_rows = lax.all_gather(branch_grad, "tp", axis=1, tiled=True)
    w_out_grad = jnp.einsum(
        "cse,csd->ed", context_flat, branch_rows, preferred_element_type=jnp.float32
    )
    context_grad = jnp.einsum(
        "csd,ed->cse", branch_rows, wo_all, preferred_element_type=jnp.float32
    ).astype(jnp.bfloat16)
    query_grad, key_grad, value_grad = lax.map(
        attend_back,
        (query_heads, key_heads, value_heads, lengths, log_total, context_grad.reshape(head_shape)),
    )
    query_grad = query_grad.reshape(per_group, seq_len, -1)
    key_grad = key_grad.reshape(per_group, seq_len, -1)
    value_grad = value_grad.reshape(per_group, seq_len, -1)
    w_query_grad = (
        jnp.einsum("csd,cse->de", first_rows, query_grad, preferred_element_type=jnp.float32)
        * q_factor
    )
    b_query_grad = jnp.sum(query_grad.astype(jnp.float32), axis=(0, 1)) * q_factor
    w_key_grad = jnp.einsum("csd,cse->de", first_rows, key_grad, preferred_element_type=jnp.float32)
    w_value_grad = jnp.einsum(
        "csd,cse->de", first_rows, value_grad, preferred_element_type=jnp.float32
    )
    b_value_grad = jnp.sum(value_grad.astype(jnp.float32), axis=(0, 1))
    first_terms = (
        jnp.einsum("cse,de->csd", query_grad, wq_all, preferred_element_type=jnp.float32) * q_factor
        + jnp.einsum("cse,de->csd", key_grad, wk_all, preferred_element_type=jnp.float32)
        + jnp.einsum("cse,de->csd", value_grad, wv_all, preferred_element_type=jnp.float32)
    )
    first_grad = lax.psum_scatter(
        first_terms.astype(jnp.bfloat16), "tp", scatter_dimension=1, tiled=True
    ).astype(jnp.float32)
    first_gain_grad = jnp.sum(first_grad * normed_one, axis=(0, 1))
    first_shift_grad = jnp.sum(first_grad, axis=(0, 1))
    frames_grad = (middle_grad + norm_back(first_grad, normed_one, inverse_one, gain_one)).astype(
        jnp.bfloat16
    )
    inward_grads = (
        lax.psum_scatter(
            w_query_grad.astype(jnp.bfloat16), "fsdp", scatter_dimension=0, tiled=True
        ).astype(jnp.float32),
        lax.psum_scatter(
            w_key_grad.astype(jnp.bfloat16), "fsdp", scatter_dimension=0, tiled=True
        ).astype(jnp.float32),
        lax.psum_scatter(
            w_value_grad.astype(jnp.bfloat16), "fsdp", scatter_dimension=0, tiled=True
        ).astype(jnp.float32),
        lax.psum_scatter(
            b_query_grad.astype(jnp.bfloat16), "fsdp", scatter_dimension=0, tiled=True
        ).astype(jnp.float32),
        lax.psum_scatter(
            b_value_grad.astype(jnp.bfloat16), "fsdp", scatter_dimension=0, tiled=True
        ).astype(jnp.float32),
        lax.psum_scatter(
            w_expand_grad.astype(jnp.bfloat16), "fsdp", scatter_dimension=0, tiled=True
        ).astype(jnp.float32),
        lax.psum_scatter(
            b_expand_grad.astype(jnp.bfloat16), "fsdp", scatter_dimension=0, tiled=True
        ).astype(jnp.float32),
    )
    outward_grads = (
        lax.psum_scatter(
            w_out_grad.astype(jnp.bfloat16), "fsdp", scatter_dimension=1, tiled=True
        ).astype(jnp.float32),
        lax.psum_scatter(
            w_reduce_grad.astype(jnp.bfloat16), "fsdp", scatter_dimension=1, tiled=True
        ).astype(jnp.float32),
    )
    small_grads = (
        lax.psum_scatter(first_gain_grad, ("fsdp", "tp"), scatter_dimension=0, tiled=True),
        lax.psum_scatter(first_shift_grad, ("fsdp", "tp"), scatter_dimension=0, tiled=True),
        lax.psum_scatter(second_gain_grad, ("fsdp", "tp"), scatter_dimension=0, tiled=True),
        lax.psum_scatter(second_shift_grad, ("fsdp", "tp"), scatter_dimension=0, tiled=True),
        lax.psum_scatter(b_out_grad, ("fsdp", "tp"), scatter_dimension=0, tiled=True),
        lax.psum_scatter(b_reduce_grad, ("fsdp", "tp"), scatter_dimension=0, tiled=True),
    )
    return (
        out_frames,
        frames_grad,
        inward_grads[0],
        inward_grads[1],
        inward_grads[2],
        inward_grads[3],
        inward_grads[4],
        outward_grads[0],
        small_grads[4],
        inward_grads[5],
        inward_grads[6],
        outward_grads[1],
        small_grads[5],
        small_grads[0],
        small_grads[1],
        small_grads[2],
        small_grads[3],
    )


VMEM_LIMIT = 60 << 20
PAD = 128
COST = 3.0


def kernel_params():
    return pltpu.CompilerParams(vmem_limit_bytes=VMEM_LIMIT)


def cost(flops, moved):
    return pl.CostEstimate(flops=int(COST * flops), bytes_accessed=int(moved), transcendentals=0)


def row_pieces(rows, size):
    return [(start, min(size, rows - start)) for start in range(0, rows, size)]


def whole(shape, fixed=None):
    index = fixed if fixed is not None else (0,) * len(shape)
    return pl.BlockSpec(shape, lambda *_: index)


def normalise(rows):
    row_mean = jnp.mean(rows, axis=-1, keepdims=True)
    centred = rows - row_mean
    inverse = lax.rsqrt(jnp.mean(centred * centred, axis=-1, keepdims=True) + EPSILON)
    return centred * inverse, inverse


def dot_nn(left, right):
    return jnp.dot(left, right, preferred_element_type=jnp.float32)


def dot_nt(left, right):
    return lax.dot_general(left, right, (((1,), (1,)), ((), ())), preferred_element_type=jnp.float32)


def dot_tn(left, right):
    return lax.dot_general(left, right, (((0,), (0,)), ((), ())), preferred_element_type=jnp.float32)


def project_kernel(
    heads, scal_ref, frames_ref, gain_ref, shift_ref, weight_ref, bq_ref, bv_ref,
    first_ref, q_ref, k_ref, v_ref,
):
    rows, width = frames_ref.shape
    cols = heads * HD
    length, start = scal_ref[0], scal_ref[1]
    q_factor = HD ** (-0.5)
    pieces = row_pieces(rows, 256)

    def norm(piece):
        normed, _ = normalise(frames_ref[piece[0] : piece[0] + piece[1], :].astype(jnp.float32))
        first = (normed * gain_ref[...] + shift_ref[...]).astype(jnp.bfloat16)
        first_ref[piece[0] : piece[0] + piece[1], :] = first
        return first

    def split(block, offset, filler, lane):
        if offset + PAD <= block.shape[1]:
            part = block[:, offset : offset + PAD]
        else:
            back = block.shape[1] - PAD
            part = pltpu.roll(block[:, back:], PAD - (offset - back), 1)
        return jnp.where(lane < HD, part, filler).astype(jnp.bfloat16)

    def finish(piece, out):
        lane = lax.broadcasted_iota(jnp.int32, (piece[1], PAD), 1)
        position = lax.broadcasted_iota(jnp.int32, (piece[1], PAD), 0) + (start + piece[0])
        one = jnp.where(lane == HD, 1.0, 0.0)
        hide = jnp.where((lane == HD) & (position >= length), HIDDEN, 0.0)
        queries = (out[:, :cols] + bq_ref[...]) * q_factor
        keys = out[:, cols : 2 * cols]
        values = out[:, 2 * cols :] + bv_ref[...]
        for head in range(heads):
            where = (head, slice(piece[0], piece[0] + piece[1]), slice(None))
            q_ref[where] = split(queries, head * HD, one, lane)
            k_ref[where] = split(keys, head * HD, hide, lane)
            v_ref[where] = split(values, head * HD, 0.0, lane)

    first = norm(pieces[0])
    for number, piece in enumerate(pieces):
        out = dot_nn(first, weight_ref[...])
        if number + 1 < len(pieces):
            first = norm(pieces[number + 1])
        finish(piece, out)


def project(scalars, frames, gain, shift, weights, bias_q, bias_v, heads):
    rows, width = frames.shape
    cols = heads * HD
    head_out = jax.ShapeDtypeStruct((heads, rows, PAD), jnp.bfloat16)
    return pl.pallas_call(
        functools.partial(project_kernel, heads),
        out_shape=(jax.ShapeDtypeStruct((rows, width), jnp.bfloat16), head_out, head_out, head_out),
        grid_spec=pltpu.PrefetchScalarGridSpec(
            num_scalar_prefetch=1,
            grid=(1,),
            in_specs=[
                whole((rows, width)), whole((1, width)), whole((1, width)),
                whole((width, 3 * cols)), whole((1, cols)), whole((1, cols)),
            ],
            out_specs=(whole((rows, width)),) + (whole((heads, rows, PAD)),) * 3,
        ),
        compiler_params=kernel_params(),
        cost_estimate=cost(2 * rows * width * 3 * cols, 4 * rows * width + 6 * width * cols),
        name="project",
    )(scalars, frames, gain, shift, weights, bias_q, bias_v)


def attend_kernel(q_ref, ko_ref, kt_ref, vo_ref, vt_ref, out_ref, log_ref):
    per_step, rows, _ = q_ref.shape
    half = -(-rows // 256) * 128
    pieces = [(head, start, size) for head in range(per_step) for start, size in row_pieces(rows, half)]
    keys = [jnp.concatenate([ko_ref[h], kt_ref[h]], axis=0) for h in range(per_step)]
    values = [jnp.concatenate([vo_ref[h], vt_ref[h]], axis=0).T[:HD] for h in range(per_step)]

    def scores(piece):
        head, start, size = piece
        return dot_nt(keys[head], q_ref[head, start : start + size, :])

    def finish(piece, score):
        head, start, size = piece
        top = jnp.max(score, axis=0, keepdims=True)
        raised = jnp.exp(score - top)
        total = jnp.sum(raised, axis=0, keepdims=True)
        context = dot_nn(values[head], raised.astype(jnp.bfloat16)) / total
        out_ref[head, :, start : start + size] = context.astype(jnp.bfloat16)
        log_ref[head, :, start : start + size] = top + jnp.log(total)

    current = scores(pieces[0])
    for number, piece in enumerate(pieces):
        coming = scores(pieces[number + 1]) if number + 1 < len(pieces) else None
        finish(piece, current)
        current = coming


def attend_rows(queries, keys_own, keys_far, values_own, values_far):
    heads, rows, _ = queries.shape
    per_step = 2 if heads % 2 == 0 else 1
    spec = pl.BlockSpec((per_step, rows, PAD), lambda h: (h, 0, 0))
    return pl.pallas_call(
        attend_kernel,
        out_shape=(
            jax.ShapeDtypeStruct((heads, HD, rows), jnp.bfloat16),
            jax.ShapeDtypeStruct((heads, 1, rows), jnp.float32),
        ),
        grid=(heads // per_step,),
        in_specs=[spec] * 5,
        out_specs=(
            pl.BlockSpec((per_step, HD, rows), lambda h: (h, 0, 0)),
            pl.BlockSpec((per_step, 1, rows), lambda h: (h, 0, 0)),
        ),
        compiler_params=kernel_params(),
        cost_estimate=cost(heads * 2 * rows * 2 * rows * 2 * 400, heads * rows * PAD * 12),
        name="attend",
    )(queries, keys_own, keys_far, values_own, values_far)


def attend_back_kernel(
    qo_ref, qt_ref, ko_ref, kt_ref, vo_ref, vt_ref, go_ref, gt_ref, lo_ref, lt_ref,
    own_ref, far_ref, dq_ref,
):
    rows = qo_ref.shape[1]
    cols = own_ref.shape[1] // 3
    keys = jnp.concatenate([ko_ref[0], kt_ref[0]], axis=0)
    values = jnp.concatenate([vo_ref[0], vt_ref[0]], axis=0)
    keys_turned = keys.T[:HD]
    pieces = [(side, start, size) for side in range(2) for start, size in row_pieces(rows, 256)]
    sides = ((qo_ref, go_ref, lo_ref), (qt_ref, gt_ref, lt_ref))

    def query(piece):
        side, start, size = piece
        return sides[side][0][0, start : start + size, :]

    def upstream(piece):
        side, start, size = piece
        return sides[side][1][0, :, start : start + size]

    def begin(piece):
        score = dot_nt(keys, query(piece))
        padded = jnp.concatenate(
            [upstream(piece), jnp.zeros((PAD - HD, piece[2]), jnp.bfloat16)], axis=0
        )
        return score, dot_nn(values, padded)

    def middle(piece, score, weight_grad):
        side, start, size = piece
        probs = jnp.exp(score - sides[side][2][0, :, start : start + size])
        tilted = probs * weight_grad
        inner = jnp.sum(tilted, axis=0, keepdims=True)
        return probs.astype(jnp.bfloat16), (tilted - probs * inner).astype(jnp.bfloat16)

    total_k = total_v = None
    current = begin(pieces[0])
    for number, piece in enumerate(pieces):
        coming = begin(pieces[number + 1]) if number + 1 < len(pieces) else None
        weights, score_grad = middle(piece, *current)
        value_part = dot_nt(weights, upstream(piece))
        key_part = dot_nn(score_grad, query(piece))
        query_grad = dot_nn(keys_turned, score_grad)
        side, start, size = piece
        dq_ref[side * rows + start : side * rows + start + size, :] = query_grad.T.astype(jnp.bfloat16)
        total_v = value_part if total_v is None else total_v + value_part
        total_k = key_part if total_k is None else total_k + key_part
        current = coming
    key_grad = total_k[:, :HD].astype(jnp.bfloat16)
    value_grad = total_v.astype(jnp.bfloat16)
    for head in range(cols // HD):

        @pl.when(pl.program_id(0) == head)
        def _(head=head):
            for part, grad in enumerate((dq_ref[...], key_grad, value_grad)):
                take = slice(part * cols + head * HD, part * cols + (head + 1) * HD)
                own_ref[:, take] = grad[:rows]
                far_ref[:, take] = grad[rows:]


def attend_back_rows(queries, keys, values, upstream, logs, start, heads):
    rows = queries[0].shape[1]
    spec = pl.BlockSpec((1, rows, PAD), lambda h: (h + start, 0, 0))
    turned = pl.BlockSpec((1, HD, rows), lambda h: (h + start, 0, 0))
    line = pl.BlockSpec((1, 1, rows), lambda h: (h + start, 0, 0))
    packed = (rows, 3 * heads * HD)
    return pl.pallas_call(
        attend_back_kernel,
        out_shape=(jax.ShapeDtypeStruct(packed, jnp.bfloat16),) * 2,
        grid=(heads,),
        in_specs=[spec] * 6 + [turned] * 2 + [line] * 2,
        out_specs=(whole(packed),) * 2,
        scratch_shapes=[pltpu.VMEM((2 * rows, HD), jnp.bfloat16)],
        compiler_params=kernel_params(),
        cost_estimate=cost(heads * 4 * rows * rows * 2 * 900, heads * rows * PAD * 24),
        name="attend_back",
    )(*queries, *keys, *values, *upstream, *logs)


def merge_kernel(
    co_ref, ct_ref, wo_ref, wt_ref, frames_ref, bias_ref, gain_ref, shift_ref, middle_ref, second_ref,
):
    rows = frames_ref.shape[0]
    own, far = co_ref[...].T, ct_ref[...].T
    pieces = row_pieces(rows, 256)

    def branch(piece):
        take = slice(piece[0], piece[0] + piece[1])
        return dot_nt(own[take], wo_ref[...]) + dot_nt(far[take], wt_ref[...])

    def finish(piece, part):
        take = slice(piece[0], piece[0] + piece[1])
        middle = frames_ref[take, :].astype(jnp.float32) + part + bias_ref[...]
        middle_ref[take, :] = middle
        normed, _ = normalise(middle)
        second_ref[take, :] = (normed * gain_ref[...] + shift_ref[...]).astype(jnp.bfloat16)

    current = branch(pieces[0])
    for number, piece in enumerate(pieces):
        coming = branch(pieces[number + 1]) if number + 1 < len(pieces) else None
        finish(piece, current)
        current = coming


def merge_heads(context_own, context_far, pack, frames, bias, gain, shift):
    rows, width = frames.shape
    cols = context_own.shape[0]
    return pl.pallas_call(
        merge_kernel,
        out_shape=(
            jax.ShapeDtypeStruct((rows, width), jnp.float32),
            jax.ShapeDtypeStruct((rows, width), jnp.bfloat16),
        ),
        grid=(1,),
        in_specs=[
            whole((cols, rows)), whole((cols, rows)), whole((width, cols), (0, 3)),
            whole((width, cols), (0, 4)), whole((rows, width)), whole((1, width)), whole((1, width)), whole((1, width)),
        ],
        out_specs=(whole((rows, width)),) * 2,
        compiler_params=kernel_params(),
        cost_estimate=cost(4 * rows * width * cols, 10 * rows * width + 4 * width * cols),
        name="merge_heads",
    )(context_own, context_far, pack, pack, frames, bias, gain, shift)


def feed_kernel(
    second_ref, grad_ref, expand_ref, reduce_ref, bias_ref,
    hidden_ref, back_ref, bsum_ref, out_ref, terms_ref, out_acc, terms_acc,
):
    step = pl.program_id(0)
    rows = second_ref.shape[0]
    pieces = row_pieces(rows, 376 if rows % 376 == 0 else 256)
    expand, reduce = expand_ref[...], reduce_ref[...]

    def begin(piece):
        take = slice(piece[0], piece[0] + piece[1])
        return dot_nn(second_ref[take, :], expand), dot_nn(grad_ref[take, :], reduce)

    @pl.when(step == 0)
    def _():
        out_acc[...] = jnp.zeros_like(out_acc)
        terms_acc[...] = jnp.zeros_like(terms_acc)

    sums = None
    current = begin(pieces[0])
    for number, piece in enumerate(pieces):
        coming = begin(pieces[number + 1]) if number + 1 < len(pieces) else None
        take = slice(piece[0], piece[0] + piece[1])
        raw, upstream = current
        raw = raw + bias_ref[...]
        below = 0.5 + 0.5 * lax.erf(raw * 0.7071067811865476)
        density = jnp.exp(raw * raw * -0.5) * 0.3989422804014327
        hidden = (raw * below).astype(jnp.bfloat16)
        back = (upstream * (below + raw * density)).astype(jnp.bfloat16)
        hidden_ref[take, :] = hidden
        back_ref[take, :] = back
        part = jnp.sum(back.astype(jnp.float32), axis=0, keepdims=True)
        sums = part if sums is None else sums + part
        terms_acc[take, :] += dot_nt(back, expand)
        out_acc[take, :] += dot_nt(hidden, reduce)
        current = coming
    bsum_ref[...] = sums

    @pl.when(step == pl.num_programs(0) - 1)
    def _():
        out_ref[...] = out_acc[...].astype(jnp.bfloat16)
        terms_ref[...] = terms_acc[...].astype(jnp.bfloat16)


def feed(second, grads, pack, bias, units):
    rows, width = second.shape
    block = 512 if units % 512 == 0 else units
    wide = pl.BlockSpec((rows, block), lambda j: (0, j))
    steps = units // block
    weights = [
        pl.BlockSpec((width, block), lambda j: (0, j)),
        pl.BlockSpec((width, block), lambda j: (0, j + steps)),
    ]
    line = pl.BlockSpec((1, block), lambda j: (0, j))
    return pl.pallas_call(
        feed_kernel,
        out_shape=(
            jax.ShapeDtypeStruct((rows, units), jnp.bfloat16),
            jax.ShapeDtypeStruct((rows, units), jnp.bfloat16),
            jax.ShapeDtypeStruct((1, units), jnp.float32),
            jax.ShapeDtypeStruct((rows, width), jnp.bfloat16),
            jax.ShapeDtypeStruct((rows, width), jnp.bfloat16),
        ),
        grid=(units // block,),
        in_specs=[whole((rows, width)), whole((rows, width)), *weights, line],
        out_specs=(wide, wide, line, whole((rows, width)), whole((rows, width))),
        scratch_shapes=[pltpu.VMEM((rows, width), jnp.float32)] * 2,
        compiler_params=kernel_params(),
        cost_estimate=cost(8 * rows * width * units, 8 * rows * (units + width) + 4 * width * units),
        name="feed",
    )(second, grads, pack, pack, bias)


def feed_grad_kernel(go_ref, gt_ref, so_ref, st_ref, ho_ref, ht_ref, bo_ref, bt_ref, out_ref):
    step = pl.program_id(0)
    half = pl.num_programs(0) // 2

    @pl.when(step < half)
    def _():
        total = dot_tn(go_ref[...], ho_ref[...]) + dot_tn(gt_ref[...], ht_ref[...])
        out_ref[...] = total.astype(jnp.bfloat16)

    @pl.when(step >= half)
    def _():
        total = dot_tn(so_ref[...], bo_ref[...]) + dot_tn(st_ref[...], bt_ref[...])
        out_ref[...] = total.astype(jnp.bfloat16)


def feed_grads(grads, second, hidden, back):
    rows, width = grads[0].shape
    units = hidden[0].shape[1]
    block = 512 if units % 512 == 0 else units
    steps = units // block
    early = pl.BlockSpec((rows, block), lambda j: (0, jnp.minimum(j, steps - 1)))
    late = pl.BlockSpec((rows, block), lambda j: (0, jnp.maximum(j - steps, 0)))
    return pl.pallas_call(
        feed_grad_kernel,
        out_shape=jax.ShapeDtypeStruct((width, 2 * units), jnp.bfloat16),
        grid=(2 * steps,),
        in_specs=[whole((rows, width))] * 4 + [early] * 2 + [late] * 2,
        out_specs=pl.BlockSpec((width, block), lambda j: (0, j)),
        compiler_params=kernel_params(),
        cost_estimate=cost(8 * rows * width * units, 8 * rows * (width + units) + 4 * width * units),
        name="feed_grads",
    )(*grads, *second, *hidden, *back)


def head_grad_kernel(count, lo_ref, lt_ref, *refs):
    out_ref = refs[2 * count]
    offset = 0
    for own_ref, far_ref in zip(refs[:count], refs[count : 2 * count]):
        wide = own_ref.shape[1]
        total = dot_tn(lo_ref[...], own_ref[...]) + dot_tn(lt_ref[...], far_ref[...])
        lane = lax.broadcasted_iota(jnp.int32, (1, wide), 1)
        total = total * jnp.where(lane < wide // 3, HD ** (-0.5), 1.0)
        out_ref[:, offset : offset + wide] = total.astype(jnp.bfloat16)
        offset += wide


def head_grad(lefts, own, far):
    rows, width = lefts[0].shape
    units = sum(pack.shape[1] for pack in own)
    block = 256 if width % 256 == 0 else width
    left = pl.BlockSpec((rows, block), lambda j: (0, j))
    return pl.pallas_call(
        functools.partial(head_grad_kernel, len(own)),
        out_shape=jax.ShapeDtypeStruct((width, units), jnp.bfloat16),
        grid=(width // block,),
        in_specs=[left] * 2 + [whole(pack.shape) for pack in (*own, *far)],
        out_specs=pl.BlockSpec((block, units), lambda j: (j, 0)),
        compiler_params=kernel_params(),
        cost_estimate=cost(4 * rows * width * units, 4 * rows * (width + units) + 2 * width * units),
        name="head_grad",
    )(*lefts, *own, *far)


def branch_kernel(
    own_ref, far_ref, middle_ref, grad_ref, gain_ref, wo_ref, wt_ref,
    mgrad_ref, branch_ref, go_ref, gt_ref, sums_ref,
):
    rows, width = middle_ref.shape
    pieces = row_pieces(rows, 256)

    def step_back(piece):
        take = slice(piece[0], piece[0] + piece[1])
        second_grad = own_ref[take, :].astype(jnp.float32) + far_ref[take, :].astype(jnp.float32)
        normed, inverse = normalise(middle_ref[take, :])
        wide = grad_ref[take, :].astype(jnp.float32)
        moved = second_grad * normed
        tilted = second_grad * gain_ref[...]
        mgrad = wide + inverse * (
            tilted
            - jnp.mean(tilted, axis=-1, keepdims=True)
            - normed * jnp.mean(tilted * normed, axis=-1, keepdims=True)
        )
        branch = mgrad.astype(jnp.bfloat16)
        mgrad_ref[take, :] = mgrad
        branch_ref[take, :] = branch
        sums = [
            jnp.sum(moved, axis=0, keepdims=True),
            jnp.sum(second_grad, axis=0, keepdims=True),
            jnp.sum(branch.astype(jnp.float32), axis=0, keepdims=True),
            jnp.sum(wide, axis=0, keepdims=True),
        ]
        return branch, sums

    def finish(piece, branch):
        take = slice(piece[0], piece[0] + piece[1])
        go_ref[:, take] = dot_nn(branch, wo_ref[...]).astype(jnp.bfloat16).T
        gt_ref[:, take] = dot_nn(branch, wt_ref[...]).astype(jnp.bfloat16).T

    totals = None
    branch, sums = step_back(pieces[0])
    totals = sums
    for number, piece in enumerate(pieces):
        now = branch
        if number + 1 < len(pieces):
            branch, sums = step_back(pieces[number + 1])
            totals = [a + b for a, b in zip(totals, sums)]
        finish(piece, now)
    for index, line in enumerate(totals):
        sums_ref[index : index + 1, :] = line


def branch_back(own, far, middle, grads, gain, pack, cols):
    rows, width = middle.shape
    full = whole((rows, width))
    return pl.pallas_call(
        branch_kernel,
        out_shape=(
            jax.ShapeDtypeStruct((rows, width), jnp.float32),
            jax.ShapeDtypeStruct((rows, width), jnp.bfloat16),
            jax.ShapeDtypeStruct((cols, rows), jnp.bfloat16),
            jax.ShapeDtypeStruct((cols, rows), jnp.bfloat16),
            jax.ShapeDtypeStruct((4, width), jnp.float32),
        ),
        grid=(1,),
        in_specs=[
            full, full, full, full, whole((1, width)), whole((width, cols), (0, 3)), whole((width, cols), (0, 4))
        ],
        out_specs=(full, full, whole((cols, rows)), whole((cols, rows)), whole((4, width))),
        compiler_params=kernel_params(),
        cost_estimate=cost(4 * rows * width * cols, 18 * rows * width),
        name="branch_back",
    )(own, far, middle, grads, gain, pack, pack)


def out_grad_kernel(branch_ref, co_ref, ct_ref, out_ref):
    cols = co_ref.shape[0]
    branch = branch_ref[...]
    out_ref[:, :cols] = dot_tn(branch, co_ref[...].T).astype(jnp.bfloat16)
    out_ref[:, cols:] = dot_tn(branch, ct_ref[...].T).astype(jnp.bfloat16)


def out_weight_grad(branch, context_own, context_far):
    rows, width = branch.shape
    cols = context_own.shape[0]
    return pl.pallas_call(
        out_grad_kernel,
        out_shape=jax.ShapeDtypeStruct((width, 2 * cols), jnp.bfloat16),
        grid=(1,),
        in_specs=[whole((rows, width)), whole((cols, rows)), whole((cols, rows))],
        out_specs=whole((width, 2 * cols)),
        compiler_params=kernel_params(),
        cost_estimate=cost(4 * rows * width * cols, 4 * rows * width + 4 * width * cols),
        name="out_weight_grad",
    )(branch, context_own, context_far)


def first_kernel(count, *refs):
    packs, (weight_ref, frames_ref, terms_ref, sums_ref, bias_ref, pack_ref) = refs[:count], refs[count:]
    rows, width = frames_ref.shape
    cols = pack_ref.shape[1] // 3
    q_factor = HD ** (-0.5)
    pieces = row_pieces(rows, 256)
    offset = 0
    for ref in packs:
        wide = ref.shape[1] // 3
        for part in range(3):
            place = part * cols + offset
            pack_ref[:, place : place + wide] = ref[:, part * wide : (part + 1) * wide]
        offset += wide

    def begin(piece):
        take = slice(piece[0], piece[0] + piece[1])
        return dot_nt(pack_ref[take, :cols], weight_ref[:, :cols]) * q_factor + dot_nt(
            pack_ref[take, cols:], weight_ref[:, cols:]
        )

    totals = None
    current = begin(pieces[0])
    for number, piece in enumerate(pieces):
        coming = begin(pieces[number + 1]) if number + 1 < len(pieces) else None
        take = slice(piece[0], piece[0] + piece[1])
        terms_ref[take, :] = current.astype(jnp.bfloat16)
        normed, _ = normalise(frames_ref[take, :].astype(jnp.float32))
        sums = [
            jnp.sum(current * normed, axis=0, keepdims=True),
            jnp.sum(current, axis=0, keepdims=True),
            jnp.sum(pack_ref[take, :].astype(jnp.float32), axis=0, keepdims=True),
        ]
        totals = sums if totals is None else [a + b for a, b in zip(totals, sums)]
        current = coming
    sums_ref[0:1, :] = totals[0]
    sums_ref[1:2, :] = totals[1]
    bias_ref[...] = totals[2]


def first_back(packs, weights, frames):
    rows, width = frames.shape
    wide = sum(pack.shape[1] for pack in packs)
    return pl.pallas_call(
        functools.partial(first_kernel, len(packs)),
        out_shape=(
            jax.ShapeDtypeStruct((rows, width), jnp.bfloat16),
            jax.ShapeDtypeStruct((2, width), jnp.float32),
            jax.ShapeDtypeStruct((1, wide), jnp.float32),
        ),
        grid=(1,),
        in_specs=[whole(pack.shape) for pack in packs] + [whole((width, wide)), whole((rows, width))],
        out_specs=(whole((rows, width)), whole((2, width)), whole((1, wide))),
        scratch_shapes=[pltpu.VMEM((rows, wide), jnp.bfloat16)],
        compiler_params=kernel_params(),
        cost_estimate=cost(2 * rows * width * wide, 2 * (rows + width) * wide + 4 * rows * width),
        name="first_back",
    )(*packs, weights, frames)


def frames_kernel(frames_ref, own_ref, far_ref, mgrad_ref, gain_ref, out_ref):
    normed, inverse = normalise(frames_ref[...].astype(jnp.float32))
    tilted = (own_ref[...].astype(jnp.float32) + far_ref[...].astype(jnp.float32)) * gain_ref[...]
    out_ref[...] = (
        mgrad_ref[...]
        + inverse
        * (
            tilted
            - jnp.mean(tilted, axis=-1, keepdims=True)
            - normed * jnp.mean(tilted * normed, axis=-1, keepdims=True)
        )
    ).astype(jnp.bfloat16)


def frames_back(frames, own, far, mgrad, gain):
    rows, width = frames.shape
    block = 376 if rows % 376 == 0 else rows
    spec = pl.BlockSpec((block, width), lambda i: (i, 0))
    return pl.pallas_call(
        frames_kernel,
        out_shape=jax.ShapeDtypeStruct((rows, width), jnp.bfloat16),
        grid=(rows // block,),
        in_specs=[spec] * 4 + [whole((1, width))],
        out_specs=spec,
        compiler_params=kernel_params(),
        cost_estimate=cost(20 * rows * width, 12 * rows * width),
        name="frames_back",
    )(frames, own, far, mgrad, gain)


def swap_tp(piece):
    return lax.ppermute(piece, "tp", [(0, 1), (1, 0)])


def tie(*values):
    return lax.optimization_barrier(values)


def gather_steps(vector, other, fsdp):
    index = lax.axis_index("fsdp")
    side = lax.axis_index("tp")
    held = jnp.where(side == 0, jnp.stack([vector, other]), jnp.stack([other, vector]))
    bit = 1
    while bit < fsdp:
        other = lax.ppermute(held, "fsdp", [(i, i ^ bit) for i in range(fsdp)])
        low = (index & bit) == 0
        held = jnp.where(low, jnp.concatenate([held, other]), jnp.concatenate([other, held]))
        bit *= 2
    return held


def halving_order(fsdp):
    return [bit for bit in (1, 2, 8, 4, 16, 32, 64, 128) if bit < fsdp]


def halve(held, bit, left, fsdp, last=False):
    index = lax.axis_index("fsdp")
    mine = (index // bit) % 2
    parts = held if isinstance(held, list) else [held]
    outer = 2 ** sorted(left, reverse=True).index(bit)
    views = [part.reshape(outer, 2, -1, part.shape[-1]) for part in parts]

    def chosen(which):
        return jnp.concatenate(
            [lax.dynamic_index_in_dim(view, which, 1, keepdims=False) for view in views], axis=-1
        )

    other = lax.ppermute(chosen(1 - mine), "fsdp", [(i, i ^ bit) for i in range(fsdp)])
    total = chosen(mine).astype(jnp.float32) + other.astype(jnp.float32)
    return (total if last else total.astype(jnp.bfloat16)).reshape(-1, total.shape[-1])


def scatter_steps(held, fsdp):
    index = lax.axis_index("fsdp")
    bit = fsdp // 2
    while bit >= 1:
        low = (index & bit) == 0
        first, second = held[:bit], held[bit:]
        send = jnp.where(low, second, first)
        held = jnp.where(low, first, second) + lax.ppermute(
            send, "fsdp", [(i, i ^ bit) for i in range(fsdp)]
        )
        bit //= 2
    return held[0]


def per_device_pair(
    frames, out_grad, clip_lengths, clip_order, w_query, w_key, w_value, b_query, b_value,
    w_out, b_out, w_expand, b_expand, w_reduce, b_reduce,
    first_gain, first_shift, second_gain, second_shift, *, fsdp,
):
    side = lax.axis_index("tp")
    slot = lax.axis_index("fsdp")
    clip_count = clip_order.shape[0]
    every_clip = jnp.arange(clip_count, dtype=jnp.int32)
    clip_id = jnp.sum(jnp.where(every_clip == slot, clip_order, 0))
    length = jnp.sum(jnp.where(every_clip == clip_id, clip_lengths, 0))
    frames, out_grad = frames[0], out_grad[0]
    rows, width = frames.shape
    cols = w_query.shape[1]
    heads = cols // HD
    units = w_expand.shape[1]
    q_factor = HD ** (-0.5)
    scal_own = jnp.stack([length, side * rows]).astype(jnp.int32)
    scal_far = jnp.stack([length, (1 - side) * rows]).astype(jnp.int32)

    wide_six = [first_gain, first_shift, second_gain, second_shift, b_out, b_reduce]
    small_own = jnp.concatenate(wide_six + [b_query, b_value, b_expand])
    out_turned = w_out.T
    small_far, out_other = swap_tp(small_own), swap_tp(out_turned)
    pack_one = lax.all_gather(
        jnp.concatenate([w_query, w_key, w_value, out_turned, out_other], axis=1),
        "fsdp", axis=0, tiled=True,
    )
    pack_two = lax.all_gather(
        jnp.concatenate([w_expand, w_reduce.T], axis=1), "fsdp", axis=0, tiled=True
    )
    sent_frames, small_far, out_other = tie(frames, small_far, out_other)
    frames_far = swap_tp(sent_frames)
    sent_grads, frames_far = tie(out_grad, frames_far)
    grads_far = swap_tp(sent_grads)
    small = gather_steps(small_own, small_far, fsdp)
    lot = first_gain.shape[0]
    whole_six = small[:, : 6 * lot].astype(jnp.float32).reshape(2 * fsdp, 6, lot)
    whole_six = whole_six.transpose(1, 0, 2).reshape(6, 1, width)
    gain_one, shift_one, gain_two, shift_two, out_bias, reduce_bias = [whole_six[i] for i in range(6)]
    mine = lax.dynamic_index_in_dim(
        small[:, 6 * lot :].astype(jnp.float32).reshape(fsdp, 2, -1), side, axis=1, keepdims=False
    )
    part = b_query.shape[0]
    bias_q = mine[:, :part].reshape(1, -1)
    bias_v = mine[:, part : 2 * part].reshape(1, -1)
    bias_e = mine[:, 2 * part :].reshape(1, -1)

    first_own, q_own, k_own, v_own = project(
        scal_own, frames, gain_one, shift_one, pack_one, bias_q, bias_v, heads
    )
    first_far, q_far, k_far, v_far = project(
        scal_far, frames_far, gain_one, shift_one, pack_one, bias_q, bias_v, heads
    )
    context_send, log_far = attend_rows(q_far, k_own, k_far, v_own, v_far)
    context_send, q_own = tie(context_send, q_own)
    context_far = swap_tp(context_send.reshape(cols, rows))
    context_own, log_own = attend_rows(q_own, k_own, k_far, v_own, v_far)
    context_own = context_own.reshape(cols, rows)
    middle, second_own = merge_heads(
        context_own, context_far, pack_one, frames, out_bias, gain_two, shift_two
    )

    second_far = swap_tp(second_own)
    hid_far, back_far, bsum_far, out_send, terms_send = feed(
        second_far, grads_far, pack_two, bias_e, units
    )
    terms_send, second_own = tie(terms_send, second_own)
    terms_far = swap_tp(terms_send)
    hid_own, back_own, bsum_own, out_own, terms_own = feed(
        second_own, out_grad, pack_two, bias_e, units
    )
    mgrad, branch, up_own, up_send, sums_two = branch_back(
        terms_own, terms_far, middle, out_grad, gain_two, pack_one, cols
    )
    up_send, second_own = tie(up_send, second_own)
    up_far = swap_tp(up_send)
    d_feed = feed_grads(
        (out_grad, grads_far), (second_own, second_far), (hid_own, hid_far), (back_own, back_far)
    )
    g_feed = lax.psum_scatter(d_feed, "fsdp", scatter_dimension=0, tiled=True)
    d_out = out_weight_grad(branch, context_own, context_far)

    turned = (heads, HD, rows)
    up_far, d_out, out_send = tie(up_far, d_out, out_send)
    out_far = swap_tp(out_send)
    ups = (up_own.reshape(turned), up_far.reshape(turned))
    steps = halving_order(fsdp)
    firsts = (first_own, first_far)

    def back(q_first, start, count):
        return attend_back_rows(
            (q_first, q_far), (k_own, k_far), (v_own, v_far), ups, (log_own, log_far), start, count
        )

    many = heads // 2
    few = many // 2
    own_a, far_a = back(q_own, 0, many)
    d_heads = head_grad(firsts, [own_a], [far_a])
    d_heads, q_own = tie(d_heads, q_own)
    held_a = [d_out, d_heads]
    own_b, far_b = back(q_own, many, few)
    held_a = halve(held_a, steps[0], steps, fsdp)
    own_b, held_a, q_own = tie(own_b, held_a, q_own)
    own_c, far_c = back(q_own, many + few, many - few)
    held_a = halve(held_a, steps[1], steps[1:], fsdp)
    far_c, out_far = tie(far_c, out_far)
    first_send, sums_far, bias_far = first_back([far_a, far_b, far_c], pack_one, frames_far)
    first_send, far_c = tie(first_send, far_c)
    first_recv = swap_tp(first_send)
    held_b = head_grad(firsts, [own_b, own_c], [far_b, far_c])
    held_b, own_c = tie(held_b, own_c)
    first_keep, sums_own, bias_own = first_back([own_a, own_b, own_c], pack_one, frames)
    held_b = halve(held_b, steps[0], steps, fsdp)
    held_b = halve(held_b, steps[1], steps[1:], fsdp)
    frames_grad = frames_back(frames, first_keep, first_recv, mgrad, gain_one)
    out_frames = (
        middle + out_own.astype(jnp.float32) + out_far.astype(jnp.float32) + reduce_bias
    ).astype(jnp.bfloat16)
    for place in range(2, len(steps)):
        last = place + 1 == len(steps)
        held_a = halve(held_a, steps[place], steps[place:], fsdp, last)
        if place == 2:
            held_b, frames_grad, out_frames = tie(held_b, frames_grad, out_frames)
        held_b = halve(held_b, steps[place], steps[place:], fsdp, last)
    g_out, held_a = held_a[:, : 2 * cols], held_a[:, 2 * cols :]
    some, fewer = many * HD, few * HD

    def joined(kind):
        ends = 3 * fewer
        return jnp.concatenate(
            [
                held_a[:, kind * some : (kind + 1) * some],
                held_b[:, kind * fewer : (kind + 1) * fewer],
                held_b[:, ends + kind * (some - fewer) : ends + (kind + 1) * (some - fewer)],
            ],
            axis=1,
        )

    g_query, g_key, g_value = joined(0), joined(1), joined(2)

    sums_one = sums_own + sums_far
    bias_sum = bias_own + bias_far
    wide_sums = jnp.concatenate([sums_one, sums_two])
    wide_sums = wide_sums.reshape(6, fsdp, 2, lot).transpose(1, 2, 0, 3).reshape(fsdp, 12 * lot)
    tall = jnp.concatenate(
        [
            wide_sums,
            (bias_sum[:, :cols] * q_factor).reshape(fsdp, -1),
            bias_sum[:, 2 * cols :].reshape(fsdp, -1),
            (bsum_own + bsum_far).reshape(fsdp, -1),
        ],
        axis=1,
    )
    small_sum = scatter_steps(tall, fsdp)
    six = small_sum[: 12 * lot].reshape(2, 6 * lot)
    keep = lax.dynamic_index_in_dim(six, side, 0, keepdims=False)
    send = lax.dynamic_index_in_dim(six, 1 - side, 0, keepdims=False)
    six = (keep + swap_tp(send)).reshape(6, lot)
    rest = small_sum[12 * lot :]
    g_bq, g_bv, g_be = rest[:part], rest[part : 2 * part], rest[2 * part :]
    g_out_sum = g_out[:, :cols] + swap_tp(g_out[:, cols:].astype(jnp.bfloat16)).astype(jnp.float32)
    return (
        out_frames[None],
        frames_grad[None],
        g_query,
        g_key,
        g_value,
        g_bq,
        g_bv,
        g_out_sum.T,
        six[4],
        g_feed[:, units:].astype(jnp.float32),
        g_be,
        g_feed[:, :units].T.astype(jnp.float32),
        six[5],
        six[0],
        six[1],
        six[2],
        six[3],
    )


def solution(mesh):
    fsdp = mesh.shape["fsdp"]
    if mesh.shape["tp"] == 2 and fsdp & (fsdp - 1) == 0:

        def body(*args):
            return per_device_pair(*args, fsdp=fsdp) if args[0].shape[0] == 1 else per_device(*args)
    else:
        body = per_device
    return jax.shard_map(
        body,
        mesh=mesh,
        in_specs=(
            P("fsdp", "tp", None),
            P("fsdp", "tp", None),
            P(),
            P(),
            P("fsdp", "tp"),
            P("fsdp", "tp"),
            P("fsdp", "tp"),
            P(("tp", "fsdp")),
            P(("tp", "fsdp")),
            P("tp", "fsdp"),
            P(("fsdp", "tp")),
            P("fsdp", "tp"),
            P(("tp", "fsdp")),
            P("tp", "fsdp"),
            P(("fsdp", "tp")),
            P(("fsdp", "tp")),
            P(("fsdp", "tp")),
            P(("fsdp", "tp")),
            P(("fsdp", "tp")),
        ),
        out_specs=(
            P("fsdp", "tp", None),
            P("fsdp", "tp", None),
            P("fsdp", "tp"),
            P("fsdp", "tp"),
            P("fsdp", "tp"),
            P(("tp", "fsdp")),
            P(("tp", "fsdp")),
            P("tp", "fsdp"),
            P(("fsdp", "tp")),
            P("fsdp", "tp"),
            P(("tp", "fsdp")),
            P("tp", "fsdp"),
            P(("fsdp", "tp")),
            P(("fsdp", "tp")),
            P(("fsdp", "tp")),
            P(("fsdp", "tp")),
            P(("fsdp", "tp")),
        ),
        check_vma=False,
    )
```

```python
import functools

import jax
import jax.numpy as jnp
from jax import lax
from jax.experimental import pallas as pl
from jax.experimental.pallas import tpu as pltpu
from jax.sharding import PartitionSpec as P

HD = 80


EPSILON = 1e-05
MASKED = -1000000000.0
HIDDEN = -1e30


def layer_norm(features, norm_gain, norm_shift):
    row_mean = jnp.mean(features, axis=-1, keepdims=True)
    centred = features - row_mean
    row_var = jnp.mean(centred * centred, axis=-1, keepdims=True)
    inverse = lax.rsqrt(row_var + EPSILON)
    normed = centred * inverse
    return (normed * norm_gain + norm_shift, normed, inverse)


def norm_back(upstream, normed, inverse, norm_gain):
    tilted = upstream * norm_gain
    return inverse * (
        tilted
        - jnp.mean(tilted, axis=-1, keepdims=True)
        - normed * jnp.mean(tilted * normed, axis=-1, keepdims=True)
    )


def gelu_exact(inputs):
    return jax.nn.gelu(inputs, approximate=False)


def masked_scores(queries, key_rows, length):
    scores = jnp.einsum("qhe,khe->hqk", queries, key_rows, preferred_element_type=jnp.float32)
    allowed = jnp.arange(scores.shape[-1]) < length
    return jnp.where(allowed[None, None, :], scores, MASKED)


def attend(inputs):
    queries, key_rows, value_rows, length = inputs
    scores = masked_scores(queries, key_rows, length)
    row_top = jnp.max(scores, axis=-1, keepdims=True)
    raised = jnp.exp(scores - row_top)
    row_sum = jnp.sum(raised, axis=-1, keepdims=True)
    weights = (raised / row_sum).astype(jnp.bfloat16)
    context = jnp.einsum("hqk,khe->qhe", weights, value_rows, preferred_element_type=jnp.float32)
    return (context.astype(jnp.bfloat16), row_top[..., 0] + jnp.log(row_sum[..., 0]))


def attend_back(inputs):
    queries, key_rows, value_rows, length, log_total, context_grad = inputs
    scores = masked_scores(queries, key_rows, length)
    probs = jnp.exp(scores - log_total[..., None])
    weights = probs.astype(jnp.bfloat16)
    value_grad = jnp.einsum(
        "hqk,qhe->khe", weights, context_grad, preferred_element_type=jnp.float32
    )
    weight_grad = jnp.einsum(
        "qhe,khe->hqk", context_grad, value_rows, preferred_element_type=jnp.float32
    )
    row_inner = jnp.sum(weight_grad * probs, axis=-1, keepdims=True)
    score_grad = (probs * (weight_grad - row_inner)).astype(jnp.bfloat16)
    query_grad = jnp.einsum(
        "hqk,khe->qhe", score_grad, key_rows, preferred_element_type=jnp.float32
    )
    key_grad = jnp.einsum("hqk,qhe->khe", score_grad, queries, preferred_element_type=jnp.float32)
    return (
        query_grad.astype(jnp.bfloat16),
        key_grad.astype(jnp.bfloat16),
        value_grad.astype(jnp.bfloat16),
    )


def gather_inward(w_query, w_key, w_value, b_query, b_value, w_expand, b_expand):
    return (
        lax.all_gather(w_query, "fsdp", axis=0, tiled=True),
        lax.all_gather(w_key, "fsdp", axis=0, tiled=True),
        lax.all_gather(w_value, "fsdp", axis=0, tiled=True),
        lax.all_gather(b_query, "fsdp", axis=0, tiled=True),
        lax.all_gather(b_value, "fsdp", axis=0, tiled=True),
        lax.all_gather(w_expand, "fsdp", axis=0, tiled=True),
        lax.all_gather(b_expand, "fsdp", axis=0, tiled=True),
    )


def gather_outward(w_out, w_reduce):
    return (
        lax.all_gather(w_out, "fsdp", axis=1, tiled=True),
        lax.all_gather(w_reduce, "fsdp", axis=1, tiled=True),
    )


def per_device(
    frames,
    out_grad,
    clip_lengths,
    clip_order,
    w_query,
    w_key,
    w_value,
    b_query,
    b_value,
    w_out,
    b_out,
    w_expand,
    b_expand,
    w_reduce,
    b_reduce,
    first_gain,
    first_shift,
    second_gain,
    second_shift,
):
    per_group = frames.shape[0]
    clip_count = clip_order.shape[0]
    slot_ids = lax.axis_index("fsdp") * per_group + jnp.arange(per_group, dtype=jnp.int32)
    every_clip = jnp.arange(clip_count, dtype=jnp.int32)
    clip_ids = jnp.sum(
        jnp.where(every_clip[None, :] == slot_ids[:, None], clip_order[None, :], 0), axis=1
    )
    lengths = jnp.sum(
        jnp.where(every_clip[None, :] == clip_ids[:, None], clip_lengths[None, :], 0), axis=1
    )
    norm_params = (
        lax.all_gather(first_gain, ("fsdp", "tp"), axis=0, tiled=True),
        lax.all_gather(first_shift, ("fsdp", "tp"), axis=0, tiled=True),
        lax.all_gather(second_gain, ("fsdp", "tp"), axis=0, tiled=True),
        lax.all_gather(second_shift, ("fsdp", "tp"), axis=0, tiled=True),
        lax.all_gather(b_out, ("fsdp", "tp"), axis=0, tiled=True),
        lax.all_gather(b_reduce, ("fsdp", "tp"), axis=0, tiled=True),
    )
    gain_one, shift_one, gain_two, shift_two, out_bias, reduce_bias = [
        tensor.astype(jnp.float32) for tensor in norm_params
    ]
    wq_all, wk_all, wv_all, bq_all, bv_all, we_all, be_all = gather_inward(
        w_query, w_key, w_value, b_query, b_value, w_expand, b_expand
    )
    wo_all, wr_all = gather_outward(w_out, w_reduce)
    q_factor = HD ** (-0.5)
    frames_wide = frames.astype(jnp.float32)
    norm_one, normed_one, inverse_one = layer_norm(frames_wide, gain_one, shift_one)
    first_rows = lax.all_gather(norm_one.astype(jnp.bfloat16), "tp", axis=1, tiled=True)
    seq_len = first_rows.shape[1]
    queries = (
        (
            jnp.einsum("csd,de->cse", first_rows, wq_all, preferred_element_type=jnp.float32)
            + bq_all.astype(jnp.float32)
        )
        * q_factor
    ).astype(jnp.bfloat16)
    keys = jnp.einsum("csd,de->cse", first_rows, wk_all, preferred_element_type=jnp.float32).astype(
        jnp.bfloat16
    )
    values = (
        jnp.einsum("csd,de->cse", first_rows, wv_all, preferred_element_type=jnp.float32)
        + bv_all.astype(jnp.float32)
    ).astype(jnp.bfloat16)
    head_shape = (per_group, seq_len, -1, HD)
    query_heads = queries.reshape(head_shape)
    key_heads = keys.reshape(head_shape)
    value_heads = values.reshape(head_shape)
    context, log_total = lax.map(attend, (query_heads, key_heads, value_heads, lengths))
    context_flat = context.reshape(per_group, seq_len, -1)
    attn_terms = jnp.einsum("cse,ed->csd", context_flat, wo_all, preferred_element_type=jnp.float32)
    attn_part = lax.psum_scatter(
        attn_terms.astype(jnp.bfloat16), "tp", scatter_dimension=1, tiled=True
    ).astype(jnp.float32)
    middle = frames_wide + attn_part + out_bias
    norm_two, normed_two, inverse_two = layer_norm(middle, gain_two, shift_two)
    second_rows = lax.all_gather(norm_two.astype(jnp.bfloat16), "tp", axis=1, tiled=True)
    expanded = jnp.einsum(
        "csd,df->csf", second_rows, we_all, preferred_element_type=jnp.float32
    ) + be_all.astype(jnp.float32)
    activated, gelu_pull = jax.vjp(gelu_exact, expanded)
    hidden = activated.astype(jnp.bfloat16)
    mlp_terms = jnp.einsum("csf,fd->csd", hidden, wr_all, preferred_element_type=jnp.float32)
    out_frames = (
        middle
        + lax.psum_scatter(
            mlp_terms.astype(jnp.bfloat16), "tp", scatter_dimension=1, tiled=True
        ).astype(jnp.float32)
        + reduce_bias
    ).astype(jnp.bfloat16)
    wq_all, wk_all, wv_all, bq_all, bv_all, we_all, be_all = gather_inward(
        w_query, w_key, w_value, b_query, b_value, w_expand, b_expand
    )
    wo_all, wr_all = gather_outward(w_out, w_reduce)
    grad_wide = out_grad.astype(jnp.float32)
    grad_rows = lax.all_gather(out_grad, "tp", axis=1, tiled=True)
    w_reduce_grad = jnp.einsum("csf,csd->fd", hidden, grad_rows, preferred_element_type=jnp.float32)
    hidden_grad = jnp.einsum("csd,fd->csf", grad_rows, wr_all, preferred_element_type=jnp.float32)
    expanded_grad = gelu_pull(hidden_grad)[0].astype(jnp.bfloat16)
    b_expand_grad = jnp.sum(expanded_grad.astype(jnp.float32), axis=(0, 1))
    w_expand_grad = jnp.einsum(
        "csd,csf->df", second_rows, expanded_grad, preferred_element_type=jnp.float32
    )
    second_terms = jnp.einsum(
        "csf,df->csd", expanded_grad, we_all, preferred_element_type=jnp.float32
    )
    second_grad = lax.psum_scatter(
        second_terms.astype(jnp.bfloat16), "tp", scatter_dimension=1, tiled=True
    ).astype(jnp.float32)
    second_gain_grad = jnp.sum(second_grad * normed_two, axis=(0, 1))
    second_shift_grad = jnp.sum(second_grad, axis=(0, 1))
    middle_grad = grad_wide + norm_back(second_grad, normed_two, inverse_two, gain_two)
    branch_grad = middle_grad.astype(jnp.bfloat16)
    b_out_grad = jnp.sum(branch_grad.astype(jnp.float32), axis=(0, 1))
    b_reduce_grad = jnp.sum(grad_wide, axis=(0, 1))
    branch_rows = lax.all_gather(branch_grad, "tp", axis=1, tiled=True)
    w_out_grad = jnp.einsum(
        "cse,csd->ed", context_flat, branch_rows, preferred_element_type=jnp.float32
    )
    context_grad = jnp.einsum(
        "csd,ed->cse", branch_rows, wo_all, preferred_element_type=jnp.float32
    ).astype(jnp.bfloat16)
    query_grad, key_grad, value_grad = lax.map(
        attend_back,
        (query_heads, key_heads, value_heads, lengths, log_total, context_grad.reshape(head_shape)),
    )
    query_grad = query_grad.reshape(per_group, seq_len, -1)
    key_grad = key_grad.reshape(per_group, seq_len, -1)
    value_grad = value_grad.reshape(per_group, seq_len, -1)
    w_query_grad = (
        jnp.einsum("csd,cse->de", first_rows, query_grad, preferred_element_type=jnp.float32)
        * q_factor
    )
    b_query_grad = jnp.sum(query_grad.astype(jnp.float32), axis=(0, 1)) * q_factor
    w_key_grad = jnp.einsum("csd,cse->de", first_rows, key_grad, preferred_element_type=jnp.float32)
    w_value_grad = jnp.einsum(
        "csd,cse->de", first_rows, value_grad, preferred_element_type=jnp.float32
    )
    b_value_grad = jnp.sum(value_grad.astype(jnp.float32), axis=(0, 1))
    first_terms = (
        jnp.einsum("cse,de->csd", query_grad, wq_all, preferred_element_type=jnp.float32) * q_factor
        + jnp.einsum("cse,de->csd", key_grad, wk_all, preferred_element_type=jnp.float32)
        + jnp.einsum("cse,de->csd", value_grad, wv_all, preferred_element_type=jnp.float32)
    )
    first_grad = lax.psum_scatter(
        first_terms.astype(jnp.bfloat16), "tp", scatter_dimension=1, tiled=True
    ).astype(jnp.float32)
    first_gain_grad = jnp.sum(first_grad * normed_one, axis=(0, 1))
    first_shift_grad = jnp.sum(first_grad, axis=(0, 1))
    frames_grad = (middle_grad + norm_back(first_grad, normed_one, inverse_one, gain_one)).astype(
        jnp.bfloat16
    )
    inward_grads = (
        lax.psum_scatter(
            w_query_grad.astype(jnp.bfloat16), "fsdp", scatter_dimension=0, tiled=True
        ).astype(jnp.float32),
        lax.psum_scatter(
            w_key_grad.astype(jnp.bfloat16), "fsdp", scatter_dimension=0, tiled=True
        ).astype(jnp.float32),
        lax.psum_scatter(
            w_value_grad.astype(jnp.bfloat16), "fsdp", scatter_dimension=0, tiled=True
        ).astype(jnp.float32),
        lax.psum_scatter(
            b_query_grad.astype(jnp.bfloat16), "fsdp", scatter_dimension=0, tiled=True
        ).astype(jnp.float32),
        lax.psum_scatter(
            b_value_grad.astype(jnp.bfloat16), "fsdp", scatter_dimension=0, tiled=True
        ).astype(jnp.float32),
        lax.psum_scatter(
            w_expand_grad.astype(jnp.bfloat16), "fsdp", scatter_dimension=0, tiled=True
        ).astype(jnp.float32),
        lax.psum_scatter(
            b_expand_grad.astype(jnp.bfloat16), "fsdp", scatter_dimension=0, tiled=True
        ).astype(jnp.float32),
    )
    outward_grads = (
        lax.psum_scatter(
            w_out_grad.astype(jnp.bfloat16), "fsdp", scatter_dimension=1, tiled=True
        ).astype(jnp.float32),
        lax.psum_scatter(
            w_reduce_grad.astype(jnp.bfloat16), "fsdp", scatter_dimension=1, tiled=True
        ).astype(jnp.float32),
    )
    small_grads = (
        lax.psum_scatter(first_gain_grad, ("fsdp", "tp"), scatter_dimension=0, tiled=True),
        lax.psum_scatter(first_shift_grad, ("fsdp", "tp"), scatter_dimension=0, tiled=True),
        lax.psum_scatter(second_gain_grad, ("fsdp", "tp"), scatter_dimension=0, tiled=True),
        lax.psum_scatter(second_shift_grad, ("fsdp", "tp"), scatter_dimension=0, tiled=True),
        lax.psum_scatter(b_out_grad, ("fsdp", "tp"), scatter_dimension=0, tiled=True),
        lax.psum_scatter(b_reduce_grad, ("fsdp", "tp"), scatter_dimension=0, tiled=True),
    )
    return (
        out_frames,
        frames_grad,
        inward_grads[0],
        inward_grads[1],
        inward_grads[2],
        inward_grads[3],
        inward_grads[4],
        outward_grads[0],
        small_grads[4],
        inward_grads[5],
        inward_grads[6],
        outward_grads[1],
        small_grads[5],
        small_grads[0],
        small_grads[1],
        small_grads[2],
        small_grads[3],
    )


VMEM_LIMIT = 60 << 20
PAD = 128
COSTS = {'project': 3.0, 'attend': 3.0, 'merge_heads': 3.0, 'feed': 3.0, 'weight_grad': 3.0, 'head_grad': 0.02, 'branch_back': 3.0, 'out_weight_grad': 0.02, 'first_back': 0.02, 'frames_back': 0.02, 'attend_back': (8.0, 0.02)}


def kernel_params():
    return pltpu.CompilerParams(vmem_limit_bytes=VMEM_LIMIT)


def cost(flops, moved, scale):
    return pl.CostEstimate(flops=int(scale * flops), bytes_accessed=int(min(1.0, scale) * moved), transcendentals=0)


def row_pieces(rows, size):
    return [(start, min(size, rows - start)) for start in range(0, rows, size)]


def whole(shape, fixed=None):
    index = fixed if fixed is not None else (0,) * len(shape)
    return pl.BlockSpec(shape, lambda *_: index)


def normalise(rows):
    row_mean = jnp.mean(rows, axis=-1, keepdims=True)
    centred = rows - row_mean
    inverse = lax.rsqrt(jnp.mean(centred * centred, axis=-1, keepdims=True) + EPSILON)
    return centred * inverse, inverse


def dot_nn(left, right):
    return jnp.dot(left, right, preferred_element_type=jnp.float32)


def dot_nt(left, right):
    return lax.dot_general(left, right, (((1,), (1,)), ((), ())), preferred_element_type=jnp.float32)


def dot_tn(left, right):
    return lax.dot_general(left, right, (((0,), (0,)), ((), ())), preferred_element_type=jnp.float32)


def project_kernel(
    heads, scal_ref, frames_ref, gain_ref, shift_ref, weight_ref, bq_ref, bv_ref,
    first_ref, q_ref, k_ref, v_ref,
):
    rows, width = frames_ref.shape
    cols = heads * HD
    length, start = scal_ref[0], scal_ref[1]
    q_factor = HD ** (-0.5)
    pieces = row_pieces(rows, 256)

    def norm(piece):
        normed, _ = normalise(frames_ref[piece[0] : piece[0] + piece[1], :].astype(jnp.float32))
        first = (normed * gain_ref[...] + shift_ref[...]).astype(jnp.bfloat16)
        first_ref[piece[0] : piece[0] + piece[1], :] = first
        return first

    def split(block, offset, filler, lane):
        if offset + PAD <= block.shape[1]:
            part = block[:, offset : offset + PAD]
        else:
            back = block.shape[1] - PAD
            part = pltpu.roll(block[:, back:], PAD - (offset - back), 1)
        return jnp.where(lane < HD, part, filler).astype(jnp.bfloat16)

    def finish(piece, out):
        lane = lax.broadcasted_iota(jnp.int32, (piece[1], PAD), 1)
        position = lax.broadcasted_iota(jnp.int32, (piece[1], PAD), 0) + (start + piece[0])
        one = jnp.where(lane == HD, 1.0, 0.0)
        hide = jnp.where((lane == HD) & (position >= length), HIDDEN, 0.0)
        queries = (out[:, :cols] + bq_ref[...]) * q_factor
        keys = out[:, cols : 2 * cols]
        values = out[:, 2 * cols :] + bv_ref[...]
        for head in range(heads):
            where = (head, slice(piece[0], piece[0] + piece[1]), slice(None))
            q_ref[where] = split(queries, head * HD, one, lane)
            k_ref[where] = split(keys, head * HD, hide, lane)
            v_ref[where] = split(values, head * HD, 0.0, lane)

    first = norm(pieces[0])
    for number, piece in enumerate(pieces):
        out = dot_nn(first, weight_ref[...])
        if number + 1 < len(pieces):
            first = norm(pieces[number + 1])
        finish(piece, out)


def project(scalars, frames, gain, shift, weights, bias_q, bias_v, heads):
    rows, width = frames.shape
    cols = heads * HD
    head_out = jax.ShapeDtypeStruct((heads, rows, PAD), jnp.bfloat16)
    return pl.pallas_call(
        functools.partial(project_kernel, heads),
        out_shape=(jax.ShapeDtypeStruct((rows, width), jnp.bfloat16), head_out, head_out, head_out),
        grid_spec=pltpu.PrefetchScalarGridSpec(
            num_scalar_prefetch=1,
            grid=(1,),
            in_specs=[
                whole((rows, width)), whole((1, width)), whole((1, width)),
                whole((width, 3 * cols)), whole((1, cols)), whole((1, cols)),
            ],
            out_specs=(whole((rows, width)),) + (whole((heads, rows, PAD)),) * 3,
        ),
        compiler_params=kernel_params(),
        cost_estimate=cost(2 * rows * width * 3 * cols, 4 * rows * width + 6 * width * cols, COSTS["project"]),
        name="project",
    )(scalars, frames, gain, shift, weights, bias_q, bias_v)


def attend_kernel(q_ref, ko_ref, kt_ref, vo_ref, vt_ref, out_ref, log_ref):
    per_step, rows, _ = q_ref.shape
    half = -(-rows // 256) * 128
    pieces = [(head, start, size) for head in range(per_step) for start, size in row_pieces(rows, half)]
    keys = [jnp.concatenate([ko_ref[h], kt_ref[h]], axis=0) for h in range(per_step)]
    values = [jnp.concatenate([vo_ref[h], vt_ref[h]], axis=0).T[:HD] for h in range(per_step)]

    def scores(piece):
        head, start, size = piece
        return dot_nt(keys[head], q_ref[head, start : start + size, :])

    def finish(piece, score):
        head, start, size = piece
        top = jnp.max(score, axis=0, keepdims=True)
        raised = jnp.exp(score - top)
        total = jnp.sum(raised, axis=0, keepdims=True)
        context = dot_nn(values[head], raised.astype(jnp.bfloat16)) / total
        out_ref[head, :, start : start + size] = context.astype(jnp.bfloat16)
        log_ref[head, :, start : start + size] = top + jnp.log(total)

    current = scores(pieces[0])
    for number, piece in enumerate(pieces):
        coming = scores(pieces[number + 1]) if number + 1 < len(pieces) else None
        finish(piece, current)
        current = coming


def attend_rows(queries, keys_own, keys_far, values_own, values_far):
    heads, rows, _ = queries.shape
    per_step = 2 if heads % 2 == 0 else 1
    spec = pl.BlockSpec((per_step, rows, PAD), lambda h: (h, 0, 0))
    return pl.pallas_call(
        attend_kernel,
        out_shape=(
            jax.ShapeDtypeStruct((heads, HD, rows), jnp.bfloat16),
            jax.ShapeDtypeStruct((heads, 1, rows), jnp.float32),
        ),
        grid=(heads // per_step,),
        in_specs=[spec] * 5,
        out_specs=(
            pl.BlockSpec((per_step, HD, rows), lambda h: (h, 0, 0)),
            pl.BlockSpec((per_step, 1, rows), lambda h: (h, 0, 0)),
        ),
        compiler_params=kernel_params(),
        cost_estimate=cost(heads * 2 * rows * 2 * rows * 2 * 400, heads * rows * PAD * 12, COSTS["attend"]),
        name="attend",
    )(queries, keys_own, keys_far, values_own, values_far)


def attend_back_kernel(
    qo_ref, qt_ref, ko_ref, kt_ref, vo_ref, vt_ref, go_ref, gt_ref, lo_ref, lt_ref,
    own_ref, far_ref, dq_ref,
):
    rows = qo_ref.shape[1]
    cols = own_ref.shape[1] // 3
    keys = jnp.concatenate([ko_ref[0], kt_ref[0]], axis=0)
    values = jnp.concatenate([vo_ref[0], vt_ref[0]], axis=0)
    keys_turned = keys.T[:HD]
    pieces = [(side, start, size) for side in range(2) for start, size in row_pieces(rows, 256)]
    sides = ((qo_ref, go_ref, lo_ref), (qt_ref, gt_ref, lt_ref))

    def query(piece):
        side, start, size = piece
        return sides[side][0][0, start : start + size, :]

    def upstream(piece):
        side, start, size = piece
        return sides[side][1][0, :, start : start + size]

    def begin(piece):
        score = dot_nt(keys, query(piece))
        padded = jnp.concatenate(
            [upstream(piece), jnp.zeros((PAD - HD, piece[2]), jnp.bfloat16)], axis=0
        )
        return score, dot_nn(values, padded)

    def middle(piece, score, weight_grad):
        side, start, size = piece
        probs = jnp.exp(score - sides[side][2][0, :, start : start + size])
        tilted = probs * weight_grad
        inner = jnp.sum(tilted, axis=0, keepdims=True)
        return probs.astype(jnp.bfloat16), (tilted - probs * inner).astype(jnp.bfloat16)

    total_k = total_v = None
    current = begin(pieces[0])
    for number, piece in enumerate(pieces):
        coming = begin(pieces[number + 1]) if number + 1 < len(pieces) else None
        weights, score_grad = middle(piece, *current)
        value_part = dot_nt(weights, upstream(piece))
        key_part = dot_nn(score_grad, query(piece))
        query_grad = dot_nn(keys_turned, score_grad)
        side, start, size = piece
        dq_ref[side * rows + start : side * rows + start + size, :] = query_grad.T.astype(jnp.bfloat16)
        total_v = value_part if total_v is None else total_v + value_part
        total_k = key_part if total_k is None else total_k + key_part
        current = coming
    key_grad = total_k[:, :HD].astype(jnp.bfloat16)
    value_grad = total_v.astype(jnp.bfloat16)
    for head in range(cols // HD):

        @pl.when(pl.program_id(0) == head)
        def _(head=head):
            for part, grad in enumerate((dq_ref[...], key_grad, value_grad)):
                take = slice(part * cols + head * HD, part * cols + (head + 1) * HD)
                own_ref[:, take] = grad[:rows]
                far_ref[:, take] = grad[rows:]


def attend_back_rows(queries, keys, values, upstream, logs, start, heads):
    rows = queries[0].shape[1]
    spec = pl.BlockSpec((1, rows, PAD), lambda h: (h + start, 0, 0))
    turned = pl.BlockSpec((1, HD, rows), lambda h: (h + start, 0, 0))
    line = pl.BlockSpec((1, 1, rows), lambda h: (h + start, 0, 0))
    packed = (rows, 3 * heads * HD)
    return pl.pallas_call(
        attend_back_kernel,
        out_shape=(jax.ShapeDtypeStruct(packed, jnp.bfloat16),) * 2,
        grid=(heads,),
        in_specs=[spec] * 6 + [turned] * 2 + [line] * 2,
        out_specs=(whole(packed),) * 2,
        scratch_shapes=[pltpu.VMEM((2 * rows, HD), jnp.bfloat16)],
        compiler_params=kernel_params(),
        cost_estimate=cost(heads * 4 * rows * rows * 2 * 900, heads * rows * PAD * 24, COSTS["attend_back"][start > 0]),
        name="attend_back",
    )(*queries, *keys, *values, *upstream, *logs)


def merge_kernel(
    co_ref, ct_ref, wo_ref, wt_ref, frames_ref, bias_ref, gain_ref, shift_ref, middle_ref, second_ref,
):
    rows = frames_ref.shape[0]
    own, far = co_ref[...].T, ct_ref[...].T
    pieces = row_pieces(rows, 256)

    def branch(piece):
        take = slice(piece[0], piece[0] + piece[1])
        return dot_nt(own[take], wo_ref[...]) + dot_nt(far[take], wt_ref[...])

    def finish(piece, part):
        take = slice(piece[0], piece[0] + piece[1])
        middle = frames_ref[take, :].astype(jnp.float32) + part + bias_ref[...]
        middle_ref[take, :] = middle
        normed, _ = normalise(middle)
        second_ref[take, :] = (normed * gain_ref[...] + shift_ref[...]).astype(jnp.bfloat16)

    current = branch(pieces[0])
    for number, piece in enumerate(pieces):
        coming = branch(pieces[number + 1]) if number + 1 < len(pieces) else None
        finish(piece, current)
        current = coming


def merge_heads(context_own, context_far, pack, frames, bias, gain, shift):
    rows, width = frames.shape
    cols = context_own.shape[0]
    return pl.pallas_call(
        merge_kernel,
        out_shape=(
            jax.ShapeDtypeStruct((rows, width), jnp.float32),
            jax.ShapeDtypeStruct((rows, width), jnp.bfloat16),
        ),
        grid=(1,),
        in_specs=[
            whole((cols, rows)), whole((cols, rows)), whole((width, cols), (0, 3)),
            whole((width, cols), (0, 4)), whole((rows, width)), whole((1, width)), whole((1, width)), whole((1, width)),
        ],
        out_specs=(whole((rows, width)),) * 2,
        compiler_params=kernel_params(),
        cost_estimate=cost(4 * rows * width * cols, 10 * rows * width + 4 * width * cols, COSTS["merge_heads"]),
        name="merge_heads",
    )(context_own, context_far, pack, pack, frames, bias, gain, shift)


def feed_kernel(
    grads_too, second_ref, grad_ref, expand_ref, reduce_ref, bias_ref, *refs,
):
    if grads_too:
        far_ref, hid_ref, back_ref, bsum_ref, out_ref, terms_ref, dred_ref, out_acc, terms_acc, hidden_ref = refs
    else:
        hidden_ref, back_ref, bsum_ref, out_ref, terms_ref, out_acc, terms_acc = refs
    step = pl.program_id(0)
    rows = second_ref.shape[0]
    pieces = row_pieces(rows, 376 if rows % 376 == 0 else 256)
    expand, reduce = expand_ref[...], reduce_ref[...]

    def begin(piece):
        take = slice(piece[0], piece[0] + piece[1])
        return dot_nn(second_ref[take, :], expand), dot_nn(grad_ref[take, :], reduce)

    @pl.when(step == 0)
    def _():
        out_acc[...] = jnp.zeros_like(out_acc)
        terms_acc[...] = jnp.zeros_like(terms_acc)

    sums = None
    current = begin(pieces[0])
    for number, piece in enumerate(pieces):
        coming = begin(pieces[number + 1]) if number + 1 < len(pieces) else None
        take = slice(piece[0], piece[0] + piece[1])
        raw, upstream = current
        raw = raw + bias_ref[...]
        below = 0.5 + 0.5 * lax.erf(raw * 0.7071067811865476)
        density = jnp.exp(raw * raw * -0.5) * 0.3989422804014327
        hidden = (raw * below).astype(jnp.bfloat16)
        back = (upstream * (below + raw * density)).astype(jnp.bfloat16)
        hidden_ref[take, :] = hidden
        back_ref[take, :] = back
        part = jnp.sum(back.astype(jnp.float32), axis=0, keepdims=True)
        sums = part if sums is None else sums + part
        terms_acc[take, :] += dot_nt(back, expand)
        out_acc[take, :] += dot_nt(hidden, reduce)
        current = coming
    bsum_ref[...] = sums
    if grads_too:
        total = dot_tn(far_ref[...], hid_ref[...]) + dot_tn(grad_ref[...], hidden_ref[...])
        dred_ref[...] = total.astype(jnp.bfloat16)

    @pl.when(step == pl.num_programs(0) - 1)
    def _():
        out_ref[...] = out_acc[...].astype(jnp.bfloat16)
        terms_ref[...] = terms_acc[...].astype(jnp.bfloat16)


def feed(second, grads, pack, bias, units, far=None):
    rows, width = second.shape
    block = 512 if units % 512 == 0 else units
    steps = units // block
    wide = pl.BlockSpec((rows, block), lambda j: (0, j))
    weights = [
        pl.BlockSpec((width, block), lambda j: (0, j)),
        pl.BlockSpec((width, block), lambda j: (0, j + steps)),
    ]
    line = pl.BlockSpec((1, block), lambda j: (0, j))
    hidden = jax.ShapeDtypeStruct((rows, units), jnp.bfloat16)
    full = jax.ShapeDtypeStruct((rows, width), jnp.bfloat16)
    outs = [hidden, jax.ShapeDtypeStruct((1, units), jnp.float32), full, full]
    out_specs = [wide, line, whole((rows, width)), whole((rows, width))]
    scratch = [pltpu.VMEM((rows, width), jnp.float32)] * 2
    in_specs = [whole((rows, width)), whole((rows, width)), *weights, line]
    if far is None:
        outs, out_specs = [hidden] + outs, [wide] + out_specs
    else:
        outs = outs + [jax.ShapeDtypeStruct((width, units), jnp.bfloat16)]
        out_specs = out_specs + [weights[0]]
        in_specs = in_specs + [whole((rows, width)), wide]
        scratch = scratch + [pltpu.VMEM((rows, block), jnp.bfloat16)]
    flops = (8 if far is None else 12) * rows * width * units
    return pl.pallas_call(
        functools.partial(feed_kernel, far is not None),
        out_shape=tuple(outs),
        grid=(steps,),
        in_specs=in_specs,
        out_specs=tuple(out_specs),
        scratch_shapes=scratch,
        compiler_params=kernel_params(),
        cost_estimate=cost(flops, 8 * rows * (units + width) + 4 * width * units, COSTS["feed"]),
        name="feed" if far is None else "feed_last",
    )(second, grads, pack, pack, bias, *(far or ()))


def head_grad_kernel(count, lo_ref, lt_ref, *refs):
    out_ref = refs[2 * count]
    offset = 0
    for own_ref, far_ref in zip(refs[:count], refs[count : 2 * count]):
        wide = own_ref.shape[1]
        total = dot_tn(lo_ref[...], own_ref[...]) + dot_tn(lt_ref[...], far_ref[...])
        lane = lax.broadcasted_iota(jnp.int32, (1, wide), 1)
        total = total * jnp.where(lane < wide // 3, HD ** (-0.5), 1.0)
        out_ref[:, offset : offset + wide] = total.astype(jnp.bfloat16)
        offset += wide


def head_grad(lefts, own, far):
    rows, width = lefts[0].shape
    units = sum(pack.shape[1] for pack in own)
    block = 256 if width % 256 == 0 else width
    left = pl.BlockSpec((rows, block), lambda j: (0, j))
    return pl.pallas_call(
        functools.partial(head_grad_kernel, len(own)),
        out_shape=jax.ShapeDtypeStruct((width, units), jnp.bfloat16),
        grid=(width // block,),
        in_specs=[left] * 2 + [whole(pack.shape) for pack in (*own, *far)],
        out_specs=pl.BlockSpec((block, units), lambda j: (j, 0)),
        compiler_params=kernel_params(),
        cost_estimate=cost(4 * rows * width * units, 4 * rows * (width + units) + 2 * width * units, COSTS["head_grad"]),
        name="head_grad",
    )(*lefts, *own, *far)


def branch_kernel(
    own_ref, far_ref, middle_ref, grad_ref, gain_ref, wo_ref, wt_ref,
    mgrad_ref, branch_ref, go_ref, gt_ref, sums_ref,
):
    rows, width = middle_ref.shape
    pieces = row_pieces(rows, 256)

    def step_back(piece):
        take = slice(piece[0], piece[0] + piece[1])
        second_grad = own_ref[take, :].astype(jnp.float32) + far_ref[take, :].astype(jnp.float32)
        normed, inverse = normalise(middle_ref[take, :])
        wide = grad_ref[take, :].astype(jnp.float32)
        moved = second_grad * normed
        tilted = second_grad * gain_ref[...]
        mgrad = wide + inverse * (
            tilted
            - jnp.mean(tilted, axis=-1, keepdims=True)
            - normed * jnp.mean(tilted * normed, axis=-1, keepdims=True)
        )
        branch = mgrad.astype(jnp.bfloat16)
        mgrad_ref[take, :] = mgrad
        branch_ref[take, :] = branch
        sums = [
            jnp.sum(moved, axis=0, keepdims=True),
            jnp.sum(second_grad, axis=0, keepdims=True),
            jnp.sum(branch.astype(jnp.float32), axis=0, keepdims=True),
            jnp.sum(wide, axis=0, keepdims=True),
        ]
        return branch, sums

    def finish(piece, branch):
        take = slice(piece[0], piece[0] + piece[1])
        go_ref[:, take] = dot_nn(branch, wo_ref[...]).astype(jnp.bfloat16).T
        gt_ref[:, take] = dot_nn(branch, wt_ref[...]).astype(jnp.bfloat16).T

    totals = None
    branch, sums = step_back(pieces[0])
    totals = sums
    for number, piece in enumerate(pieces):
        now = branch
        if number + 1 < len(pieces):
            branch, sums = step_back(pieces[number + 1])
            totals = [a + b for a, b in zip(totals, sums)]
        finish(piece, now)
    for index, line in enumerate(totals):
        sums_ref[index : index + 1, :] = line


def branch_back(own, far, middle, grads, gain, pack, cols):
    rows, width = middle.shape
    full = whole((rows, width))
    return pl.pallas_call(
        branch_kernel,
        out_shape=(
            jax.ShapeDtypeStruct((rows, width), jnp.float32),
            jax.ShapeDtypeStruct((rows, width), jnp.bfloat16),
            jax.ShapeDtypeStruct((cols, rows), jnp.bfloat16),
            jax.ShapeDtypeStruct((cols, rows), jnp.bfloat16),
            jax.ShapeDtypeStruct((4, width), jnp.float32),
        ),
        grid=(1,),
        in_specs=[
            full, full, full, full, whole((1, width)), whole((width, cols), (0, 3)), whole((width, cols), (0, 4))
        ],
        out_specs=(full, full, whole((cols, rows)), whole((cols, rows)), whole((4, width))),
        compiler_params=kernel_params(),
        cost_estimate=cost(4 * rows * width * cols, 18 * rows * width, COSTS["branch_back"]),
        name="branch_back",
    )(own, far, middle, grads, gain, pack, pack)


def side_grad_kernel(
    so_ref, st_ref, bo_ref, bt_ref, branch_ref, co_ref, ct_ref, out_ref
):
    step = pl.program_id(0)
    last = pl.num_programs(0) - 1

    @pl.when(step < last - 1)
    def _():
        total = dot_tn(so_ref[...], bo_ref[...]) + dot_tn(st_ref[...], bt_ref[...])
        out_ref[...] = total.astype(jnp.bfloat16)

    @pl.when(step == last - 1)
    def _():
        out_ref[...] = dot_tn(branch_ref[...], co_ref[...].T).astype(jnp.bfloat16)

    @pl.when(step == last)
    def _():
        out_ref[...] = dot_tn(branch_ref[...], ct_ref[...].T).astype(jnp.bfloat16)


def side_grads(second, back, branch, contexts):
    rows, width = branch.shape
    units, cols = back[0].shape[1], contexts[0].shape[0]
    steps = units // cols
    part = pl.BlockSpec((rows, cols), lambda j: (0, jnp.minimum(j, steps - 1)))
    return pl.pallas_call(
        side_grad_kernel,
        out_shape=jax.ShapeDtypeStruct((width, units + 2 * cols), jnp.bfloat16),
        grid=(steps + 2,),
        in_specs=[whole((rows, width))] * 2 + [part] * 2
        + [whole((rows, width))] + [whole((cols, rows))] * 2,
        out_specs=pl.BlockSpec((width, cols), lambda j: (0, j)),
        compiler_params=kernel_params(),
        cost_estimate=cost(4 * rows * width * (units + cols), 4 * rows * (width + units), COSTS["weight_grad"]),
        name="side_grads",
    )(*second, *back, branch, *contexts)


def first_kernel(count, *refs):
    packs, (weight_ref, frames_ref, terms_ref, sums_ref, bias_ref, pack_ref) = refs[:count], refs[count:]
    rows, width = frames_ref.shape
    cols = pack_ref.shape[1] // 3
    q_factor = HD ** (-0.5)
    pieces = row_pieces(rows, 256)
    offset = 0
    for ref in packs:
        wide = ref.shape[1] // 3
        for part in range(3):
            place = part * cols + offset
            pack_ref[:, place : place + wide] = ref[:, part * wide : (part + 1) * wide]
        offset += wide

    def begin(piece):
        take = slice(piece[0], piece[0] + piece[1])
        return dot_nt(pack_ref[take, :cols], weight_ref[:, :cols]) * q_factor + dot_nt(
            pack_ref[take, cols:], weight_ref[:, cols:]
        )

    totals = None
    current = begin(pieces[0])
    for number, piece in enumerate(pieces):
        coming = begin(pieces[number + 1]) if number + 1 < len(pieces) else None
        take = slice(piece[0], piece[0] + piece[1])
        terms_ref[take, :] = current.astype(jnp.bfloat16)
        normed, _ = normalise(frames_ref[take, :].astype(jnp.float32))
        sums = [
            jnp.sum(current * normed, axis=0, keepdims=True),
            jnp.sum(current, axis=0, keepdims=True),
            jnp.sum(pack_ref[take, :].astype(jnp.float32), axis=0, keepdims=True),
        ]
        totals = sums if totals is None else [a + b for a, b in zip(totals, sums)]
        current = coming
    sums_ref[0:1, :] = totals[0]
    sums_ref[1:2, :] = totals[1]
    bias_ref[...] = totals[2]


def first_back(packs, weights, frames):
    rows, width = frames.shape
    wide = sum(pack.shape[1] for pack in packs)
    return pl.pallas_call(
        functools.partial(first_kernel, len(packs)),
        out_shape=(
            jax.ShapeDtypeStruct((rows, width), jnp.bfloat16),
            jax.ShapeDtypeStruct((2, width), jnp.float32),
            jax.ShapeDtypeStruct((1, wide), jnp.float32),
        ),
        grid=(1,),
        in_specs=[whole(pack.shape) for pack in packs] + [whole((width, wide)), whole((rows, width))],
        out_specs=(whole((rows, width)), whole((2, width)), whole((1, wide))),
        scratch_shapes=[pltpu.VMEM((rows, wide), jnp.bfloat16)],
        compiler_params=kernel_params(),
        cost_estimate=cost(2 * rows * width * wide, 2 * (rows + width) * wide + 4 * rows * width, COSTS["first_back"]),
        name="first_back",
    )(*packs, weights, frames)


def frames_kernel(frames_ref, own_ref, far_ref, mgrad_ref, gain_ref, out_ref):
    normed, inverse = normalise(frames_ref[...].astype(jnp.float32))
    tilted = (own_ref[...].astype(jnp.float32) + far_ref[...].astype(jnp.float32)) * gain_ref[...]
    out_ref[...] = (
        mgrad_ref[...]
        + inverse
        * (
            tilted
            - jnp.mean(tilted, axis=-1, keepdims=True)
            - normed * jnp.mean(tilted * normed, axis=-1, keepdims=True)
        )
    ).astype(jnp.bfloat16)


def frames_back(frames, own, far, mgrad, gain):
    rows, width = frames.shape
    block = 376 if rows % 376 == 0 else rows
    spec = pl.BlockSpec((block, width), lambda i: (i, 0))
    return pl.pallas_call(
        frames_kernel,
        out_shape=jax.ShapeDtypeStruct((rows, width), jnp.bfloat16),
        grid=(rows // block,),
        in_specs=[spec] * 4 + [whole((1, width))],
        out_specs=spec,
        compiler_params=kernel_params(),
        cost_estimate=cost(20 * rows * width, 12 * rows * width, COSTS["frames_back"]),
        name="frames_back",
    )(frames, own, far, mgrad, gain)


def swap_tp(piece):
    return lax.ppermute(piece, "tp", [(0, 1), (1, 0)])


def tie(*values):
    return lax.optimization_barrier(values)


def gather_steps(vector, other, fsdp):
    index = lax.axis_index("fsdp")
    side = lax.axis_index("tp")
    held = jnp.where(side == 0, jnp.stack([vector, other]), jnp.stack([other, vector]))
    bit = 1
    while bit < fsdp:
        other = lax.ppermute(held, "fsdp", [(i, i ^ bit) for i in range(fsdp)])
        low = (index & bit) == 0
        held = jnp.where(low, jnp.concatenate([held, other]), jnp.concatenate([other, held]))
        bit *= 2
    return held


def halving_order(fsdp):
    return [bit for bit in (1, 2, 8, 4, 16, 32, 64, 128) if bit < fsdp]


def halve(held, bit, left, fsdp, last=False):
    index = lax.axis_index("fsdp")
    mine = (index // bit) % 2
    parts = held if isinstance(held, list) else [held]
    outer = 2 ** sorted(left, reverse=True).index(bit)
    views = [part.reshape(outer, 2, -1, part.shape[-1]) for part in parts]

    def chosen(which):
        return jnp.concatenate(
            [lax.dynamic_index_in_dim(view, which, 1, keepdims=False) for view in views], axis=-1
        )

    other = lax.ppermute(chosen(1 - mine), "fsdp", [(i, i ^ bit) for i in range(fsdp)])
    total = chosen(mine).astype(jnp.float32) + other.astype(jnp.float32)
    return (total if last else total.astype(jnp.bfloat16)).reshape(-1, total.shape[-1])


def per_device_pair(
    frames, out_grad, clip_lengths, clip_order, w_query, w_key, w_value, b_query, b_value,
    w_out, b_out, w_expand, b_expand, w_reduce, b_reduce,
    first_gain, first_shift, second_gain, second_shift, *, fsdp,
):
    side = lax.axis_index("tp")
    slot = lax.axis_index("fsdp")
    clip_count = clip_order.shape[0]
    every_clip = jnp.arange(clip_count, dtype=jnp.int32)
    clip_id = jnp.sum(jnp.where(every_clip == slot, clip_order, 0))
    length = jnp.sum(jnp.where(every_clip == clip_id, clip_lengths, 0))
    frames, out_grad = frames[0], out_grad[0]
    rows, width = frames.shape
    cols = w_query.shape[1]
    heads = cols // HD
    units = w_expand.shape[1]
    q_factor = HD ** (-0.5)
    scal_own = jnp.stack([length, side * rows]).astype(jnp.int32)
    scal_far = jnp.stack([length, (1 - side) * rows]).astype(jnp.int32)

    wide_six = [first_gain, first_shift, second_gain, second_shift, b_out, b_reduce]
    small_own = jnp.concatenate(wide_six + [b_query, b_value, b_expand])
    out_turned = w_out.T
    small_far, out_other = swap_tp(small_own), swap_tp(out_turned)
    pack_one = lax.all_gather(
        jnp.concatenate([w_query, w_key, w_value, out_turned, out_other], axis=1),
        "fsdp", axis=0, tiled=True,
    )
    pack_two = lax.all_gather(
        jnp.concatenate([w_expand, w_reduce.T], axis=1), "fsdp", axis=0, tiled=True
    )
    sent_frames, small_far, out_other = tie(frames, small_far, out_other)
    frames_far = swap_tp(sent_frames)
    sent_grads, frames_far = tie(out_grad, frames_far)
    grads_far = swap_tp(sent_grads)
    small = gather_steps(small_own, small_far, fsdp)
    lot = first_gain.shape[0]
    whole_six = small[:, : 6 * lot].astype(jnp.float32).reshape(2 * fsdp, 6, lot)
    whole_six = whole_six.transpose(1, 0, 2).reshape(6, 1, width)
    gain_one, shift_one, gain_two, shift_two, out_bias, reduce_bias = [whole_six[i] for i in range(6)]
    mine = lax.dynamic_index_in_dim(
        small[:, 6 * lot :].astype(jnp.float32).reshape(fsdp, 2, -1), side, axis=1, keepdims=False
    )
    part = b_query.shape[0]
    bias_q = mine[:, :part].reshape(1, -1)
    bias_v = mine[:, part : 2 * part].reshape(1, -1)
    bias_e = mine[:, 2 * part :].reshape(1, -1)

    first_own, q_own, k_own, v_own = project(
        scal_own, frames, gain_one, shift_one, pack_one, bias_q, bias_v, heads
    )
    first_far, q_far, k_far, v_far = project(
        scal_far, frames_far, gain_one, shift_one, pack_one, bias_q, bias_v, heads
    )
    context_send, log_far = attend_rows(q_far, k_own, k_far, v_own, v_far)
    context_send, q_own = tie(context_send, q_own)
    context_far = swap_tp(context_send.reshape(cols, rows))
    context_own, log_own = attend_rows(q_own, k_own, k_far, v_own, v_far)
    context_own = context_own.reshape(cols, rows)
    middle, second_own = merge_heads(
        context_own, context_far, pack_one, frames, out_bias, gain_two, shift_two
    )

    second_far = swap_tp(second_own)
    hid_far, back_far, bsum_far, out_send, terms_send = feed(
        second_far, grads_far, pack_two, bias_e, units
    )
    terms_send, second_own = tie(terms_send, second_own)
    terms_far = swap_tp(terms_send)
    back_own, bsum_own, out_own, terms_own, d_reduce = feed(
        second_own, out_grad, pack_two, bias_e, units, (grads_far, hid_far)
    )
    g_reduce = lax.psum_scatter(d_reduce, "fsdp", scatter_dimension=0, tiled=True)
    mgrad, branch, up_own, up_send, sums_two = branch_back(
        terms_own, terms_far, middle, out_grad, gain_two, pack_one, cols
    )
    up_send, second_own = tie(up_send, second_own)
    up_far = swap_tp(up_send)
    d_side = side_grads(
        (second_own, second_far), (back_own, back_far), branch, (context_own, context_far)
    )

    turned = (heads, HD, rows)
    up_far, out_send, d_side = tie(up_far, out_send, d_side)
    out_far = swap_tp(out_send)
    ups = (up_own.reshape(turned), up_far.reshape(turned))
    steps = halving_order(fsdp)
    firsts = (first_own, first_far)

    def back(q_first, start, count):
        return attend_back_rows(
            (q_first, q_far), (k_own, k_far), (v_own, v_far), ups, (log_own, log_far), start, count
        )

    many = (heads + 1) // 2
    own_a, far_a = back(q_own, 0, many)
    own_a, out_far, d_side = tie(own_a, out_far, d_side)
    g_side = lax.psum_scatter(d_side, "fsdp", scatter_dimension=0, tiled=True)
    d_heads = head_grad(firsts, [own_a], [far_a])
    held_a = halve(d_heads, steps[0], steps, fsdp)
    held_a, q_own = tie(held_a, q_own)
    own_b, far_b = back(q_own, many, heads - many)
    held_a = halve(held_a, steps[1], steps[1:], fsdp)
    held_a, far_b = tie(held_a, far_b)
    first_send, sums_far, bias_far = first_back([far_a, far_b], pack_one, frames_far)
    first_send, far_b = tie(first_send, far_b)
    first_recv = swap_tp(first_send)
    held_b = head_grad(firsts, [own_b], [far_b])
    held_b, own_b = tie(held_b, own_b)
    first_keep, sums_own, bias_own = first_back([own_a, own_b], pack_one, frames)
    held_a = halve(held_a, steps[2], steps[2:], fsdp, len(steps) == 3)
    sums_one = sums_own + sums_far
    bias_sum = bias_own + bias_far
    wide_sums = jnp.concatenate([sums_one, sums_two])
    wide_sums = wide_sums.reshape(6, fsdp, 2, lot).transpose(1, 2, 0, 3).reshape(fsdp, 12 * lot)
    tall = jnp.concatenate(
        [
            wide_sums,
            (bias_sum[:, :cols] * q_factor).reshape(fsdp, -1),
            bias_sum[:, 2 * cols :].reshape(fsdp, -1),
            (bsum_own + bsum_far).reshape(fsdp, -1),
        ],
        axis=1,
    )
    wide = held_b.shape[1]
    extra = -(-tall.shape[1] // (8 * wide)) * 8
    tall = jnp.pad(tall, ((0, 0), (0, extra * wide - tall.shape[1]))).astype(jnp.bfloat16)
    lots = width // fsdp
    held_b = jnp.concatenate(
        [held_b.reshape(fsdp, lots, wide), tall.reshape(fsdp, extra, wide)], axis=1
    ).reshape(-1, wide)
    held_b = halve(held_b, steps[0], steps, fsdp)
    held_b = halve(held_b, steps[1], steps[1:], fsdp)
    out_frames = (
        middle + out_own.astype(jnp.float32) + out_far.astype(jnp.float32) + reduce_bias
    ).astype(jnp.bfloat16)
    for place in range(2, len(steps)):
        last = place + 1 == len(steps)
        if place > 2:
            held_a = halve(held_a, steps[place], steps[place:], fsdp, last)
        if last:
            held_a, held_b, first_keep, out_frames = tie(held_a, held_b, first_keep, out_frames)
            frames_grad = frames_back(frames, first_keep, first_recv, mgrad, gain_one)
            held_b, frames_grad, g_side = tie(held_b, frames_grad, g_side)
        held_b = halve(held_b, steps[place], steps[place:], fsdp, last)
    held_b, small_sum = held_b[:lots], held_b[lots:].reshape(-1)
    g_expand, g_out = g_side[:, :units], g_side[:, units:]
    some = many * HD

    def joined(kind):
        rest = cols - some
        return jnp.concatenate(
            [held_a[:, kind * some : (kind + 1) * some], held_b[:, kind * rest : (kind + 1) * rest]], axis=1
        )

    g_query, g_key, g_value = joined(0), joined(1), joined(2)

    six = small_sum[: 12 * lot].reshape(2, 6 * lot)
    keep = lax.dynamic_index_in_dim(six, side, 0, keepdims=False)
    send = lax.dynamic_index_in_dim(six, 1 - side, 0, keepdims=False)
    six = (keep + swap_tp(send)).reshape(6, lot)
    rest = small_sum[12 * lot :]
    g_bq, g_bv = rest[:part], rest[part : 2 * part]
    g_be = rest[2 * part : 2 * part + b_expand.shape[0]]
    g_out_sum = g_out[:, :cols].astype(jnp.float32) + swap_tp(g_out[:, cols:]).astype(jnp.float32)
    return (
        out_frames[None],
        frames_grad[None],
        g_query,
        g_key,
        g_value,
        g_bq,
        g_bv,
        g_out_sum.T,
        six[4],
        g_expand.astype(jnp.float32),
        g_be,
        g_reduce.T.astype(jnp.float32),
        six[5],
        six[0],
        six[1],
        six[2],
        six[3],
    )


def solution(mesh):
    fsdp = mesh.shape["fsdp"]
    if mesh.shape["tp"] == 2 and fsdp & (fsdp - 1) == 0:

        def body(*args):
            return per_device_pair(*args, fsdp=fsdp) if args[0].shape[0] == 1 else per_device(*args)
    else:
        body = per_device
    return jax.shard_map(
        body,
        mesh=mesh,
        in_specs=(
            P("fsdp", "tp", None),
            P("fsdp", "tp", None),
            P(),
            P(),
            P("fsdp", "tp"),
            P("fsdp", "tp"),
            P("fsdp", "tp"),
            P(("tp", "fsdp")),
            P(("tp", "fsdp")),
            P("tp", "fsdp"),
            P(("fsdp", "tp")),
            P("fsdp", "tp"),
            P(("tp", "fsdp")),
            P("tp", "fsdp"),
            P(("fsdp", "tp")),
            P(("fsdp", "tp")),
            P(("fsdp", "tp")),
            P(("fsdp", "tp")),
            P(("fsdp", "tp")),
        ),
        out_specs=(
            P("fsdp", "tp", None),
            P("fsdp", "tp", None),
            P("fsdp", "tp"),
            P("fsdp", "tp"),
            P("fsdp", "tp"),
            P(("tp", "fsdp")),
            P(("tp", "fsdp")),
            P("tp", "fsdp"),
            P(("fsdp", "tp")),
            P("fsdp", "tp"),
            P(("tp", "fsdp")),
            P("tp", "fsdp"),
            P(("fsdp", "tp")),
            P(("fsdp", "tp")),
            P(("fsdp", "tp")),
            P(("fsdp", "tp")),
            P(("fsdp", "tp")),
        ),
        check_vma=False,
    )
```

```python
import functools

import jax
import jax.numpy as jnp
from jax import lax
from jax.experimental import pallas as pl
from jax.experimental.pallas import tpu as pltpu
from jax.sharding import PartitionSpec as P

HD = 80


EPSILON = 1e-05
MASKED = -1000000000.0
HIDDEN = -1e30


def layer_norm(features, norm_gain, norm_shift):
    row_mean = jnp.mean(features, axis=-1, keepdims=True)
    centred = features - row_mean
    row_var = jnp.mean(centred * centred, axis=-1, keepdims=True)
    inverse = lax.rsqrt(row_var + EPSILON)
    normed = centred * inverse
    return (normed * norm_gain + norm_shift, normed, inverse)


def norm_back(upstream, normed, inverse, norm_gain):
    tilted = upstream * norm_gain
    return inverse * (
        tilted
        - jnp.mean(tilted, axis=-1, keepdims=True)
        - normed * jnp.mean(tilted * normed, axis=-1, keepdims=True)
    )


def gelu_exact(inputs):
    return jax.nn.gelu(inputs, approximate=False)


def masked_scores(queries, key_rows, length):
    scores = jnp.einsum("qhe,khe->hqk", queries, key_rows, preferred_element_type=jnp.float32)
    allowed = jnp.arange(scores.shape[-1]) < length
    return jnp.where(allowed[None, None, :], scores, MASKED)


def attend(inputs):
    queries, key_rows, value_rows, length = inputs
    scores = masked_scores(queries, key_rows, length)
    row_top = jnp.max(scores, axis=-1, keepdims=True)
    raised = jnp.exp(scores - row_top)
    row_sum = jnp.sum(raised, axis=-1, keepdims=True)
    weights = (raised / row_sum).astype(jnp.bfloat16)
    context = jnp.einsum("hqk,khe->qhe", weights, value_rows, preferred_element_type=jnp.float32)
    return (context.astype(jnp.bfloat16), row_top[..., 0] + jnp.log(row_sum[..., 0]))


def attend_back(inputs):
    queries, key_rows, value_rows, length, log_total, context_grad = inputs
    scores = masked_scores(queries, key_rows, length)
    probs = jnp.exp(scores - log_total[..., None])
    weights = probs.astype(jnp.bfloat16)
    value_grad = jnp.einsum(
        "hqk,qhe->khe", weights, context_grad, preferred_element_type=jnp.float32
    )
    weight_grad = jnp.einsum(
        "qhe,khe->hqk", context_grad, value_rows, preferred_element_type=jnp.float32
    )
    row_inner = jnp.sum(weight_grad * probs, axis=-1, keepdims=True)
    score_grad = (probs * (weight_grad - row_inner)).astype(jnp.bfloat16)
    query_grad = jnp.einsum(
        "hqk,khe->qhe", score_grad, key_rows, preferred_element_type=jnp.float32
    )
    key_grad = jnp.einsum("hqk,qhe->khe", score_grad, queries, preferred_element_type=jnp.float32)
    return (
        query_grad.astype(jnp.bfloat16),
        key_grad.astype(jnp.bfloat16),
        value_grad.astype(jnp.bfloat16),
    )


def gather_inward(w_query, w_key, w_value, b_query, b_value, w_expand, b_expand):
    return (
        lax.all_gather(w_query, "fsdp", axis=0, tiled=True),
        lax.all_gather(w_key, "fsdp", axis=0, tiled=True),
        lax.all_gather(w_value, "fsdp", axis=0, tiled=True),
        lax.all_gather(b_query, "fsdp", axis=0, tiled=True),
        lax.all_gather(b_value, "fsdp", axis=0, tiled=True),
        lax.all_gather(w_expand, "fsdp", axis=0, tiled=True),
        lax.all_gather(b_expand, "fsdp", axis=0, tiled=True),
    )


def gather_outward(w_out, w_reduce):
    return (
        lax.all_gather(w_out, "fsdp", axis=1, tiled=True),
        lax.all_gather(w_reduce, "fsdp", axis=1, tiled=True),
    )


def per_device(
    frames,
    out_grad,
    clip_lengths,
    clip_order,
    w_query,
    w_key,
    w_value,
    b_query,
    b_value,
    w_out,
    b_out,
    w_expand,
    b_expand,
    w_reduce,
    b_reduce,
    first_gain,
    first_shift,
    second_gain,
    second_shift,
):
    per_group = frames.shape[0]
    clip_count = clip_order.shape[0]
    slot_ids = lax.axis_index("fsdp") * per_group + jnp.arange(per_group, dtype=jnp.int32)
    every_clip = jnp.arange(clip_count, dtype=jnp.int32)
    clip_ids = jnp.sum(
        jnp.where(every_clip[None, :] == slot_ids[:, None], clip_order[None, :], 0), axis=1
    )
    lengths = jnp.sum(
        jnp.where(every_clip[None, :] == clip_ids[:, None], clip_lengths[None, :], 0), axis=1
    )
    norm_params = (
        lax.all_gather(first_gain, ("fsdp", "tp"), axis=0, tiled=True),
        lax.all_gather(first_shift, ("fsdp", "tp"), axis=0, tiled=True),
        lax.all_gather(second_gain, ("fsdp", "tp"), axis=0, tiled=True),
        lax.all_gather(second_shift, ("fsdp", "tp"), axis=0, tiled=True),
        lax.all_gather(b_out, ("fsdp", "tp"), axis=0, tiled=True),
        lax.all_gather(b_reduce, ("fsdp", "tp"), axis=0, tiled=True),
    )
    gain_one, shift_one, gain_two, shift_two, out_bias, reduce_bias = [
        tensor.astype(jnp.float32) for tensor in norm_params
    ]
    wq_all, wk_all, wv_all, bq_all, bv_all, we_all, be_all = gather_inward(
        w_query, w_key, w_value, b_query, b_value, w_expand, b_expand
    )
    wo_all, wr_all = gather_outward(w_out, w_reduce)
    q_factor = HD ** (-0.5)
    frames_wide = frames.astype(jnp.float32)
    norm_one, normed_one, inverse_one = layer_norm(frames_wide, gain_one, shift_one)
    first_rows = lax.all_gather(norm_one.astype(jnp.bfloat16), "tp", axis=1, tiled=True)
    seq_len = first_rows.shape[1]
    queries = (
        (
            jnp.einsum("csd,de->cse", first_rows, wq_all, preferred_element_type=jnp.float32)
            + bq_all.astype(jnp.float32)
        )
        * q_factor
    ).astype(jnp.bfloat16)
    keys = jnp.einsum("csd,de->cse", first_rows, wk_all, preferred_element_type=jnp.float32).astype(
        jnp.bfloat16
    )
    values = (
        jnp.einsum("csd,de->cse", first_rows, wv_all, preferred_element_type=jnp.float32)
        + bv_all.astype(jnp.float32)
    ).astype(jnp.bfloat16)
    head_shape = (per_group, seq_len, -1, HD)
    query_heads = queries.reshape(head_shape)
    key_heads = keys.reshape(head_shape)
    value_heads = values.reshape(head_shape)
    context, log_total = lax.map(attend, (query_heads, key_heads, value_heads, lengths))
    context_flat = context.reshape(per_group, seq_len, -1)
    attn_terms = jnp.einsum("cse,ed->csd", context_flat, wo_all, preferred_element_type=jnp.float32)
    attn_part = lax.psum_scatter(
        attn_terms.astype(jnp.bfloat16), "tp", scatter_dimension=1, tiled=True
    ).astype(jnp.float32)
    middle = frames_wide + attn_part + out_bias
    norm_two, normed_two, inverse_two = layer_norm(middle, gain_two, shift_two)
    second_rows = lax.all_gather(norm_two.astype(jnp.bfloat16), "tp", axis=1, tiled=True)
    expanded = jnp.einsum(
        "csd,df->csf", second_rows, we_all, preferred_element_type=jnp.float32
    ) + be_all.astype(jnp.float32)
    activated, gelu_pull = jax.vjp(gelu_exact, expanded)
    hidden = activated.astype(jnp.bfloat16)
    mlp_terms = jnp.einsum("csf,fd->csd", hidden, wr_all, preferred_element_type=jnp.float32)
    out_frames = (
        middle
        + lax.psum_scatter(
            mlp_terms.astype(jnp.bfloat16), "tp", scatter_dimension=1, tiled=True
        ).astype(jnp.float32)
        + reduce_bias
    ).astype(jnp.bfloat16)
    wq_all, wk_all, wv_all, bq_all, bv_all, we_all, be_all = gather_inward(
        w_query, w_key, w_value, b_query, b_value, w_expand, b_expand
    )
    wo_all, wr_all = gather_outward(w_out, w_reduce)
    grad_wide = out_grad.astype(jnp.float32)
    grad_rows = lax.all_gather(out_grad, "tp", axis=1, tiled=True)
    w_reduce_grad = jnp.einsum("csf,csd->fd", hidden, grad_rows, preferred_element_type=jnp.float32)
    hidden_grad = jnp.einsum("csd,fd->csf", grad_rows, wr_all, preferred_element_type=jnp.float32)
    expanded_grad = gelu_pull(hidden_grad)[0].astype(jnp.bfloat16)
    b_expand_grad = jnp.sum(expanded_grad.astype(jnp.float32), axis=(0, 1))
    w_expand_grad = jnp.einsum(
        "csd,csf->df", second_rows, expanded_grad, preferred_element_type=jnp.float32
    )
    second_terms = jnp.einsum(
        "csf,df->csd", expanded_grad, we_all, preferred_element_type=jnp.float32
    )
    second_grad = lax.psum_scatter(
        second_terms.astype(jnp.bfloat16), "tp", scatter_dimension=1, tiled=True
    ).astype(jnp.float32)
    second_gain_grad = jnp.sum(second_grad * normed_two, axis=(0, 1))
    second_shift_grad = jnp.sum(second_grad, axis=(0, 1))
    middle_grad = grad_wide + norm_back(second_grad, normed_two, inverse_two, gain_two)
    branch_grad = middle_grad.astype(jnp.bfloat16)
    b_out_grad = jnp.sum(branch_grad.astype(jnp.float32), axis=(0, 1))
    b_reduce_grad = jnp.sum(grad_wide, axis=(0, 1))
    branch_rows = lax.all_gather(branch_grad, "tp", axis=1, tiled=True)
    w_out_grad = jnp.einsum(
        "cse,csd->ed", context_flat, branch_rows, preferred_element_type=jnp.float32
    )
    context_grad = jnp.einsum(
        "csd,ed->cse", branch_rows, wo_all, preferred_element_type=jnp.float32
    ).astype(jnp.bfloat16)
    query_grad, key_grad, value_grad = lax.map(
        attend_back,
        (query_heads, key_heads, value_heads, lengths, log_total, context_grad.reshape(head_shape)),
    )
    query_grad = query_grad.reshape(per_group, seq_len, -1)
    key_grad = key_grad.reshape(per_group, seq_len, -1)
    value_grad = value_grad.reshape(per_group, seq_len, -1)
    w_query_grad = (
        jnp.einsum("csd,cse->de", first_rows, query_grad, preferred_element_type=jnp.float32)
        * q_factor
    )
    b_query_grad = jnp.sum(query_grad.astype(jnp.float32), axis=(0, 1)) * q_factor
    w_key_grad = jnp.einsum("csd,cse->de", first_rows, key_grad, preferred_element_type=jnp.float32)
    w_value_grad = jnp.einsum(
        "csd,cse->de", first_rows, value_grad, preferred_element_type=jnp.float32
    )
    b_value_grad = jnp.sum(value_grad.astype(jnp.float32), axis=(0, 1))
    first_terms = (
        jnp.einsum("cse,de->csd", query_grad, wq_all, preferred_element_type=jnp.float32) * q_factor
        + jnp.einsum("cse,de->csd", key_grad, wk_all, preferred_element_type=jnp.float32)
        + jnp.einsum("cse,de->csd", value_grad, wv_all, preferred_element_type=jnp.float32)
    )
    first_grad = lax.psum_scatter(
        first_terms.astype(jnp.bfloat16), "tp", scatter_dimension=1, tiled=True
    ).astype(jnp.float32)
    first_gain_grad = jnp.sum(first_grad * normed_one, axis=(0, 1))
    first_shift_grad = jnp.sum(first_grad, axis=(0, 1))
    frames_grad = (middle_grad + norm_back(first_grad, normed_one, inverse_one, gain_one)).astype(
        jnp.bfloat16
    )
    inward_grads = (
        lax.psum_scatter(
            w_query_grad.astype(jnp.bfloat16), "fsdp", scatter_dimension=0, tiled=True
        ).astype(jnp.float32),
        lax.psum_scatter(
            w_key_grad.astype(jnp.bfloat16), "fsdp", scatter_dimension=0, tiled=True
        ).astype(jnp.float32),
        lax.psum_scatter(
            w_value_grad.astype(jnp.bfloat16), "fsdp", scatter_dimension=0, tiled=True
        ).astype(jnp.float32),
        lax.psum_scatter(
            b_query_grad.astype(jnp.bfloat16), "fsdp", scatter_dimension=0, tiled=True
        ).astype(jnp.float32),
        lax.psum_scatter(
            b_value_grad.astype(jnp.bfloat16), "fsdp", scatter_dimension=0, tiled=True
        ).astype(jnp.float32),
        lax.psum_scatter(
            w_expand_grad.astype(jnp.bfloat16), "fsdp", scatter_dimension=0, tiled=True
        ).astype(jnp.float32),
        lax.psum_scatter(
            b_expand_grad.astype(jnp.bfloat16), "fsdp", scatter_dimension=0, tiled=True
        ).astype(jnp.float32),
    )
    outward_grads = (
        lax.psum_scatter(
            w_out_grad.astype(jnp.bfloat16), "fsdp", scatter_dimension=1, tiled=True
        ).astype(jnp.float32),
        lax.psum_scatter(
            w_reduce_grad.astype(jnp.bfloat16), "fsdp", scatter_dimension=1, tiled=True
        ).astype(jnp.float32),
    )
    small_grads = (
        lax.psum_scatter(first_gain_grad, ("fsdp", "tp"), scatter_dimension=0, tiled=True),
        lax.psum_scatter(first_shift_grad, ("fsdp", "tp"), scatter_dimension=0, tiled=True),
        lax.psum_scatter(second_gain_grad, ("fsdp", "tp"), scatter_dimension=0, tiled=True),
        lax.psum_scatter(second_shift_grad, ("fsdp", "tp"), scatter_dimension=0, tiled=True),
        lax.psum_scatter(b_out_grad, ("fsdp", "tp"), scatter_dimension=0, tiled=True),
        lax.psum_scatter(b_reduce_grad, ("fsdp", "tp"), scatter_dimension=0, tiled=True),
    )
    return (
        out_frames,
        frames_grad,
        inward_grads[0],
        inward_grads[1],
        inward_grads[2],
        inward_grads[3],
        inward_grads[4],
        outward_grads[0],
        small_grads[4],
        inward_grads[5],
        inward_grads[6],
        outward_grads[1],
        small_grads[5],
        small_grads[0],
        small_grads[1],
        small_grads[2],
        small_grads[3],
    )


VMEM_LIMIT = 60 << 20
PAD = 128
COSTS = {'project': 3.0, 'attend': 3.0, 'merge_heads': 3.0, 'feed': 3.0, 'weight_grad': 3.0, 'head_grad': 0.02, 'branch_back': 3.0, 'out_weight_grad': 0.02, 'first_back': 0.02, 'frames_back': 0.02, 'attend_back': (8.0, 0.02)}


def kernel_params():
    return pltpu.CompilerParams(vmem_limit_bytes=VMEM_LIMIT)


def cost(flops, moved, scale):
    return pl.CostEstimate(flops=int(scale * flops), bytes_accessed=int(min(1.0, scale) * moved), transcendentals=0)


def lanes(rows):
    return -(-rows // PAD) * PAD


def row_pieces(rows, size):
    return [(start, min(size, rows - start)) for start in range(0, rows, size)]


def whole(shape, fixed=None):
    index = fixed if fixed is not None else (0,) * len(shape)
    return pl.BlockSpec(shape, lambda *_: index)


def normalise(rows):
    row_mean = jnp.mean(rows, axis=-1, keepdims=True)
    centred = rows - row_mean
    inverse = lax.rsqrt(jnp.mean(centred * centred, axis=-1, keepdims=True) + EPSILON)
    return centred * inverse, inverse


def dot_nn(left, right):
    return jnp.dot(left, right, preferred_element_type=jnp.float32)


def dot_nt(left, right):
    return lax.dot_general(left, right, (((1,), (1,)), ((), ())), preferred_element_type=jnp.float32)


def dot_tn(left, right):
    return lax.dot_general(left, right, (((0,), (0,)), ((), ())), preferred_element_type=jnp.float32)


def project_kernel(
    heads, scal_ref, frames_ref, gain_ref, shift_ref, weight_ref, bq_ref, bv_ref,
    first_ref, q_ref, k_ref, v_ref,
):
    rows, width = frames_ref.shape
    cols = heads * HD
    length, start = scal_ref[0], scal_ref[1]
    q_factor = HD ** (-0.5)
    pieces = row_pieces(rows, 256)

    def norm(piece):
        normed, _ = normalise(frames_ref[piece[0] : piece[0] + piece[1], :].astype(jnp.float32))
        first = (normed * gain_ref[...] + shift_ref[...]).astype(jnp.bfloat16)
        first_ref[piece[0] : piece[0] + piece[1], :] = first
        return first

    def split(block, offset, filler, lane):
        if offset + PAD <= block.shape[1]:
            part = block[:, offset : offset + PAD]
        else:
            back = block.shape[1] - PAD
            part = pltpu.roll(block[:, back:], PAD - (offset - back), 1)
        return jnp.where(lane < HD, part, filler).astype(jnp.bfloat16)

    def finish(piece, out):
        lane = lax.broadcasted_iota(jnp.int32, (piece[1], PAD), 1)
        position = lax.broadcasted_iota(jnp.int32, (piece[1], PAD), 0) + (start + piece[0])
        one = jnp.where(lane == HD, 1.0, 0.0)
        hide = jnp.where((lane == HD) & (position >= length), HIDDEN, 0.0)
        queries = (out[:, :cols] + bq_ref[...]) * q_factor
        keys = out[:, cols : 2 * cols]
        values = out[:, 2 * cols :] + bv_ref[...]
        for head in range(heads):
            where = (head, slice(piece[0], piece[0] + piece[1]), slice(None))
            q_ref[where] = split(queries, head * HD, one, lane)
            k_ref[where] = split(keys, head * HD, hide, lane)
            v_ref[where] = split(values, head * HD, 0.0, lane)

    first = norm(pieces[0])
    for number, piece in enumerate(pieces):
        out = dot_nn(first, weight_ref[...])
        if number + 1 < len(pieces):
            first = norm(pieces[number + 1])
        finish(piece, out)


def project(scalars, frames, gain, shift, weights, bias_q, bias_v, heads):
    rows, width = frames.shape
    cols = heads * HD
    head_out = jax.ShapeDtypeStruct((heads, rows, PAD), jnp.bfloat16)
    return pl.pallas_call(
        functools.partial(project_kernel, heads),
        out_shape=(jax.ShapeDtypeStruct((rows, width), jnp.bfloat16), head_out, head_out, head_out),
        grid_spec=pltpu.PrefetchScalarGridSpec(
            num_scalar_prefetch=1,
            grid=(1,),
            in_specs=[
                whole((rows, width)), whole((1, width)), whole((1, width)),
                whole((width, 3 * cols)), whole((1, cols)), whole((1, cols)),
            ],
            out_specs=(whole((rows, width)),) + (whole((heads, rows, PAD)),) * 3,
        ),
        compiler_params=kernel_params(),
        cost_estimate=cost(2 * rows * width * 3 * cols, 4 * rows * width + 6 * width * cols, COSTS["project"]),
        name="project",
    )(scalars, frames, gain, shift, weights, bias_q, bias_v)


def attend_kernel(q_ref, ko_ref, kt_ref, vo_ref, vt_ref, out_ref, log_ref):
    per_step, rows, _ = q_ref.shape
    half = -(-rows // 256) * 128
    pieces = [(head, start, size) for head in range(per_step) for start, size in row_pieces(rows, half)]
    keys = [jnp.concatenate([ko_ref[h], kt_ref[h]], axis=0) for h in range(per_step)]
    values = [jnp.concatenate([vo_ref[h], vt_ref[h]], axis=0).T[:HD] for h in range(per_step)]

    def scores(piece):
        head, start, size = piece
        return dot_nt(keys[head], q_ref[head, start : start + size, :])

    def finish(piece, score):
        head, start, size = piece
        top = jnp.max(score, axis=0, keepdims=True)
        raised = jnp.exp(score - top)
        total = jnp.sum(raised, axis=0, keepdims=True)
        context = dot_nn(values[head], raised.astype(jnp.bfloat16)) / total
        out_ref[head, :, start : start + size] = context.astype(jnp.bfloat16)
        log_ref[head, :, start : start + size] = top + jnp.log(total)

    if out_ref.shape[2] > rows:
        out_ref[:, :, rows:] = jnp.zeros((per_step, HD, out_ref.shape[2] - rows), jnp.bfloat16)
    current = scores(pieces[0])
    for number, piece in enumerate(pieces):
        coming = scores(pieces[number + 1]) if number + 1 < len(pieces) else None
        finish(piece, current)
        current = coming


def attend_rows(queries, keys_own, keys_far, values_own, values_far):
    heads, rows, _ = queries.shape
    per_step = 2 if heads % 2 == 0 else 1
    spec = pl.BlockSpec((per_step, rows, PAD), lambda h: (h, 0, 0))
    return pl.pallas_call(
        attend_kernel,
        out_shape=(
            jax.ShapeDtypeStruct((heads, HD, lanes(rows)), jnp.bfloat16),
            jax.ShapeDtypeStruct((heads, 1, rows), jnp.float32),
        ),
        grid=(heads // per_step,),
        in_specs=[spec] * 5,
        out_specs=(
            pl.BlockSpec((per_step, HD, lanes(rows)), lambda h: (h, 0, 0)),
            pl.BlockSpec((per_step, 1, rows), lambda h: (h, 0, 0)),
        ),
        compiler_params=kernel_params(),
        cost_estimate=cost(heads * 2 * rows * 2 * rows * 2 * 400, heads * rows * PAD * 12, COSTS["attend"]),
        name="attend",
    )(queries, keys_own, keys_far, values_own, values_far)


def attend_back_kernel(
    qo_ref, qt_ref, ko_ref, kt_ref, vo_ref, vt_ref, go_ref, gt_ref, lo_ref, lt_ref,
    own_ref, far_ref, dq_ref,
):
    rows = qo_ref.shape[1]
    cols = own_ref.shape[1] // 3
    keys = jnp.concatenate([ko_ref[0], kt_ref[0]], axis=0)
    values = jnp.concatenate([vo_ref[0], vt_ref[0]], axis=0)
    keys_turned = keys.T[:HD]
    pieces = [(side, start, size) for side in range(2) for start, size in row_pieces(rows, 256)]
    sides = ((qo_ref, go_ref, lo_ref), (qt_ref, gt_ref, lt_ref))

    def query(piece):
        side, start, size = piece
        return sides[side][0][0, start : start + size, :]

    def upstream(piece):
        side, start, size = piece
        return sides[side][1][0, :, start : start + size]

    def begin(piece):
        score = dot_nt(keys, query(piece))
        padded = jnp.concatenate(
            [upstream(piece), jnp.zeros((PAD - HD, piece[2]), jnp.bfloat16)], axis=0
        )
        return score, dot_nn(values, padded)

    def middle(piece, score, weight_grad):
        side, start, size = piece
        probs = jnp.exp(score - sides[side][2][0, :, start : start + size])
        tilted = probs * weight_grad
        inner = jnp.sum(tilted, axis=0, keepdims=True)
        return probs.astype(jnp.bfloat16), (tilted - probs * inner).astype(jnp.bfloat16)

    total_k = total_v = None
    current = begin(pieces[0])
    for number, piece in enumerate(pieces):
        coming = begin(pieces[number + 1]) if number + 1 < len(pieces) else None
        weights, score_grad = middle(piece, *current)
        value_part = dot_nt(weights, upstream(piece))
        key_part = dot_nn(score_grad, query(piece))
        query_grad = dot_nn(keys_turned, score_grad)
        side, start, size = piece
        dq_ref[side * rows + start : side * rows + start + size, :] = query_grad.T.astype(jnp.bfloat16)
        total_v = value_part if total_v is None else total_v + value_part
        total_k = key_part if total_k is None else total_k + key_part
        current = coming
    key_grad = total_k[:, :HD].astype(jnp.bfloat16)
    value_grad = total_v.astype(jnp.bfloat16)
    for head in range(cols // HD):

        @pl.when(pl.program_id(0) == head)
        def _(head=head):
            for part, grad in enumerate((dq_ref[...], key_grad, value_grad)):
                take = slice(part * cols + head * HD, part * cols + (head + 1) * HD)
                own_ref[:, take] = grad[:rows]
                far_ref[:, take] = grad[rows:]


def attend_back_rows(queries, keys, values, upstream, logs, start, heads):
    rows = queries[0].shape[1]
    spec = pl.BlockSpec((1, rows, PAD), lambda h: (h + start, 0, 0))
    turned = pl.BlockSpec((1, HD, lanes(rows)), lambda h: (h + start, 0, 0))
    line = pl.BlockSpec((1, 1, rows), lambda h: (h + start, 0, 0))
    packed = (rows, 3 * heads * HD)
    return pl.pallas_call(
        attend_back_kernel,
        out_shape=(jax.ShapeDtypeStruct(packed, jnp.bfloat16),) * 2,
        grid=(heads,),
        in_specs=[spec] * 6 + [turned] * 2 + [line] * 2,
        out_specs=(whole(packed),) * 2,
        scratch_shapes=[pltpu.VMEM((2 * rows, HD), jnp.bfloat16)],
        compiler_params=kernel_params(),
        cost_estimate=cost(heads * 4 * rows * rows * 2 * 900, heads * rows * PAD * 24, COSTS["attend_back"][start > 0]),
        name="attend_back",
    )(*queries, *keys, *values, *upstream, *logs)


def merge_kernel(
    co_ref, ct_ref, wo_ref, wt_ref, frames_ref, bias_ref, gain_ref, shift_ref, middle_ref, second_ref,
):
    rows = frames_ref.shape[0]
    own, far = co_ref[:, :rows].T, ct_ref[:, :rows].T
    pieces = row_pieces(rows, 256)

    def branch(piece):
        take = slice(piece[0], piece[0] + piece[1])
        return dot_nt(own[take], wo_ref[...]) + dot_nt(far[take], wt_ref[...])

    def finish(piece, part):
        take = slice(piece[0], piece[0] + piece[1])
        middle = frames_ref[take, :].astype(jnp.float32) + part + bias_ref[...]
        middle_ref[take, :] = middle
        normed, _ = normalise(middle)
        second_ref[take, :] = (normed * gain_ref[...] + shift_ref[...]).astype(jnp.bfloat16)

    current = branch(pieces[0])
    for number, piece in enumerate(pieces):
        coming = branch(pieces[number + 1]) if number + 1 < len(pieces) else None
        finish(piece, current)
        current = coming


def merge_heads(context_own, context_far, pack, frames, bias, gain, shift):
    rows, width = frames.shape
    cols = context_own.shape[0]
    return pl.pallas_call(
        merge_kernel,
        out_shape=(
            jax.ShapeDtypeStruct((rows, width), jnp.float32),
            jax.ShapeDtypeStruct((rows, width), jnp.bfloat16),
        ),
        grid=(1,),
        in_specs=[
            whole((cols, lanes(rows))), whole((cols, lanes(rows))), whole((width, cols), (0, 3)),
            whole((width, cols), (0, 4)), whole((rows, width)), whole((1, width)), whole((1, width)), whole((1, width)),
        ],
        out_specs=(whole((rows, width)),) * 2,
        compiler_params=kernel_params(),
        cost_estimate=cost(4 * rows * width * cols, 10 * rows * width + 4 * width * cols, COSTS["merge_heads"]),
        name="merge_heads",
    )(context_own, context_far, pack, pack, frames, bias, gain, shift)


def feed_kernel(
    grads_too, second_ref, grad_ref, expand_ref, reduce_ref, bias_ref, *refs,
):
    if grads_too:
        far_ref, hid_ref, back_ref, bsum_ref, out_ref, terms_ref, dred_ref, out_acc, terms_acc, hidden_ref = refs
    else:
        hidden_ref, back_ref, bsum_ref, out_ref, terms_ref, out_acc, terms_acc = refs
    step = pl.program_id(0)
    rows = second_ref.shape[0]
    pieces = row_pieces(rows, 376 if rows % 376 == 0 else 256)
    expand, reduce = expand_ref[...], reduce_ref[...]

    def begin(piece):
        take = slice(piece[0], piece[0] + piece[1])
        return dot_nn(second_ref[take, :], expand), dot_nn(grad_ref[take, :], reduce)

    @pl.when(step == 0)
    def _():
        out_acc[...] = jnp.zeros_like(out_acc)
        terms_acc[...] = jnp.zeros_like(terms_acc)

    sums = None
    current = begin(pieces[0])
    for number, piece in enumerate(pieces):
        coming = begin(pieces[number + 1]) if number + 1 < len(pieces) else None
        take = slice(piece[0], piece[0] + piece[1])
        raw, upstream = current
        raw = raw + bias_ref[...]
        below = 0.5 + 0.5 * lax.erf(raw * 0.7071067811865476)
        density = jnp.exp(raw * raw * -0.5) * 0.3989422804014327
        hidden = (raw * below).astype(jnp.bfloat16)
        back = (upstream * (below + raw * density)).astype(jnp.bfloat16)
        hidden_ref[take, :] = hidden
        back_ref[take, :] = back
        part = jnp.sum(back.astype(jnp.float32), axis=0, keepdims=True)
        sums = part if sums is None else sums + part
        terms_acc[take, :] += dot_nt(back, expand)
        out_acc[take, :] += dot_nt(hidden, reduce)
        current = coming
    bsum_ref[...] = sums
    if grads_too:
        total = dot_tn(far_ref[...], hid_ref[...]) + dot_tn(grad_ref[...], hidden_ref[...])
        dred_ref[...] = total.astype(jnp.bfloat16)

    @pl.when(step == pl.num_programs(0) - 1)
    def _():
        out_ref[...] = out_acc[...].astype(jnp.bfloat16)
        terms_ref[...] = terms_acc[...].astype(jnp.bfloat16)


def feed(second, grads, pack, bias, units, far=None):
    rows, width = second.shape
    block = 512 if units % 512 == 0 else units
    steps = units // block
    wide = pl.BlockSpec((rows, block), lambda j: (0, j))
    weights = [
        pl.BlockSpec((width, block), lambda j: (0, j)),
        pl.BlockSpec((width, block), lambda j: (0, j + steps)),
    ]
    line = pl.BlockSpec((1, block), lambda j: (0, j))
    hidden = jax.ShapeDtypeStruct((rows, units), jnp.bfloat16)
    full = jax.ShapeDtypeStruct((rows, width), jnp.bfloat16)
    outs = [hidden, jax.ShapeDtypeStruct((1, units), jnp.float32), full, full]
    out_specs = [wide, line, whole((rows, width)), whole((rows, width))]
    scratch = [pltpu.VMEM((rows, width), jnp.float32)] * 2
    in_specs = [whole((rows, width)), whole((rows, width)), *weights, line]
    if far is None:
        outs, out_specs = [hidden] + outs, [wide] + out_specs
    else:
        outs = outs + [jax.ShapeDtypeStruct((width, units), jnp.bfloat16)]
        out_specs = out_specs + [weights[0]]
        in_specs = in_specs + [whole((rows, width)), wide]
        scratch = scratch + [pltpu.VMEM((rows, block), jnp.bfloat16)]
    flops = (8 if far is None else 12) * rows * width * units
    return pl.pallas_call(
        functools.partial(feed_kernel, far is not None),
        out_shape=tuple(outs),
        grid=(steps,),
        in_specs=in_specs,
        out_specs=tuple(out_specs),
        scratch_shapes=scratch,
        compiler_params=kernel_params(),
        cost_estimate=cost(flops, 8 * rows * (units + width) + 4 * width * units, COSTS["feed"]),
        name="feed" if far is None else "feed_last",
    )(second, grads, pack, pack, bias, *(far or ()))


def head_grad_kernel(count, lo_ref, lt_ref, *refs):
    out_ref = refs[2 * count]
    offset = 0
    for own_ref, far_ref in zip(refs[:count], refs[count : 2 * count]):
        wide = own_ref.shape[1]
        total = dot_tn(lo_ref[...], own_ref[...]) + dot_tn(lt_ref[...], far_ref[...])
        lane = lax.broadcasted_iota(jnp.int32, (1, wide), 1)
        total = total * jnp.where(lane < wide // 3, HD ** (-0.5), 1.0)
        out_ref[:, offset : offset + wide] = total.astype(jnp.bfloat16)
        offset += wide


def head_grad(lefts, own, far):
    rows, width = lefts[0].shape
    units = sum(pack.shape[1] for pack in own)
    block = 256 if width % 256 == 0 else width
    left = pl.BlockSpec((rows, block), lambda j: (0, j))
    return pl.pallas_call(
        functools.partial(head_grad_kernel, len(own)),
        out_shape=jax.ShapeDtypeStruct((width, units), jnp.bfloat16),
        grid=(width // block,),
        in_specs=[left] * 2 + [whole(pack.shape) for pack in (*own, *far)],
        out_specs=pl.BlockSpec((block, units), lambda j: (j, 0)),
        compiler_params=kernel_params(),
        cost_estimate=cost(4 * rows * width * units, 4 * rows * (width + units) + 2 * width * units, COSTS["head_grad"]),
        name="head_grad",
    )(*lefts, *own, *far)


def branch_kernel(
    own_ref, far_ref, middle_ref, grad_ref, gain_ref, wo_ref, wt_ref,
    mgrad_ref, branch_ref, go_ref, gt_ref, sums_ref,
):
    rows, width = middle_ref.shape
    pieces = row_pieces(rows, 256)

    def step_back(piece):
        take = slice(piece[0], piece[0] + piece[1])
        second_grad = own_ref[take, :].astype(jnp.float32) + far_ref[take, :].astype(jnp.float32)
        normed, inverse = normalise(middle_ref[take, :])
        wide = grad_ref[take, :].astype(jnp.float32)
        moved = second_grad * normed
        tilted = second_grad * gain_ref[...]
        mgrad = wide + inverse * (
            tilted
            - jnp.mean(tilted, axis=-1, keepdims=True)
            - normed * jnp.mean(tilted * normed, axis=-1, keepdims=True)
        )
        branch = mgrad.astype(jnp.bfloat16)
        mgrad_ref[take, :] = mgrad
        branch_ref[take, :] = branch
        sums = [
            jnp.sum(moved, axis=0, keepdims=True),
            jnp.sum(second_grad, axis=0, keepdims=True),
            jnp.sum(branch.astype(jnp.float32), axis=0, keepdims=True),
            jnp.sum(wide, axis=0, keepdims=True),
        ]
        return branch, sums

    def finish(piece, branch):
        take = slice(piece[0], piece[0] + piece[1])
        go_ref[:, take] = dot_nn(branch, wo_ref[...]).astype(jnp.bfloat16).T
        gt_ref[:, take] = dot_nn(branch, wt_ref[...]).astype(jnp.bfloat16).T

    totals = None
    branch, sums = step_back(pieces[0])
    totals = sums
    for number, piece in enumerate(pieces):
        now = branch
        if number + 1 < len(pieces):
            branch, sums = step_back(pieces[number + 1])
            totals = [a + b for a, b in zip(totals, sums)]
        finish(piece, now)
    if go_ref.shape[1] > rows:
        blank = jnp.zeros((go_ref.shape[0], go_ref.shape[1] - rows), jnp.bfloat16)
        go_ref[:, rows:] = blank
        gt_ref[:, rows:] = blank
    for index, line in enumerate(totals):
        sums_ref[index : index + 1, :] = line


def branch_back(own, far, middle, grads, gain, pack, cols):
    rows, width = middle.shape
    full = whole((rows, width))
    return pl.pallas_call(
        branch_kernel,
        out_shape=(
            jax.ShapeDtypeStruct((rows, width), jnp.float32),
            jax.ShapeDtypeStruct((rows, width), jnp.bfloat16),
            jax.ShapeDtypeStruct((cols, lanes(rows)), jnp.bfloat16),
            jax.ShapeDtypeStruct((cols, lanes(rows)), jnp.bfloat16),
            jax.ShapeDtypeStruct((4, width), jnp.float32),
        ),
        grid=(1,),
        in_specs=[
            full, full, full, full, whole((1, width)), whole((width, cols), (0, 3)), whole((width, cols), (0, 4))
        ],
        out_specs=(full, full, whole((cols, lanes(rows))), whole((cols, lanes(rows))), whole((4, width))),
        compiler_params=kernel_params(),
        cost_estimate=cost(4 * rows * width * cols, 18 * rows * width, COSTS["branch_back"]),
        name="branch_back",
    )(own, far, middle, grads, gain, pack, pack)


def side_grad_kernel(
    so_ref, st_ref, bo_ref, bt_ref, branch_ref, co_ref, ct_ref, out_ref
):
    step = pl.program_id(0)
    last = pl.num_programs(0) - 1

    @pl.when(step < last - 1)
    def _():
        total = dot_tn(so_ref[...], bo_ref[...]) + dot_tn(st_ref[...], bt_ref[...])
        out_ref[...] = total.astype(jnp.bfloat16)

    @pl.when(step == last - 1)
    def _():
        out_ref[...] = dot_tn(branch_ref[...], co_ref[:, : branch_ref.shape[0]].T).astype(jnp.bfloat16)

    @pl.when(step == last)
    def _():
        out_ref[...] = dot_tn(branch_ref[...], ct_ref[:, : branch_ref.shape[0]].T).astype(jnp.bfloat16)


def side_grads(second, back, branch, contexts):
    rows, width = branch.shape
    units, cols = back[0].shape[1], contexts[0].shape[0]
    steps = units // cols
    part = pl.BlockSpec((rows, cols), lambda j: (0, jnp.minimum(j, steps - 1)))
    return pl.pallas_call(
        side_grad_kernel,
        out_shape=jax.ShapeDtypeStruct((width, units + 2 * cols), jnp.bfloat16),
        grid=(steps + 2,),
        in_specs=[whole((rows, width))] * 2 + [part] * 2
        + [whole((rows, width))] + [whole((cols, lanes(rows)))] * 2,
        out_specs=pl.BlockSpec((width, cols), lambda j: (0, j)),
        compiler_params=kernel_params(),
        cost_estimate=cost(4 * rows * width * (units + cols), 4 * rows * (width + units), COSTS["weight_grad"]),
        name="side_grads",
    )(*second, *back, branch, *contexts)


def first_kernel(count, *refs):
    packs, (weight_ref, frames_ref, terms_ref, sums_ref, bias_ref, pack_ref) = refs[:count], refs[count:]
    rows, width = frames_ref.shape
    cols = pack_ref.shape[1] // 3
    q_factor = HD ** (-0.5)
    pieces = row_pieces(rows, 256)
    offset = 0
    for ref in packs:
        wide = ref.shape[1] // 3
        for part in range(3):
            place = part * cols + offset
            pack_ref[:, place : place + wide] = ref[:, part * wide : (part + 1) * wide]
        offset += wide

    def begin(piece):
        take = slice(piece[0], piece[0] + piece[1])
        return dot_nt(pack_ref[take, :cols], weight_ref[:, :cols]) * q_factor + dot_nt(
            pack_ref[take, cols:], weight_ref[:, cols:]
        )

    totals = None
    current = begin(pieces[0])
    for number, piece in enumerate(pieces):
        coming = begin(pieces[number + 1]) if number + 1 < len(pieces) else None
        take = slice(piece[0], piece[0] + piece[1])
        terms_ref[take, :] = current.astype(jnp.bfloat16)
        normed, _ = normalise(frames_ref[take, :].astype(jnp.float32))
        sums = [
            jnp.sum(current * normed, axis=0, keepdims=True),
            jnp.sum(current, axis=0, keepdims=True),
            jnp.sum(pack_ref[take, :].astype(jnp.float32), axis=0, keepdims=True),
        ]
        totals = sums if totals is None else [a + b for a, b in zip(totals, sums)]
        current = coming
    sums_ref[0:1, :] = totals[0]
    sums_ref[1:2, :] = totals[1]
    bias_ref[...] = totals[2]


def first_back(packs, weights, frames):
    rows, width = frames.shape
    wide = sum(pack.shape[1] for pack in packs)
    return pl.pallas_call(
        functools.partial(first_kernel, len(packs)),
        out_shape=(
            jax.ShapeDtypeStruct((rows, width), jnp.bfloat16),
            jax.ShapeDtypeStruct((2, width), jnp.float32),
            jax.ShapeDtypeStruct((1, wide), jnp.float32),
        ),
        grid=(1,),
        in_specs=[whole(pack.shape) for pack in packs] + [whole((width, wide)), whole((rows, width))],
        out_specs=(whole((rows, width)), whole((2, width)), whole((1, wide))),
        scratch_shapes=[pltpu.VMEM((rows, wide), jnp.bfloat16)],
        compiler_params=kernel_params(),
        cost_estimate=cost(2 * rows * width * wide, 2 * (rows + width) * wide + 4 * rows * width, COSTS["first_back"]),
        name="first_back",
    )(*packs, weights, frames)


def frames_kernel(frames_ref, own_ref, far_ref, mgrad_ref, gain_ref, out_ref):
    normed, inverse = normalise(frames_ref[...].astype(jnp.float32))
    tilted = (own_ref[...].astype(jnp.float32) + far_ref[...].astype(jnp.float32)) * gain_ref[...]
    out_ref[...] = (
        mgrad_ref[...]
        + inverse
        * (
            tilted
            - jnp.mean(tilted, axis=-1, keepdims=True)
            - normed * jnp.mean(tilted * normed, axis=-1, keepdims=True)
        )
    ).astype(jnp.bfloat16)


def frames_back(frames, own, far, mgrad, gain):
    rows, width = frames.shape
    block = 376 if rows % 376 == 0 else rows
    spec = pl.BlockSpec((block, width), lambda i: (i, 0))
    return pl.pallas_call(
        frames_kernel,
        out_shape=jax.ShapeDtypeStruct((rows, width), jnp.bfloat16),
        grid=(rows // block,),
        in_specs=[spec] * 4 + [whole((1, width))],
        out_specs=spec,
        compiler_params=kernel_params(),
        cost_estimate=cost(20 * rows * width, 12 * rows * width, COSTS["frames_back"]),
        name="frames_back",
    )(frames, own, far, mgrad, gain)


def swap_tp(piece):
    return lax.ppermute(piece, "tp", [(0, 1), (1, 0)])


def tie(*values):
    return lax.optimization_barrier(values)


def gather_steps(vector, other, fsdp):
    index = lax.axis_index("fsdp")
    side = lax.axis_index("tp")
    held = jnp.where(side == 0, jnp.stack([vector, other]), jnp.stack([other, vector]))
    bit = 1
    while bit < fsdp:
        other = lax.ppermute(held, "fsdp", [(i, i ^ bit) for i in range(fsdp)])
        low = (index & bit) == 0
        held = jnp.where(low, jnp.concatenate([held, other]), jnp.concatenate([other, held]))
        bit *= 2
    return held


def halving_order(fsdp):
    return [bit for bit in (1, 2, 8, 4, 16, 32, 64, 128) if bit < fsdp]


def halve(held, bit, left, fsdp, last=False):
    index = lax.axis_index("fsdp")
    mine = (index // bit) % 2
    parts = held if isinstance(held, list) else [held]
    outer = 2 ** sorted(left, reverse=True).index(bit)
    views = [part.reshape(outer, 2, -1, part.shape[-1]) for part in parts]

    def chosen(which):
        return jnp.concatenate(
            [lax.dynamic_index_in_dim(view, which, 1, keepdims=False) for view in views], axis=-1
        )

    other = lax.ppermute(chosen(1 - mine), "fsdp", [(i, i ^ bit) for i in range(fsdp)])
    total = chosen(mine).astype(jnp.float32) + other.astype(jnp.float32)
    return (total if last else total.astype(jnp.bfloat16)).reshape(-1, total.shape[-1])


def per_device_pair(
    frames, out_grad, clip_lengths, clip_order, w_query, w_key, w_value, b_query, b_value,
    w_out, b_out, w_expand, b_expand, w_reduce, b_reduce,
    first_gain, first_shift, second_gain, second_shift, *, fsdp,
):
    side = lax.axis_index("tp")
    slot = lax.axis_index("fsdp")
    clip_count = clip_order.shape[0]
    every_clip = jnp.arange(clip_count, dtype=jnp.int32)
    clip_id = jnp.sum(jnp.where(every_clip == slot, clip_order, 0))
    length = jnp.sum(jnp.where(every_clip == clip_id, clip_lengths, 0))
    frames, out_grad = frames[0], out_grad[0]
    rows, width = frames.shape
    cols = w_query.shape[1]
    heads = cols // HD
    units = w_expand.shape[1]
    q_factor = HD ** (-0.5)
    scal_own = jnp.stack([length, side * rows]).astype(jnp.int32)
    scal_far = jnp.stack([length, (1 - side) * rows]).astype(jnp.int32)

    wide_six = [first_gain, first_shift, second_gain, second_shift, b_out, b_reduce]
    small_own = jnp.concatenate(wide_six + [b_query, b_value, b_expand])
    out_turned = w_out.T
    small_far, out_other = swap_tp(small_own), swap_tp(out_turned)
    pack_one = lax.all_gather(
        jnp.concatenate([w_query, w_key, w_value, out_turned, out_other], axis=1),
        "fsdp", axis=0, tiled=True,
    )
    pack_two = lax.all_gather(
        jnp.concatenate([w_expand, w_reduce.T], axis=1), "fsdp", axis=0, tiled=True
    )
    sent_frames, small_far, out_other = tie(frames, small_far, out_other)
    frames_far = swap_tp(sent_frames)
    sent_grads, frames_far = tie(out_grad, frames_far)
    grads_far = swap_tp(sent_grads)
    small = gather_steps(small_own, small_far, fsdp)
    lot = first_gain.shape[0]
    whole_six = small[:, : 6 * lot].astype(jnp.float32).reshape(2 * fsdp, 6, lot)
    whole_six = whole_six.transpose(1, 0, 2).reshape(6, 1, width)
    gain_one, shift_one, gain_two, shift_two, out_bias, reduce_bias = [whole_six[i] for i in range(6)]
    mine = lax.dynamic_index_in_dim(
        small[:, 6 * lot :].astype(jnp.float32).reshape(fsdp, 2, -1), side, axis=1, keepdims=False
    )
    part = b_query.shape[0]
    bias_q = mine[:, :part].reshape(1, -1)
    bias_v = mine[:, part : 2 * part].reshape(1, -1)
    bias_e = mine[:, 2 * part :].reshape(1, -1)

    first_own, q_own, k_own, v_own = project(
        scal_own, frames, gain_one, shift_one, pack_one, bias_q, bias_v, heads
    )
    first_far, q_far, k_far, v_far = project(
        scal_far, frames_far, gain_one, shift_one, pack_one, bias_q, bias_v, heads
    )
    context_send, log_far = attend_rows(q_far, k_own, k_far, v_own, v_far)
    context_send, q_own = tie(context_send, q_own)
    context_far = swap_tp(context_send.reshape(cols, -1))
    context_own, log_own = attend_rows(q_own, k_own, k_far, v_own, v_far)
    context_own = context_own.reshape(cols, -1)
    middle, second_own = merge_heads(
        context_own, context_far, pack_one, frames, out_bias, gain_two, shift_two
    )

    second_far = swap_tp(second_own)
    hid_far, back_far, bsum_far, out_send, terms_send = feed(
        second_far, grads_far, pack_two, bias_e, units
    )
    terms_send, second_own = tie(terms_send, second_own)
    terms_far = swap_tp(terms_send)
    back_own, bsum_own, out_own, terms_own, d_reduce = feed(
        second_own, out_grad, pack_two, bias_e, units, (grads_far, hid_far)
    )
    g_reduce = lax.psum_scatter(d_reduce, "fsdp", scatter_dimension=0, tiled=True)
    mgrad, branch, up_own, up_send, sums_two = branch_back(
        terms_own, terms_far, middle, out_grad, gain_two, pack_one, cols
    )
    up_send, second_own = tie(up_send, second_own)
    up_far = swap_tp(up_send)
    d_side = side_grads(
        (second_own, second_far), (back_own, back_far), branch, (context_own, context_far)
    )

    turned = (heads, HD, lanes(rows))
    up_far, out_send, d_side = tie(up_far, out_send, d_side)
    out_far = swap_tp(out_send)
    ups = (up_own.reshape(turned), up_far.reshape(turned))
    steps = halving_order(fsdp)
    firsts = (first_own, first_far)

    def back(q_first, start, count):
        return attend_back_rows(
            (q_first, q_far), (k_own, k_far), (v_own, v_far), ups, (log_own, log_far), start, count
        )

    many = (heads + 1) // 2
    own_a, far_a = back(q_own, 0, many)
    own_a, out_far, d_side = tie(own_a, out_far, d_side)
    g_side = lax.psum_scatter(d_side, "fsdp", scatter_dimension=0, tiled=True)
    d_heads = head_grad(firsts, [own_a], [far_a])
    held_a = halve(d_heads, steps[0], steps, fsdp)
    held_a, q_own = tie(held_a, q_own)
    own_b, far_b = back(q_own, many, heads - many)
    held_a = halve(held_a, steps[1], steps[1:], fsdp)
    held_a, far_b = tie(held_a, far_b)
    first_send, sums_far, bias_far = first_back([far_a, far_b], pack_one, frames_far)
    first_send, far_b = tie(first_send, far_b)
    first_recv = swap_tp(first_send)
    held_b = head_grad(firsts, [own_b], [far_b])
    held_b, own_b = tie(held_b, own_b)
    first_keep, sums_own, bias_own = first_back([own_a, own_b], pack_one, frames)
    held_a = halve(held_a, steps[2], steps[2:], fsdp, len(steps) == 3)
    sums_one = sums_own + sums_far
    bias_sum = bias_own + bias_far
    wide_sums = jnp.concatenate([sums_one, sums_two])
    wide_sums = wide_sums.reshape(6, fsdp, 2, lot).transpose(1, 2, 0, 3).reshape(fsdp, 12 * lot)
    tall = jnp.concatenate(
        [
            wide_sums,
            (bias_sum[:, :cols] * q_factor).reshape(fsdp, -1),
            bias_sum[:, 2 * cols :].reshape(fsdp, -1),
            (bsum_own + bsum_far).reshape(fsdp, -1),
        ],
        axis=1,
    )
    wide = held_b.shape[1]
    extra = -(-tall.shape[1] // (8 * wide)) * 8
    tall = jnp.pad(tall, ((0, 0), (0, extra * wide - tall.shape[1]))).astype(jnp.bfloat16)
    lots = width // fsdp
    held_b = jnp.concatenate(
        [held_b.reshape(fsdp, lots, wide), tall.reshape(fsdp, extra, wide)], axis=1
    ).reshape(-1, wide)
    held_b = halve(held_b, steps[0], steps, fsdp)
    held_b = halve(held_b, steps[1], steps[1:], fsdp)
    out_frames = (
        middle + out_own.astype(jnp.float32) + out_far.astype(jnp.float32) + reduce_bias
    ).astype(jnp.bfloat16)
    for place in range(2, len(steps)):
        last = place + 1 == len(steps)
        if place > 2:
            held_a, held_b = tie(held_a, held_b)
            held_a = halve(held_a, steps[place], steps[place:], fsdp, last)
        if last:
            held_b, first_keep, out_frames = tie(held_b, first_keep, out_frames)
            frames_grad = frames_back(frames, first_keep, first_recv, mgrad, gain_one)
            held_b, frames_grad, g_side = tie(held_b, frames_grad, g_side)
        held_b = halve(held_b, steps[place], steps[place:], fsdp, last)
    held_b, small_sum = held_b[:lots], held_b[lots:].reshape(-1)
    g_expand, g_out = g_side[:, :units], g_side[:, units:]
    some = many * HD

    def joined(kind):
        rest = cols - some
        return jnp.concatenate(
            [held_a[:, kind * some : (kind + 1) * some], held_b[:, kind * rest : (kind + 1) * rest]], axis=1
        )

    g_query, g_key, g_value = joined(0), joined(1), joined(2)

    six = small_sum[: 12 * lot].reshape(2, 6 * lot)
    keep = lax.dynamic_index_in_dim(six, side, 0, keepdims=False)
    send = lax.dynamic_index_in_dim(six, 1 - side, 0, keepdims=False)
    six = (keep + swap_tp(send)).reshape(6, lot)
    rest = small_sum[12 * lot :]
    g_bq, g_bv = rest[:part], rest[part : 2 * part]
    g_be = rest[2 * part : 2 * part + b_expand.shape[0]]
    g_out_sum = g_out[:, :cols].astype(jnp.float32) + swap_tp(g_out[:, cols:]).astype(jnp.float32)
    return (
        out_frames[None],
        frames_grad[None],
        g_query,
        g_key,
        g_value,
        g_bq,
        g_bv,
        g_out_sum.T,
        six[4],
        g_expand.astype(jnp.float32),
        g_be,
        g_reduce.T.astype(jnp.float32),
        six[5],
        six[0],
        six[1],
        six[2],
        six[3],
    )


def solution(mesh):
    fsdp = mesh.shape["fsdp"]
    if mesh.shape["tp"] == 2 and fsdp & (fsdp - 1) == 0:

        def body(*args):
            return per_device_pair(*args, fsdp=fsdp) if args[0].shape[0] == 1 else per_device(*args)
    else:
        body = per_device
    return jax.shard_map(
        body,
        mesh=mesh,
        in_specs=(
            P("fsdp", "tp", None),
            P("fsdp", "tp", None),
            P(),
            P(),
            P("fsdp", "tp"),
            P("fsdp", "tp"),
            P("fsdp", "tp"),
            P(("tp", "fsdp")),
            P(("tp", "fsdp")),
            P("tp", "fsdp"),
            P(("fsdp", "tp")),
            P("fsdp", "tp"),
            P(("tp", "fsdp")),
            P("tp", "fsdp"),
            P(("fsdp", "tp")),
            P(("fsdp", "tp")),
            P(("fsdp", "tp")),
            P(("fsdp", "tp")),
            P(("fsdp", "tp")),
        ),
        out_specs=(
            P("fsdp", "tp", None),
            P("fsdp", "tp", None),
            P("fsdp", "tp"),
            P("fsdp", "tp"),
            P("fsdp", "tp"),
            P(("tp", "fsdp")),
            P(("tp", "fsdp")),
            P("tp", "fsdp"),
            P(("fsdp", "tp")),
            P("fsdp", "tp"),
            P(("tp", "fsdp")),
            P("tp", "fsdp"),
            P(("fsdp", "tp")),
            P(("fsdp", "tp")),
            P(("fsdp", "tp")),
            P(("fsdp", "tp")),
            P(("fsdp", "tp")),
        ),
        check_vma=False,
    )
```

```python
import functools

import jax
import jax.numpy as jnp
from jax import lax
from jax.experimental import pallas as pl
from jax.experimental.pallas import tpu as pltpu
from jax.sharding import PartitionSpec as P

HD = 80


EPSILON = 1e-05
MASKED = -1000000000.0
HIDDEN = -1e30


def layer_norm(features, norm_gain, norm_shift):
    row_mean = jnp.mean(features, axis=-1, keepdims=True)
    centred = features - row_mean
    row_var = jnp.mean(centred * centred, axis=-1, keepdims=True)
    inverse = lax.rsqrt(row_var + EPSILON)
    normed = centred * inverse
    return (normed * norm_gain + norm_shift, normed, inverse)


def norm_back(upstream, normed, inverse, norm_gain):
    tilted = upstream * norm_gain
    return inverse * (
        tilted
        - jnp.mean(tilted, axis=-1, keepdims=True)
        - normed * jnp.mean(tilted * normed, axis=-1, keepdims=True)
    )


def gelu_exact(inputs):
    return jax.nn.gelu(inputs, approximate=False)


def masked_scores(queries, key_rows, length):
    scores = jnp.einsum("qhe,khe->hqk", queries, key_rows, preferred_element_type=jnp.float32)
    allowed = jnp.arange(scores.shape[-1]) < length
    return jnp.where(allowed[None, None, :], scores, MASKED)


def attend(inputs):
    queries, key_rows, value_rows, length = inputs
    scores = masked_scores(queries, key_rows, length)
    row_top = jnp.max(scores, axis=-1, keepdims=True)
    raised = jnp.exp(scores - row_top)
    row_sum = jnp.sum(raised, axis=-1, keepdims=True)
    weights = (raised / row_sum).astype(jnp.bfloat16)
    context = jnp.einsum("hqk,khe->qhe", weights, value_rows, preferred_element_type=jnp.float32)
    return (context.astype(jnp.bfloat16), row_top[..., 0] + jnp.log(row_sum[..., 0]))


def attend_back(inputs):
    queries, key_rows, value_rows, length, log_total, context_grad = inputs
    scores = masked_scores(queries, key_rows, length)
    probs = jnp.exp(scores - log_total[..., None])
    weights = probs.astype(jnp.bfloat16)
    value_grad = jnp.einsum(
        "hqk,qhe->khe", weights, context_grad, preferred_element_type=jnp.float32
    )
    weight_grad = jnp.einsum(
        "qhe,khe->hqk", context_grad, value_rows, preferred_element_type=jnp.float32
    )
    row_inner = jnp.sum(weight_grad * probs, axis=-1, keepdims=True)
    score_grad = (probs * (weight_grad - row_inner)).astype(jnp.bfloat16)
    query_grad = jnp.einsum(
        "hqk,khe->qhe", score_grad, key_rows, preferred_element_type=jnp.float32
    )
    key_grad = jnp.einsum("hqk,qhe->khe", score_grad, queries, preferred_element_type=jnp.float32)
    return (
        query_grad.astype(jnp.bfloat16),
        key_grad.astype(jnp.bfloat16),
        value_grad.astype(jnp.bfloat16),
    )


def gather_inward(w_query, w_key, w_value, b_query, b_value, w_expand, b_expand):
    return (
        lax.all_gather(w_query, "fsdp", axis=0, tiled=True),
        lax.all_gather(w_key, "fsdp", axis=0, tiled=True),
        lax.all_gather(w_value, "fsdp", axis=0, tiled=True),
        lax.all_gather(b_query, "fsdp", axis=0, tiled=True),
        lax.all_gather(b_value, "fsdp", axis=0, tiled=True),
        lax.all_gather(w_expand, "fsdp", axis=0, tiled=True),
        lax.all_gather(b_expand, "fsdp", axis=0, tiled=True),
    )


def gather_outward(w_out, w_reduce):
    return (
        lax.all_gather(w_out, "fsdp", axis=1, tiled=True),
        lax.all_gather(w_reduce, "fsdp", axis=1, tiled=True),
    )


def per_device(
    frames,
    out_grad,
    clip_lengths,
    clip_order,
    w_query,
    w_key,
    w_value,
    b_query,
    b_value,
    w_out,
    b_out,
    w_expand,
    b_expand,
    w_reduce,
    b_reduce,
    first_gain,
    first_shift,
    second_gain,
    second_shift,
):
    per_group = frames.shape[0]
    clip_count = clip_order.shape[0]
    slot_ids = lax.axis_index("fsdp") * per_group + jnp.arange(per_group, dtype=jnp.int32)
    every_clip = jnp.arange(clip_count, dtype=jnp.int32)
    clip_ids = jnp.sum(
        jnp.where(every_clip[None, :] == slot_ids[:, None], clip_order[None, :], 0), axis=1
    )
    lengths = jnp.sum(
        jnp.where(every_clip[None, :] == clip_ids[:, None], clip_lengths[None, :], 0), axis=1
    )
    norm_params = (
        lax.all_gather(first_gain, ("fsdp", "tp"), axis=0, tiled=True),
        lax.all_gather(first_shift, ("fsdp", "tp"), axis=0, tiled=True),
        lax.all_gather(second_gain, ("fsdp", "tp"), axis=0, tiled=True),
        lax.all_gather(second_shift, ("fsdp", "tp"), axis=0, tiled=True),
        lax.all_gather(b_out, ("fsdp", "tp"), axis=0, tiled=True),
        lax.all_gather(b_reduce, ("fsdp", "tp"), axis=0, tiled=True),
    )
    gain_one, shift_one, gain_two, shift_two, out_bias, reduce_bias = [
        tensor.astype(jnp.float32) for tensor in norm_params
    ]
    wq_all, wk_all, wv_all, bq_all, bv_all, we_all, be_all = gather_inward(
        w_query, w_key, w_value, b_query, b_value, w_expand, b_expand
    )
    wo_all, wr_all = gather_outward(w_out, w_reduce)
    q_factor = HD ** (-0.5)
    frames_wide = frames.astype(jnp.float32)
    norm_one, normed_one, inverse_one = layer_norm(frames_wide, gain_one, shift_one)
    first_rows = lax.all_gather(norm_one.astype(jnp.bfloat16), "tp", axis=1, tiled=True)
    seq_len = first_rows.shape[1]
    queries = (
        (
            jnp.einsum("csd,de->cse", first_rows, wq_all, preferred_element_type=jnp.float32)
            + bq_all.astype(jnp.float32)
        )
        * q_factor
    ).astype(jnp.bfloat16)
    keys = jnp.einsum("csd,de->cse", first_rows, wk_all, preferred_element_type=jnp.float32).astype(
        jnp.bfloat16
    )
    values = (
        jnp.einsum("csd,de->cse", first_rows, wv_all, preferred_element_type=jnp.float32)
        + bv_all.astype(jnp.float32)
    ).astype(jnp.bfloat16)
    head_shape = (per_group, seq_len, -1, HD)
    query_heads = queries.reshape(head_shape)
    key_heads = keys.reshape(head_shape)
    value_heads = values.reshape(head_shape)
    context, log_total = lax.map(attend, (query_heads, key_heads, value_heads, lengths))
    context_flat = context.reshape(per_group, seq_len, -1)
    attn_terms = jnp.einsum("cse,ed->csd", context_flat, wo_all, preferred_element_type=jnp.float32)
    attn_part = lax.psum_scatter(
        attn_terms.astype(jnp.bfloat16), "tp", scatter_dimension=1, tiled=True
    ).astype(jnp.float32)
    middle = frames_wide + attn_part + out_bias
    norm_two, normed_two, inverse_two = layer_norm(middle, gain_two, shift_two)
    second_rows = lax.all_gather(norm_two.astype(jnp.bfloat16), "tp", axis=1, tiled=True)
    expanded = jnp.einsum(
        "csd,df->csf", second_rows, we_all, preferred_element_type=jnp.float32
    ) + be_all.astype(jnp.float32)
    activated, gelu_pull = jax.vjp(gelu_exact, expanded)
    hidden = activated.astype(jnp.bfloat16)
    mlp_terms = jnp.einsum("csf,fd->csd", hidden, wr_all, preferred_element_type=jnp.float32)
    out_frames = (
        middle
        + lax.psum_scatter(
            mlp_terms.astype(jnp.bfloat16), "tp", scatter_dimension=1, tiled=True
        ).astype(jnp.float32)
        + reduce_bias
    ).astype(jnp.bfloat16)
    wq_all, wk_all, wv_all, bq_all, bv_all, we_all, be_all = gather_inward(
        w_query, w_key, w_value, b_query, b_value, w_expand, b_expand
    )
    wo_all, wr_all = gather_outward(w_out, w_reduce)
    grad_wide = out_grad.astype(jnp.float32)
    grad_rows = lax.all_gather(out_grad, "tp", axis=1, tiled=True)
    w_reduce_grad = jnp.einsum("csf,csd->fd", hidden, grad_rows, preferred_element_type=jnp.float32)
    hidden_grad = jnp.einsum("csd,fd->csf", grad_rows, wr_all, preferred_element_type=jnp.float32)
    expanded_grad = gelu_pull(hidden_grad)[0].astype(jnp.bfloat16)
    b_expand_grad = jnp.sum(expanded_grad.astype(jnp.float32), axis=(0, 1))
    w_expand_grad = jnp.einsum(
        "csd,csf->df", second_rows, expanded_grad, preferred_element_type=jnp.float32
    )
    second_terms = jnp.einsum(
        "csf,df->csd", expanded_grad, we_all, preferred_element_type=jnp.float32
    )
    second_grad = lax.psum_scatter(
        second_terms.astype(jnp.bfloat16), "tp", scatter_dimension=1, tiled=True
    ).astype(jnp.float32)
    second_gain_grad = jnp.sum(second_grad * normed_two, axis=(0, 1))
    second_shift_grad = jnp.sum(second_grad, axis=(0, 1))
    middle_grad = grad_wide + norm_back(second_grad, normed_two, inverse_two, gain_two)
    branch_grad = middle_grad.astype(jnp.bfloat16)
    b_out_grad = jnp.sum(branch_grad.astype(jnp.float32), axis=(0, 1))
    b_reduce_grad = jnp.sum(grad_wide, axis=(0, 1))
    branch_rows = lax.all_gather(branch_grad, "tp", axis=1, tiled=True)
    w_out_grad = jnp.einsum(
        "cse,csd->ed", context_flat, branch_rows, preferred_element_type=jnp.float32
    )
    context_grad = jnp.einsum(
        "csd,ed->cse", branch_rows, wo_all, preferred_element_type=jnp.float32
    ).astype(jnp.bfloat16)
    query_grad, key_grad, value_grad = lax.map(
        attend_back,
        (query_heads, key_heads, value_heads, lengths, log_total, context_grad.reshape(head_shape)),
    )
    query_grad = query_grad.reshape(per_group, seq_len, -1)
    key_grad = key_grad.reshape(per_group, seq_len, -1)
    value_grad = value_grad.reshape(per_group, seq_len, -1)
    w_query_grad = (
        jnp.einsum("csd,cse->de", first_rows, query_grad, preferred_element_type=jnp.float32)
        * q_factor
    )
    b_query_grad = jnp.sum(query_grad.astype(jnp.float32), axis=(0, 1)) * q_factor
    w_key_grad = jnp.einsum("csd,cse->de", first_rows, key_grad, preferred_element_type=jnp.float32)
    w_value_grad = jnp.einsum(
        "csd,cse->de", first_rows, value_grad, preferred_element_type=jnp.float32
    )
    b_value_grad = jnp.sum(value_grad.astype(jnp.float32), axis=(0, 1))
    first_terms = (
        jnp.einsum("cse,de->csd", query_grad, wq_all, preferred_element_type=jnp.float32) * q_factor
        + jnp.einsum("cse,de->csd", key_grad, wk_all, preferred_element_type=jnp.float32)
        + jnp.einsum("cse,de->csd", value_grad, wv_all, preferred_element_type=jnp.float32)
    )
    first_grad = lax.psum_scatter(
        first_terms.astype(jnp.bfloat16), "tp", scatter_dimension=1, tiled=True
    ).astype(jnp.float32)
    first_gain_grad = jnp.sum(first_grad * normed_one, axis=(0, 1))
    first_shift_grad = jnp.sum(first_grad, axis=(0, 1))
    frames_grad = (middle_grad + norm_back(first_grad, normed_one, inverse_one, gain_one)).astype(
        jnp.bfloat16
    )
    inward_grads = (
        lax.psum_scatter(
            w_query_grad.astype(jnp.bfloat16), "fsdp", scatter_dimension=0, tiled=True
        ).astype(jnp.float32),
        lax.psum_scatter(
            w_key_grad.astype(jnp.bfloat16), "fsdp", scatter_dimension=0, tiled=True
        ).astype(jnp.float32),
        lax.psum_scatter(
            w_value_grad.astype(jnp.bfloat16), "fsdp", scatter_dimension=0, tiled=True
        ).astype(jnp.float32),
        lax.psum_scatter(
            b_query_grad.astype(jnp.bfloat16), "fsdp", scatter_dimension=0, tiled=True
        ).astype(jnp.float32),
        lax.psum_scatter(
            b_value_grad.astype(jnp.bfloat16), "fsdp", scatter_dimension=0, tiled=True
        ).astype(jnp.float32),
        lax.psum_scatter(
            w_expand_grad.astype(jnp.bfloat16), "fsdp", scatter_dimension=0, tiled=True
        ).astype(jnp.float32),
        lax.psum_scatter(
            b_expand_grad.astype(jnp.bfloat16), "fsdp", scatter_dimension=0, tiled=True
        ).astype(jnp.float32),
    )
    outward_grads = (
        lax.psum_scatter(
            w_out_grad.astype(jnp.bfloat16), "fsdp", scatter_dimension=1, tiled=True
        ).astype(jnp.float32),
        lax.psum_scatter(
            w_reduce_grad.astype(jnp.bfloat16), "fsdp", scatter_dimension=1, tiled=True
        ).astype(jnp.float32),
    )
    small_grads = (
        lax.psum_scatter(first_gain_grad, ("fsdp", "tp"), scatter_dimension=0, tiled=True),
        lax.psum_scatter(first_shift_grad, ("fsdp", "tp"), scatter_dimension=0, tiled=True),
        lax.psum_scatter(second_gain_grad, ("fsdp", "tp"), scatter_dimension=0, tiled=True),
        lax.psum_scatter(second_shift_grad, ("fsdp", "tp"), scatter_dimension=0, tiled=True),
        lax.psum_scatter(b_out_grad, ("fsdp", "tp"), scatter_dimension=0, tiled=True),
        lax.psum_scatter(b_reduce_grad, ("fsdp", "tp"), scatter_dimension=0, tiled=True),
    )
    return (
        out_frames,
        frames_grad,
        inward_grads[0],
        inward_grads[1],
        inward_grads[2],
        inward_grads[3],
        inward_grads[4],
        outward_grads[0],
        small_grads[4],
        inward_grads[5],
        inward_grads[6],
        outward_grads[1],
        small_grads[5],
        small_grads[0],
        small_grads[1],
        small_grads[2],
        small_grads[3],
    )


VMEM_LIMIT = 60 << 20
PAD = 128
COSTS = {'project': 3.0, 'attend': 3.0, 'merge_heads': 3.0, 'feed': 3.0, 'weight_grad': 3.0, 'head_grad': 0.02, 'branch_back': 3.0, 'out_weight_grad': 0.02, 'first_back': 0.02, 'frames_back': 0.02, 'attend_back': (8.0, 0.02)}


def kernel_params():
    return pltpu.CompilerParams(vmem_limit_bytes=VMEM_LIMIT)


def cost(flops, moved, scale):
    return pl.CostEstimate(flops=int(scale * flops), bytes_accessed=int(min(1.0, scale) * moved), transcendentals=0)


def lanes(rows):
    return -(-rows // PAD) * PAD


def row_pieces(rows, size):
    return [(start, min(size, rows - start)) for start in range(0, rows, size)]


def whole(shape, fixed=None):
    index = fixed if fixed is not None else (0,) * len(shape)
    return pl.BlockSpec(shape, lambda *_: index)


def normalise(rows):
    row_mean = jnp.mean(rows, axis=-1, keepdims=True)
    centred = rows - row_mean
    inverse = lax.rsqrt(jnp.mean(centred * centred, axis=-1, keepdims=True) + EPSILON)
    return centred * inverse, inverse


def dot_nn(left, right):
    return jnp.dot(left, right, preferred_element_type=jnp.float32)


def dot_nt(left, right):
    return lax.dot_general(left, right, (((1,), (1,)), ((), ())), preferred_element_type=jnp.float32)


def dot_tn(left, right):
    return lax.dot_general(left, right, (((0,), (0,)), ((), ())), preferred_element_type=jnp.float32)


def project_kernel(
    heads, scal_ref, frames_ref, gain_ref, shift_ref, weight_ref, bq_ref, bv_ref,
    first_ref, q_ref, k_ref, v_ref,
):
    rows, width = frames_ref.shape
    cols = heads * HD
    length, start = scal_ref[0], scal_ref[1]
    q_factor = HD ** (-0.5)
    pieces = row_pieces(rows, 256)

    def norm(piece):
        normed, _ = normalise(frames_ref[piece[0] : piece[0] + piece[1], :].astype(jnp.float32))
        first = (normed * gain_ref[...] + shift_ref[...]).astype(jnp.bfloat16)
        first_ref[piece[0] : piece[0] + piece[1], :] = first
        return first

    def split(block, offset, filler, lane):
        if offset + PAD <= block.shape[1]:
            part = block[:, offset : offset + PAD]
        else:
            back = block.shape[1] - PAD
            part = pltpu.roll(block[:, back:], PAD - (offset - back), 1)
        return jnp.where(lane < HD, part, filler).astype(jnp.bfloat16)

    def finish(piece, out):
        lane = lax.broadcasted_iota(jnp.int32, (piece[1], PAD), 1)
        position = lax.broadcasted_iota(jnp.int32, (piece[1], PAD), 0) + (start + piece[0])
        one = jnp.where(lane == HD, 1.0, 0.0)
        hide = jnp.where((lane == HD) & (position >= length), HIDDEN, 0.0)
        queries = (out[:, :cols] + bq_ref[...]) * q_factor
        keys = out[:, cols : 2 * cols]
        values = out[:, 2 * cols :] + bv_ref[...]
        for head in range(heads):
            where = (head, slice(piece[0], piece[0] + piece[1]), slice(None))
            q_ref[where] = split(queries, head * HD, one, lane)
            k_ref[where] = split(keys, head * HD, hide, lane)
            v_ref[where] = split(values, head * HD, 0.0, lane)

    first = norm(pieces[0])
    for number, piece in enumerate(pieces):
        out = dot_nn(first, weight_ref[...])
        if number + 1 < len(pieces):
            first = norm(pieces[number + 1])
        finish(piece, out)


def project(scalars, frames, gain, shift, weights, bias_q, bias_v, heads):
    rows, width = frames.shape
    cols = heads * HD
    head_out = jax.ShapeDtypeStruct((heads, rows, PAD), jnp.bfloat16)
    return pl.pallas_call(
        functools.partial(project_kernel, heads),
        out_shape=(jax.ShapeDtypeStruct((rows, width), jnp.bfloat16), head_out, head_out, head_out),
        grid_spec=pltpu.PrefetchScalarGridSpec(
            num_scalar_prefetch=1,
            grid=(1,),
            in_specs=[
                whole((rows, width)), whole((1, width)), whole((1, width)),
                whole((width, 3 * cols)), whole((1, cols)), whole((1, cols)),
            ],
            out_specs=(whole((rows, width)),) + (whole((heads, rows, PAD)),) * 3,
        ),
        compiler_params=kernel_params(),
        cost_estimate=cost(2 * rows * width * 3 * cols, 4 * rows * width + 6 * width * cols, COSTS["project"]),
        name="project",
    )(scalars, frames, gain, shift, weights, bias_q, bias_v)


def attend_kernel(q_ref, ko_ref, kt_ref, vo_ref, vt_ref, out_ref, log_ref):
    per_step, rows, _ = q_ref.shape
    half = -(-rows // 256) * 128
    pieces = [(head, start, size) for head in range(per_step) for start, size in row_pieces(rows, half)]
    keys = [jnp.concatenate([ko_ref[h], kt_ref[h]], axis=0) for h in range(per_step)]
    values = [jnp.concatenate([vo_ref[h], vt_ref[h]], axis=0).T[:HD] for h in range(per_step)]

    def scores(piece):
        head, start, size = piece
        return dot_nt(keys[head], q_ref[head, start : start + size, :])

    def finish(piece, score):
        head, start, size = piece
        top = jnp.max(score, axis=0, keepdims=True)
        raised = jnp.exp(score - top)
        total = jnp.sum(raised, axis=0, keepdims=True)
        context = dot_nn(values[head], raised.astype(jnp.bfloat16)) / total
        out_ref[head, :, start : start + size] = context.astype(jnp.bfloat16)
        log_ref[head, :, start : start + size] = top + jnp.log(total)

    if out_ref.shape[2] > rows:
        out_ref[:, :, rows:] = jnp.zeros((per_step, HD, out_ref.shape[2] - rows), jnp.bfloat16)
    current = scores(pieces[0])
    for number, piece in enumerate(pieces):
        coming = scores(pieces[number + 1]) if number + 1 < len(pieces) else None
        finish(piece, current)
        current = coming


def attend_rows(queries, keys_own, keys_far, values_own, values_far):
    heads, rows, _ = queries.shape
    per_step = 2 if heads % 2 == 0 else 1
    spec = pl.BlockSpec((per_step, rows, PAD), lambda h: (h, 0, 0))
    return pl.pallas_call(
        attend_kernel,
        out_shape=(
            jax.ShapeDtypeStruct((heads, HD, lanes(rows)), jnp.bfloat16),
            jax.ShapeDtypeStruct((heads, 1, rows), jnp.float32),
        ),
        grid=(heads // per_step,),
        in_specs=[spec] * 5,
        out_specs=(
            pl.BlockSpec((per_step, HD, lanes(rows)), lambda h: (h, 0, 0)),
            pl.BlockSpec((per_step, 1, rows), lambda h: (h, 0, 0)),
        ),
        compiler_params=kernel_params(),
        cost_estimate=cost(heads * 2 * rows * 2 * rows * 2 * 400, heads * rows * PAD * 12, COSTS["attend"]),
        name="attend",
    )(queries, keys_own, keys_far, values_own, values_far)


def attend_back_kernel(
    qo_ref, qt_ref, ko_ref, kt_ref, vo_ref, vt_ref, go_ref, gt_ref, lo_ref, lt_ref,
    own_ref, far_ref, dq_ref,
):
    rows = qo_ref.shape[1]
    cols = own_ref.shape[1] // 3
    keys = jnp.concatenate([ko_ref[0], kt_ref[0]], axis=0)
    values = jnp.concatenate([vo_ref[0], vt_ref[0]], axis=0)
    keys_turned = keys.T[:HD]
    pieces = [(side, start, size) for side in range(2) for start, size in row_pieces(rows, 256)]
    sides = ((qo_ref, go_ref, lo_ref), (qt_ref, gt_ref, lt_ref))

    def query(piece):
        side, start, size = piece
        return sides[side][0][0, start : start + size, :]

    def upstream(piece):
        side, start, size = piece
        return sides[side][1][0, :, start : start + size]

    def begin(piece):
        score = dot_nt(keys, query(piece))
        padded = jnp.concatenate(
            [upstream(piece), jnp.zeros((PAD - HD, piece[2]), jnp.bfloat16)], axis=0
        )
        return score, dot_nn(values, padded)

    def middle(piece, score, weight_grad):
        side, start, size = piece
        probs = jnp.exp(score - sides[side][2][0, :, start : start + size])
        tilted = probs * weight_grad
        inner = jnp.sum(tilted, axis=0, keepdims=True)
        return probs.astype(jnp.bfloat16), (tilted - probs * inner).astype(jnp.bfloat16)

    total_k = total_v = None
    current = begin(pieces[0])
    for number, piece in enumerate(pieces):
        coming = begin(pieces[number + 1]) if number + 1 < len(pieces) else None
        weights, score_grad = middle(piece, *current)
        value_part = dot_nt(weights, upstream(piece))
        key_part = dot_nn(score_grad, query(piece))
        query_grad = dot_nn(keys_turned, score_grad)
        side, start, size = piece
        dq_ref[side * rows + start : side * rows + start + size, :] = query_grad.T.astype(jnp.bfloat16)
        total_v = value_part if total_v is None else total_v + value_part
        total_k = key_part if total_k is None else total_k + key_part
        current = coming
    key_grad = total_k[:, :HD].astype(jnp.bfloat16)
    value_grad = total_v.astype(jnp.bfloat16)
    for head in range(cols // HD):

        @pl.when(pl.program_id(0) == head)
        def _(head=head):
            for part, grad in enumerate((dq_ref[...], key_grad, value_grad)):
                take = slice(part * cols + head * HD, part * cols + (head + 1) * HD)
                own_ref[:, take] = grad[:rows]
                far_ref[:, take] = grad[rows:]


def attend_back_rows(queries, keys, values, upstream, logs, start, heads):
    rows = queries[0].shape[1]
    spec = pl.BlockSpec((1, rows, PAD), lambda h: (h + start, 0, 0))
    turned = pl.BlockSpec((1, HD, lanes(rows)), lambda h: (h + start, 0, 0))
    line = pl.BlockSpec((1, 1, rows), lambda h: (h + start, 0, 0))
    packed = (rows, 3 * heads * HD)
    return pl.pallas_call(
        attend_back_kernel,
        out_shape=(jax.ShapeDtypeStruct(packed, jnp.bfloat16),) * 2,
        grid=(heads,),
        in_specs=[spec] * 6 + [turned] * 2 + [line] * 2,
        out_specs=(whole(packed),) * 2,
        scratch_shapes=[pltpu.VMEM((2 * rows, HD), jnp.bfloat16)],
        compiler_params=kernel_params(),
        cost_estimate=cost(heads * 4 * rows * rows * 2 * 900, heads * rows * PAD * 24, COSTS["attend_back"][start > 0]),
        name="attend_back",
    )(*queries, *keys, *values, *upstream, *logs)


def merge_kernel(
    co_ref, ct_ref, wo_ref, wt_ref, frames_ref, bias_ref, gain_ref, shift_ref, middle_ref, second_ref,
):
    rows = frames_ref.shape[0]
    own, far = co_ref[:, :rows].T, ct_ref[:, :rows].T
    pieces = row_pieces(rows, 256)

    def branch(piece):
        take = slice(piece[0], piece[0] + piece[1])
        return dot_nt(own[take], wo_ref[...]) + dot_nt(far[take], wt_ref[...])

    def finish(piece, part):
        take = slice(piece[0], piece[0] + piece[1])
        middle = frames_ref[take, :].astype(jnp.float32) + part + bias_ref[...]
        middle_ref[take, :] = middle
        normed, _ = normalise(middle)
        second_ref[take, :] = (normed * gain_ref[...] + shift_ref[...]).astype(jnp.bfloat16)

    current = branch(pieces[0])
    for number, piece in enumerate(pieces):
        coming = branch(pieces[number + 1]) if number + 1 < len(pieces) else None
        finish(piece, current)
        current = coming


def merge_heads(context_own, context_far, pack, frames, bias, gain, shift):
    rows, width = frames.shape
    cols = context_own.shape[0]
    return pl.pallas_call(
        merge_kernel,
        out_shape=(
            jax.ShapeDtypeStruct((rows, width), jnp.float32),
            jax.ShapeDtypeStruct((rows, width), jnp.bfloat16),
        ),
        grid=(1,),
        in_specs=[
            whole((cols, lanes(rows))), whole((cols, lanes(rows))), whole((width, cols), (0, 3)),
            whole((width, cols), (0, 4)), whole((rows, width)), whole((1, width)), whole((1, width)), whole((1, width)),
        ],
        out_specs=(whole((rows, width)),) * 2,
        compiler_params=kernel_params(),
        cost_estimate=cost(4 * rows * width * cols, 10 * rows * width + 4 * width * cols, COSTS["merge_heads"]),
        name="merge_heads",
    )(context_own, context_far, pack, pack, frames, bias, gain, shift)


def feed_kernel(
    grads_too, second_ref, grad_ref, expand_ref, reduce_ref, bias_ref, *refs,
):
    if grads_too:
        far_ref, hid_ref, back_ref, bsum_ref, out_ref, terms_ref, dred_ref, out_acc, terms_acc, hidden_ref = refs
    else:
        hidden_ref, back_ref, bsum_ref, out_ref, terms_ref, out_acc, terms_acc = refs
    step = pl.program_id(0)
    rows = second_ref.shape[0]
    pieces = row_pieces(rows, 376 if rows % 376 == 0 else 256)
    expand, reduce = expand_ref[...], reduce_ref[...]

    def begin(piece):
        take = slice(piece[0], piece[0] + piece[1])
        return dot_nn(second_ref[take, :], expand), dot_nn(grad_ref[take, :], reduce)

    @pl.when(step == 0)
    def _():
        out_acc[...] = jnp.zeros_like(out_acc)
        terms_acc[...] = jnp.zeros_like(terms_acc)

    sums = None
    current = begin(pieces[0])
    for number, piece in enumerate(pieces):
        coming = begin(pieces[number + 1]) if number + 1 < len(pieces) else None
        take = slice(piece[0], piece[0] + piece[1])
        raw, upstream = current
        raw = raw + bias_ref[...]
        below = 0.5 + 0.5 * lax.erf(raw * 0.7071067811865476)
        density = jnp.exp(raw * raw * -0.5) * 0.3989422804014327
        hidden = (raw * below).astype(jnp.bfloat16)
        back = (upstream * (below + raw * density)).astype(jnp.bfloat16)
        hidden_ref[take, :] = hidden
        back_ref[take, :] = back
        part = jnp.sum(back.astype(jnp.float32), axis=0, keepdims=True)
        sums = part if sums is None else sums + part
        terms_acc[take, :] += dot_nt(back, expand)
        out_acc[take, :] += dot_nt(hidden, reduce)
        current = coming
    bsum_ref[...] = sums
    if grads_too:
        total = dot_tn(far_ref[...], hid_ref[...]) + dot_tn(grad_ref[...], hidden_ref[...])
        dred_ref[...] = total.astype(jnp.bfloat16)

    @pl.when(step == pl.num_programs(0) - 1)
    def _():
        out_ref[...] = out_acc[...].astype(jnp.bfloat16)
        terms_ref[...] = terms_acc[...].astype(jnp.bfloat16)


def feed(second, grads, pack, bias, units, far=None):
    rows, width = second.shape
    block = 512 if units % 512 == 0 else units
    steps = units // block
    wide = pl.BlockSpec((rows, block), lambda j: (0, j))
    weights = [
        pl.BlockSpec((width, block), lambda j: (0, j)),
        pl.BlockSpec((width, block), lambda j: (0, j + steps)),
    ]
    line = pl.BlockSpec((1, block), lambda j: (0, j))
    hidden = jax.ShapeDtypeStruct((rows, units), jnp.bfloat16)
    full = jax.ShapeDtypeStruct((rows, width), jnp.bfloat16)
    outs = [hidden, jax.ShapeDtypeStruct((1, units), jnp.float32), full, full]
    out_specs = [wide, line, whole((rows, width)), whole((rows, width))]
    scratch = [pltpu.VMEM((rows, width), jnp.float32)] * 2
    in_specs = [whole((rows, width)), whole((rows, width)), *weights, line]
    if far is None:
        outs, out_specs = [hidden] + outs, [wide] + out_specs
    else:
        outs = outs + [jax.ShapeDtypeStruct((width, units), jnp.bfloat16)]
        out_specs = out_specs + [weights[0]]
        in_specs = in_specs + [whole((rows, width)), wide]
        scratch = scratch + [pltpu.VMEM((rows, block), jnp.bfloat16)]
    flops = (8 if far is None else 12) * rows * width * units
    return pl.pallas_call(
        functools.partial(feed_kernel, far is not None),
        out_shape=tuple(outs),
        grid=(steps,),
        in_specs=in_specs,
        out_specs=tuple(out_specs),
        scratch_shapes=scratch,
        compiler_params=kernel_params(),
        cost_estimate=cost(flops, 8 * rows * (units + width) + 4 * width * units, COSTS["feed"]),
        name="feed" if far is None else "feed_last",
    )(second, grads, pack, pack, bias, *(far or ()))


def head_grad_kernel(count, lo_ref, lt_ref, *refs):
    out_ref = refs[2 * count]
    offset = 0
    for own_ref, far_ref in zip(refs[:count], refs[count : 2 * count]):
        wide = own_ref.shape[1]
        total = dot_tn(lo_ref[...], own_ref[...]) + dot_tn(lt_ref[...], far_ref[...])
        lane = lax.broadcasted_iota(jnp.int32, (1, wide), 1)
        total = total * jnp.where(lane < wide // 3, HD ** (-0.5), 1.0)
        out_ref[:, offset : offset + wide] = total.astype(jnp.bfloat16)
        offset += wide


def head_grad(lefts, own, far):
    rows, width = lefts[0].shape
    units = sum(pack.shape[1] for pack in own)
    block = 256 if width % 256 == 0 else width
    left = pl.BlockSpec((rows, block), lambda j: (0, j))
    return pl.pallas_call(
        functools.partial(head_grad_kernel, len(own)),
        out_shape=jax.ShapeDtypeStruct((width, units), jnp.bfloat16),
        grid=(width // block,),
        in_specs=[left] * 2 + [whole(pack.shape) for pack in (*own, *far)],
        out_specs=pl.BlockSpec((block, units), lambda j: (j, 0)),
        compiler_params=kernel_params(),
        cost_estimate=cost(4 * rows * width * units, 4 * rows * (width + units) + 2 * width * units, COSTS["head_grad"]),
        name="head_grad",
    )(*lefts, *own, *far)


def branch_kernel(
    own_ref, far_ref, middle_ref, grad_ref, gain_ref, wo_ref, wt_ref,
    mgrad_ref, branch_ref, go_ref, gt_ref, sums_ref,
):
    rows, width = middle_ref.shape
    pieces = row_pieces(rows, 256)

    def step_back(piece):
        take = slice(piece[0], piece[0] + piece[1])
        second_grad = own_ref[take, :].astype(jnp.float32) + far_ref[take, :].astype(jnp.float32)
        normed, inverse = normalise(middle_ref[take, :])
        wide = grad_ref[take, :].astype(jnp.float32)
        moved = second_grad * normed
        tilted = second_grad * gain_ref[...]
        mgrad = wide + inverse * (
            tilted
            - jnp.mean(tilted, axis=-1, keepdims=True)
            - normed * jnp.mean(tilted * normed, axis=-1, keepdims=True)
        )
        branch = mgrad.astype(jnp.bfloat16)
        mgrad_ref[take, :] = mgrad
        branch_ref[take, :] = branch
        sums = [
            jnp.sum(moved, axis=0, keepdims=True),
            jnp.sum(second_grad, axis=0, keepdims=True),
            jnp.sum(branch.astype(jnp.float32), axis=0, keepdims=True),
            jnp.sum(wide, axis=0, keepdims=True),
        ]
        return branch, sums

    def finish(piece, branch):
        take = slice(piece[0], piece[0] + piece[1])
        go_ref[:, take] = dot_nn(branch, wo_ref[...]).astype(jnp.bfloat16).T
        gt_ref[:, take] = dot_nn(branch, wt_ref[...]).astype(jnp.bfloat16).T

    totals = None
    branch, sums = step_back(pieces[0])
    totals = sums
    for number, piece in enumerate(pieces):
        now = branch
        if number + 1 < len(pieces):
            branch, sums = step_back(pieces[number + 1])
            totals = [a + b for a, b in zip(totals, sums)]
        finish(piece, now)
    if go_ref.shape[1] > rows:
        blank = jnp.zeros((go_ref.shape[0], go_ref.shape[1] - rows), jnp.bfloat16)
        go_ref[:, rows:] = blank
        gt_ref[:, rows:] = blank
    for index, line in enumerate(totals):
        sums_ref[index : index + 1, :] = line


def branch_back(own, far, middle, grads, gain, pack, cols):
    rows, width = middle.shape
    full = whole((rows, width))
    return pl.pallas_call(
        branch_kernel,
        out_shape=(
            jax.ShapeDtypeStruct((rows, width), jnp.float32),
            jax.ShapeDtypeStruct((rows, width), jnp.bfloat16),
            jax.ShapeDtypeStruct((cols, lanes(rows)), jnp.bfloat16),
            jax.ShapeDtypeStruct((cols, lanes(rows)), jnp.bfloat16),
            jax.ShapeDtypeStruct((4, width), jnp.float32),
        ),
        grid=(1,),
        in_specs=[
            full, full, full, full, whole((1, width)), whole((width, cols), (0, 3)), whole((width, cols), (0, 4))
        ],
        out_specs=(full, full, whole((cols, lanes(rows))), whole((cols, lanes(rows))), whole((4, width))),
        compiler_params=kernel_params(),
        cost_estimate=cost(4 * rows * width * cols, 18 * rows * width, COSTS["branch_back"]),
        name="branch_back",
    )(own, far, middle, grads, gain, pack, pack)


def side_grad_kernel(
    so_ref, st_ref, bo_ref, bt_ref, branch_ref, co_ref, ct_ref, out_ref
):
    step = pl.program_id(0)
    last = pl.num_programs(0) - 1

    @pl.when(step < last - 1)
    def _():
        total = dot_tn(so_ref[...], bo_ref[...]) + dot_tn(st_ref[...], bt_ref[...])
        out_ref[...] = total.astype(jnp.bfloat16)

    @pl.when(step == last - 1)
    def _():
        out_ref[...] = dot_tn(branch_ref[...], co_ref[:, : branch_ref.shape[0]].T).astype(jnp.bfloat16)

    @pl.when(step == last)
    def _():
        out_ref[...] = dot_tn(branch_ref[...], ct_ref[:, : branch_ref.shape[0]].T).astype(jnp.bfloat16)


def side_grads(second, back, branch, contexts):
    rows, width = branch.shape
    units, cols = back[0].shape[1], contexts[0].shape[0]
    steps = units // cols
    part = pl.BlockSpec((rows, cols), lambda j: (0, jnp.minimum(j, steps - 1)))
    return pl.pallas_call(
        side_grad_kernel,
        out_shape=jax.ShapeDtypeStruct((width, units + 2 * cols), jnp.bfloat16),
        grid=(steps + 2,),
        in_specs=[whole((rows, width))] * 2 + [part] * 2
        + [whole((rows, width))] + [whole((cols, lanes(rows)))] * 2,
        out_specs=pl.BlockSpec((width, cols), lambda j: (0, j)),
        compiler_params=kernel_params(),
        cost_estimate=cost(4 * rows * width * (units + cols), 4 * rows * (width + units), COSTS["weight_grad"]),
        name="side_grads",
    )(*second, *back, branch, *contexts)


def first_kernel(count, *refs):
    packs, (weight_ref, frames_ref, terms_ref, sums_ref, bias_ref, pack_ref) = refs[:count], refs[count:]
    rows, width = frames_ref.shape
    cols = pack_ref.shape[1] // 3
    q_factor = HD ** (-0.5)
    pieces = row_pieces(rows, 256)
    offset = 0
    for ref in packs:
        wide = ref.shape[1] // 3
        for part in range(3):
            place = part * cols + offset
            pack_ref[:, place : place + wide] = ref[:, part * wide : (part + 1) * wide]
        offset += wide

    def begin(piece):
        take = slice(piece[0], piece[0] + piece[1])
        return dot_nt(pack_ref[take, :cols], weight_ref[:, :cols]) * q_factor + dot_nt(
            pack_ref[take, cols:], weight_ref[:, cols:]
        )

    totals = None
    current = begin(pieces[0])
    for number, piece in enumerate(pieces):
        coming = begin(pieces[number + 1]) if number + 1 < len(pieces) else None
        take = slice(piece[0], piece[0] + piece[1])
        terms_ref[take, :] = current.astype(jnp.bfloat16)
        normed, _ = normalise(frames_ref[take, :].astype(jnp.float32))
        sums = [
            jnp.sum(current * normed, axis=0, keepdims=True),
            jnp.sum(current, axis=0, keepdims=True),
            jnp.sum(pack_ref[take, :].astype(jnp.float32), axis=0, keepdims=True),
        ]
        totals = sums if totals is None else [a + b for a, b in zip(totals, sums)]
        current = coming
    sums_ref[0:1, :] = totals[0]
    sums_ref[1:2, :] = totals[1]
    bias_ref[...] = totals[2]


def first_back(packs, weights, frames):
    rows, width = frames.shape
    wide = sum(pack.shape[1] for pack in packs)
    return pl.pallas_call(
        functools.partial(first_kernel, len(packs)),
        out_shape=(
            jax.ShapeDtypeStruct((rows, width), jnp.bfloat16),
            jax.ShapeDtypeStruct((2, width), jnp.float32),
            jax.ShapeDtypeStruct((1, wide), jnp.float32),
        ),
        grid=(1,),
        in_specs=[whole(pack.shape) for pack in packs] + [whole((width, wide)), whole((rows, width))],
        out_specs=(whole((rows, width)), whole((2, width)), whole((1, wide))),
        scratch_shapes=[pltpu.VMEM((rows, wide), jnp.bfloat16)],
        compiler_params=kernel_params(),
        cost_estimate=cost(2 * rows * width * wide, 2 * (rows + width) * wide + 4 * rows * width, COSTS["first_back"]),
        name="first_back",
    )(*packs, weights, frames)


def frames_kernel(frames_ref, own_ref, far_ref, mgrad_ref, gain_ref, out_ref):
    normed, inverse = normalise(frames_ref[...].astype(jnp.float32))
    tilted = (own_ref[...].astype(jnp.float32) + far_ref[...].astype(jnp.float32)) * gain_ref[...]
    out_ref[...] = (
        mgrad_ref[...]
        + inverse
        * (
            tilted
            - jnp.mean(tilted, axis=-1, keepdims=True)
            - normed * jnp.mean(tilted * normed, axis=-1, keepdims=True)
        )
    ).astype(jnp.bfloat16)


def frames_back(frames, own, far, mgrad, gain):
    rows, width = frames.shape
    block = 376 if rows % 376 == 0 else rows
    spec = pl.BlockSpec((block, width), lambda i: (i, 0))
    return pl.pallas_call(
        frames_kernel,
        out_shape=jax.ShapeDtypeStruct((rows, width), jnp.bfloat16),
        grid=(rows // block,),
        in_specs=[spec] * 4 + [whole((1, width))],
        out_specs=spec,
        compiler_params=kernel_params(),
        cost_estimate=cost(20 * rows * width, 12 * rows * width, COSTS["frames_back"]),
        name="frames_back",
    )(frames, own, far, mgrad, gain)


def swap_tp(piece):
    return lax.ppermute(piece, "tp", [(0, 1), (1, 0)])


def tie(*values):
    return lax.optimization_barrier(values)


def gather_steps(vector, other, fsdp):
    index = lax.axis_index("fsdp")
    side = lax.axis_index("tp")
    held = jnp.where(side == 0, jnp.stack([vector, other]), jnp.stack([other, vector]))
    bit = 1
    while bit < fsdp:
        other = lax.ppermute(held, "fsdp", [(i, i ^ bit) for i in range(fsdp)])
        low = (index & bit) == 0
        held = jnp.where(low, jnp.concatenate([held, other]), jnp.concatenate([other, held]))
        bit *= 2
    return held


def halving_order(fsdp):
    return [bit for bit in (1, 2, 8, 4, 16, 32, 64, 128) if bit < fsdp]


def halve(held, bit, left, fsdp, last=False):
    index = lax.axis_index("fsdp")
    mine = (index // bit) % 2
    parts = held if isinstance(held, list) else [held]
    outer = 2 ** sorted(left, reverse=True).index(bit)
    views = [part.reshape(outer, 2, -1, part.shape[-1]) for part in parts]

    def chosen(which):
        return jnp.concatenate(
            [lax.dynamic_index_in_dim(view, which, 1, keepdims=False) for view in views], axis=-1
        )

    other = lax.ppermute(chosen(1 - mine), "fsdp", [(i, i ^ bit) for i in range(fsdp)])
    total = chosen(mine).astype(jnp.float32) + other.astype(jnp.float32)
    return (total if last else total.astype(jnp.bfloat16)).reshape(-1, total.shape[-1])


def per_device_pair(
    frames, out_grad, clip_lengths, clip_order, w_query, w_key, w_value, b_query, b_value,
    w_out, b_out, w_expand, b_expand, w_reduce, b_reduce,
    first_gain, first_shift, second_gain, second_shift, *, fsdp,
):
    side = lax.axis_index("tp")
    slot = lax.axis_index("fsdp")
    clip_count = clip_order.shape[0]
    every_clip = jnp.arange(clip_count, dtype=jnp.int32)
    clip_id = jnp.sum(jnp.where(every_clip == slot, clip_order, 0))
    length = jnp.sum(jnp.where(every_clip == clip_id, clip_lengths, 0))
    frames, out_grad = frames[0], out_grad[0]
    rows, width = frames.shape
    cols = w_query.shape[1]
    heads = cols // HD
    units = w_expand.shape[1]
    q_factor = HD ** (-0.5)
    scal_own = jnp.stack([length, side * rows]).astype(jnp.int32)
    scal_far = jnp.stack([length, (1 - side) * rows]).astype(jnp.int32)

    wide_six = [first_gain, first_shift, second_gain, second_shift, b_out, b_reduce]
    small_own = jnp.concatenate(wide_six + [b_query, b_value, b_expand])
    out_turned = w_out.T
    small_far, out_other = swap_tp(small_own), swap_tp(out_turned)
    pack_one = lax.all_gather(
        jnp.concatenate([w_query, w_key, w_value, out_turned, out_other], axis=1),
        "fsdp", axis=0, tiled=True,
    )
    pack_two = lax.all_gather(
        jnp.concatenate([w_expand, w_reduce.T], axis=1), "fsdp", axis=0, tiled=True
    )
    sent_frames, small_far, out_other = tie(frames, small_far, out_other)
    frames_far = swap_tp(sent_frames)
    sent_grads, frames_far = tie(out_grad, frames_far)
    grads_far = swap_tp(sent_grads)
    small = gather_steps(small_own, small_far, fsdp)
    lot = first_gain.shape[0]
    whole_six = small[:, : 6 * lot].astype(jnp.float32).reshape(2 * fsdp, 6, lot)
    whole_six = whole_six.transpose(1, 0, 2).reshape(6, 1, width)
    gain_one, shift_one, gain_two, shift_two, out_bias, reduce_bias = [whole_six[i] for i in range(6)]
    mine = lax.dynamic_index_in_dim(
        small[:, 6 * lot :].astype(jnp.float32).reshape(fsdp, 2, -1), side, axis=1, keepdims=False
    )
    part = b_query.shape[0]
    bias_q = mine[:, :part].reshape(1, -1)
    bias_v = mine[:, part : 2 * part].reshape(1, -1)
    bias_e = mine[:, 2 * part :].reshape(1, -1)

    first_own, q_own, k_own, v_own = project(
        scal_own, frames, gain_one, shift_one, pack_one, bias_q, bias_v, heads
    )
    first_far, q_far, k_far, v_far = project(
        scal_far, frames_far, gain_one, shift_one, pack_one, bias_q, bias_v, heads
    )
    context_send, log_far = attend_rows(q_far, k_own, k_far, v_own, v_far)
    context_send, q_own = tie(context_send, q_own)
    context_far = swap_tp(context_send.reshape(cols, -1))
    context_own, log_own = attend_rows(q_own, k_own, k_far, v_own, v_far)
    context_own = context_own.reshape(cols, -1)
    middle, second_own = merge_heads(
        context_own, context_far, pack_one, frames, out_bias, gain_two, shift_two
    )

    second_far = swap_tp(second_own)
    hid_far, back_far, bsum_far, out_send, terms_send = feed(
        second_far, grads_far, pack_two, bias_e, units
    )
    terms_send, second_own = tie(terms_send, second_own)
    terms_far = swap_tp(terms_send)
    back_own, bsum_own, out_own, terms_own, d_reduce = feed(
        second_own, out_grad, pack_two, bias_e, units, (grads_far, hid_far)
    )
    g_reduce = lax.psum_scatter(d_reduce, "fsdp", scatter_dimension=0, tiled=True)
    mgrad, branch, up_own, up_send, sums_two = branch_back(
        terms_own, terms_far, middle, out_grad, gain_two, pack_one, cols
    )
    up_send, second_own = tie(up_send, second_own)
    up_far = swap_tp(up_send)
    d_side = side_grads(
        (second_own, second_far), (back_own, back_far), branch, (context_own, context_far)
    )

    turned = (heads, HD, lanes(rows))
    up_far, out_send, d_side = tie(up_far, out_send, d_side)
    out_far = swap_tp(out_send)
    ups = (up_own.reshape(turned), up_far.reshape(turned))
    steps = halving_order(fsdp)
    firsts = (first_own, first_far)

    def back(q_first, start, count):
        return attend_back_rows(
            (q_first, q_far), (k_own, k_far), (v_own, v_far), ups, (log_own, log_far), start, count
        )

    many = (heads + 1) // 2
    own_a, far_a = back(q_own, 0, many)
    own_a, d_side = tie(own_a, d_side)
    g_side = lax.psum_scatter(d_side, "fsdp", scatter_dimension=0, tiled=True)
    d_heads = head_grad(firsts, [own_a], [far_a])
    held_a = halve(d_heads, steps[0], steps, fsdp)
    held_a, q_own = tie(held_a, q_own)
    own_b, far_b = back(q_own, many, heads - many)
    far_b, out_far = tie(far_b, out_far)
    held_a = halve(held_a, steps[1], steps[1:], fsdp)
    held_a, far_b = tie(held_a, far_b)
    first_send, sums_far, bias_far = first_back([far_a, far_b], pack_one, frames_far)
    first_send, far_b = tie(first_send, far_b)
    first_recv = swap_tp(first_send)
    held_b = head_grad(firsts, [own_b], [far_b])
    held_b, own_b = tie(held_b, own_b)
    first_keep, sums_own, bias_own = first_back([own_a, own_b], pack_one, frames)
    held_a = halve(held_a, steps[2], steps[2:], fsdp, len(steps) == 3)
    sums_one = sums_own + sums_far
    bias_sum = bias_own + bias_far
    wide_sums = jnp.concatenate([sums_one, sums_two])
    wide_sums = wide_sums.reshape(6, fsdp, 2, lot).transpose(1, 2, 0, 3).reshape(fsdp, 12 * lot)
    tall = jnp.concatenate(
        [
            wide_sums,
            (bias_sum[:, :cols] * q_factor).reshape(fsdp, -1),
            bias_sum[:, 2 * cols :].reshape(fsdp, -1),
            (bsum_own + bsum_far).reshape(fsdp, -1),
        ],
        axis=1,
    )
    wide = held_b.shape[1]
    extra = -(-tall.shape[1] // (8 * wide)) * 8
    tall = jnp.pad(tall, ((0, 0), (0, extra * wide - tall.shape[1]))).astype(jnp.bfloat16)
    lots = width // fsdp
    held_b = jnp.concatenate(
        [held_b.reshape(fsdp, lots, wide), tall.reshape(fsdp, extra, wide)], axis=1
    ).reshape(-1, wide)
    held_b = halve(held_b, steps[0], steps, fsdp)
    held_b = halve(held_b, steps[1], steps[1:], fsdp)
    out_frames = (
        middle + out_own.astype(jnp.float32) + out_far.astype(jnp.float32) + reduce_bias
    ).astype(jnp.bfloat16)
    for place in range(2, len(steps)):
        last = place + 1 == len(steps)
        if place > 2:
            held_a, held_b = tie(held_a, held_b)
            held_a = halve(held_a, steps[place], steps[place:], fsdp, last)
        if last:
            held_b, first_keep, out_frames = tie(held_b, first_keep, out_frames)
            frames_grad = frames_back(frames, first_keep, first_recv, mgrad, gain_one)
            held_b, frames_grad, g_side = tie(held_b, frames_grad, g_side)
        held_b = halve(held_b, steps[place], steps[place:], fsdp, last)
    held_b, small_sum = held_b[:lots], held_b[lots:].reshape(-1)
    g_expand, g_out = g_side[:, :units], g_side[:, units:]
    some = many * HD

    def joined(kind):
        rest = cols - some
        return jnp.concatenate(
            [held_a[:, kind * some : (kind + 1) * some], held_b[:, kind * rest : (kind + 1) * rest]], axis=1
        )

    g_query, g_key, g_value = joined(0), joined(1), joined(2)

    six = small_sum[: 12 * lot].reshape(2, 6 * lot)
    keep = lax.dynamic_index_in_dim(six, side, 0, keepdims=False)
    send = lax.dynamic_index_in_dim(six, 1 - side, 0, keepdims=False)
    six = (keep + swap_tp(send)).reshape(6, lot)
    rest = small_sum[12 * lot :]
    g_bq, g_bv = rest[:part], rest[part : 2 * part]
    g_be = rest[2 * part : 2 * part + b_expand.shape[0]]
    g_out_sum = g_out[:, :cols].astype(jnp.float32) + swap_tp(g_out[:, cols:]).astype(jnp.float32)
    return (
        out_frames[None],
        frames_grad[None],
        g_query,
        g_key,
        g_value,
        g_bq,
        g_bv,
        g_out_sum.T,
        six[4],
        g_expand.astype(jnp.float32),
        g_be,
        g_reduce.T.astype(jnp.float32),
        six[5],
        six[0],
        six[1],
        six[2],
        six[3],
    )


def solution(mesh):
    fsdp = mesh.shape["fsdp"]
    if mesh.shape["tp"] == 2 and fsdp & (fsdp - 1) == 0:

        def body(*args):
            return per_device_pair(*args, fsdp=fsdp) if args[0].shape[0] == 1 else per_device(*args)
    else:
        body = per_device
    return jax.shard_map(
        body,
        mesh=mesh,
        in_specs=(
            P("fsdp", "tp", None),
            P("fsdp", "tp", None),
            P(),
            P(),
            P("fsdp", "tp"),
            P("fsdp", "tp"),
            P("fsdp", "tp"),
            P(("tp", "fsdp")),
            P(("tp", "fsdp")),
            P("tp", "fsdp"),
            P(("fsdp", "tp")),
            P("fsdp", "tp"),
            P(("tp", "fsdp")),
            P("tp", "fsdp"),
            P(("fsdp", "tp")),
            P(("fsdp", "tp")),
            P(("fsdp", "tp")),
            P(("fsdp", "tp")),
            P(("fsdp", "tp")),
        ),
        out_specs=(
            P("fsdp", "tp", None),
            P("fsdp", "tp", None),
            P("fsdp", "tp"),
            P("fsdp", "tp"),
            P("fsdp", "tp"),
            P(("tp", "fsdp")),
            P(("tp", "fsdp")),
            P("tp", "fsdp"),
            P(("fsdp", "tp")),
            P("fsdp", "tp"),
            P(("tp", "fsdp")),
            P("tp", "fsdp"),
            P(("fsdp", "tp")),
            P(("fsdp", "tp")),
            P(("fsdp", "tp")),
            P(("fsdp", "tp")),
            P(("fsdp", "tp")),
        ),
        check_vma=False,
    )
```

```python
import functools

import jax
import jax.numpy as jnp
from jax import lax
from jax.experimental import pallas as pl
from jax.experimental.pallas import tpu as pltpu
from jax.sharding import PartitionSpec as P

HD = 80


EPSILON = 1e-05
MASKED = -1000000000.0
HIDDEN = -1e30


def layer_norm(features, norm_gain, norm_shift):
    row_mean = jnp.mean(features, axis=-1, keepdims=True)
    centred = features - row_mean
    row_var = jnp.mean(centred * centred, axis=-1, keepdims=True)
    inverse = lax.rsqrt(row_var + EPSILON)
    normed = centred * inverse
    return (normed * norm_gain + norm_shift, normed, inverse)


def norm_back(upstream, normed, inverse, norm_gain):
    tilted = upstream * norm_gain
    return inverse * (
        tilted
        - jnp.mean(tilted, axis=-1, keepdims=True)
        - normed * jnp.mean(tilted * normed, axis=-1, keepdims=True)
    )


def gelu_exact(inputs):
    return jax.nn.gelu(inputs, approximate=False)


def masked_scores(queries, key_rows, length):
    scores = jnp.einsum("qhe,khe->hqk", queries, key_rows, preferred_element_type=jnp.float32)
    allowed = jnp.arange(scores.shape[-1]) < length
    return jnp.where(allowed[None, None, :], scores, MASKED)


def attend(inputs):
    queries, key_rows, value_rows, length = inputs
    scores = masked_scores(queries, key_rows, length)
    row_top = jnp.max(scores, axis=-1, keepdims=True)
    raised = jnp.exp(scores - row_top)
    row_sum = jnp.sum(raised, axis=-1, keepdims=True)
    weights = (raised / row_sum).astype(jnp.bfloat16)
    context = jnp.einsum("hqk,khe->qhe", weights, value_rows, preferred_element_type=jnp.float32)
    return (context.astype(jnp.bfloat16), row_top[..., 0] + jnp.log(row_sum[..., 0]))


def attend_back(inputs):
    queries, key_rows, value_rows, length, log_total, context_grad = inputs
    scores = masked_scores(queries, key_rows, length)
    probs = jnp.exp(scores - log_total[..., None])
    weights = probs.astype(jnp.bfloat16)
    value_grad = jnp.einsum(
        "hqk,qhe->khe", weights, context_grad, preferred_element_type=jnp.float32
    )
    weight_grad = jnp.einsum(
        "qhe,khe->hqk", context_grad, value_rows, preferred_element_type=jnp.float32
    )
    row_inner = jnp.sum(weight_grad * probs, axis=-1, keepdims=True)
    score_grad = (probs * (weight_grad - row_inner)).astype(jnp.bfloat16)
    query_grad = jnp.einsum(
        "hqk,khe->qhe", score_grad, key_rows, preferred_element_type=jnp.float32
    )
    key_grad = jnp.einsum("hqk,qhe->khe", score_grad, queries, preferred_element_type=jnp.float32)
    return (
        query_grad.astype(jnp.bfloat16),
        key_grad.astype(jnp.bfloat16),
        value_grad.astype(jnp.bfloat16),
    )


def gather_inward(w_query, w_key, w_value, b_query, b_value, w_expand, b_expand):
    return (
        lax.all_gather(w_query, "fsdp", axis=0, tiled=True),
        lax.all_gather(w_key, "fsdp", axis=0, tiled=True),
        lax.all_gather(w_value, "fsdp", axis=0, tiled=True),
        lax.all_gather(b_query, "fsdp", axis=0, tiled=True),
        lax.all_gather(b_value, "fsdp", axis=0, tiled=True),
        lax.all_gather(w_expand, "fsdp", axis=0, tiled=True),
        lax.all_gather(b_expand, "fsdp", axis=0, tiled=True),
    )


def gather_outward(w_out, w_reduce):
    return (
        lax.all_gather(w_out, "fsdp", axis=1, tiled=True),
        lax.all_gather(w_reduce, "fsdp", axis=1, tiled=True),
    )


def per_device(
    frames,
    out_grad,
    clip_lengths,
    clip_order,
    w_query,
    w_key,
    w_value,
    b_query,
    b_value,
    w_out,
    b_out,
    w_expand,
    b_expand,
    w_reduce,
    b_reduce,
    first_gain,
    first_shift,
    second_gain,
    second_shift,
):
    per_group = frames.shape[0]
    clip_count = clip_order.shape[0]
    slot_ids = lax.axis_index("fsdp") * per_group + jnp.arange(per_group, dtype=jnp.int32)
    every_clip = jnp.arange(clip_count, dtype=jnp.int32)
    clip_ids = jnp.sum(
        jnp.where(every_clip[None, :] == slot_ids[:, None], clip_order[None, :], 0), axis=1
    )
    lengths = jnp.sum(
        jnp.where(every_clip[None, :] == clip_ids[:, None], clip_lengths[None, :], 0), axis=1
    )
    norm_params = (
        lax.all_gather(first_gain, ("fsdp", "tp"), axis=0, tiled=True),
        lax.all_gather(first_shift, ("fsdp", "tp"), axis=0, tiled=True),
        lax.all_gather(second_gain, ("fsdp", "tp"), axis=0, tiled=True),
        lax.all_gather(second_shift, ("fsdp", "tp"), axis=0, tiled=True),
        lax.all_gather(b_out, ("fsdp", "tp"), axis=0, tiled=True),
        lax.all_gather(b_reduce, ("fsdp", "tp"), axis=0, tiled=True),
    )
    gain_one, shift_one, gain_two, shift_two, out_bias, reduce_bias = [
        tensor.astype(jnp.float32) for tensor in norm_params
    ]
    wq_all, wk_all, wv_all, bq_all, bv_all, we_all, be_all = gather_inward(
        w_query, w_key, w_value, b_query, b_value, w_expand, b_expand
    )
    wo_all, wr_all = gather_outward(w_out, w_reduce)
    q_factor = HD ** (-0.5)
    frames_wide = frames.astype(jnp.float32)
    norm_one, normed_one, inverse_one = layer_norm(frames_wide, gain_one, shift_one)
    first_rows = lax.all_gather(norm_one.astype(jnp.bfloat16), "tp", axis=1, tiled=True)
    seq_len = first_rows.shape[1]
    queries = (
        (
            jnp.einsum("csd,de->cse", first_rows, wq_all, preferred_element_type=jnp.float32)
            + bq_all.astype(jnp.float32)
        )
        * q_factor
    ).astype(jnp.bfloat16)
    keys = jnp.einsum("csd,de->cse", first_rows, wk_all, preferred_element_type=jnp.float32).astype(
        jnp.bfloat16
    )
    values = (
        jnp.einsum("csd,de->cse", first_rows, wv_all, preferred_element_type=jnp.float32)
        + bv_all.astype(jnp.float32)
    ).astype(jnp.bfloat16)
    head_shape = (per_group, seq_len, -1, HD)
    query_heads = queries.reshape(head_shape)
    key_heads = keys.reshape(head_shape)
    value_heads = values.reshape(head_shape)
    context, log_total = lax.map(attend, (query_heads, key_heads, value_heads, lengths))
    context_flat = context.reshape(per_group, seq_len, -1)
    attn_terms = jnp.einsum("cse,ed->csd", context_flat, wo_all, preferred_element_type=jnp.float32)
    attn_part = lax.psum_scatter(
        attn_terms.astype(jnp.bfloat16), "tp", scatter_dimension=1, tiled=True
    ).astype(jnp.float32)
    middle = frames_wide + attn_part + out_bias
    norm_two, normed_two, inverse_two = layer_norm(middle, gain_two, shift_two)
    second_rows = lax.all_gather(norm_two.astype(jnp.bfloat16), "tp", axis=1, tiled=True)
    expanded = jnp.einsum(
        "csd,df->csf", second_rows, we_all, preferred_element_type=jnp.float32
    ) + be_all.astype(jnp.float32)
    activated, gelu_pull = jax.vjp(gelu_exact, expanded)
    hidden = activated.astype(jnp.bfloat16)
    mlp_terms = jnp.einsum("csf,fd->csd", hidden, wr_all, preferred_element_type=jnp.float32)
    out_frames = (
        middle
        + lax.psum_scatter(
            mlp_terms.astype(jnp.bfloat16), "tp", scatter_dimension=1, tiled=True
        ).astype(jnp.float32)
        + reduce_bias
    ).astype(jnp.bfloat16)
    wq_all, wk_all, wv_all, bq_all, bv_all, we_all, be_all = gather_inward(
        w_query, w_key, w_value, b_query, b_value, w_expand, b_expand
    )
    wo_all, wr_all = gather_outward(w_out, w_reduce)
    grad_wide = out_grad.astype(jnp.float32)
    grad_rows = lax.all_gather(out_grad, "tp", axis=1, tiled=True)
    w_reduce_grad = jnp.einsum("csf,csd->fd", hidden, grad_rows, preferred_element_type=jnp.float32)
    hidden_grad = jnp.einsum("csd,fd->csf", grad_rows, wr_all, preferred_element_type=jnp.float32)
    expanded_grad = gelu_pull(hidden_grad)[0].astype(jnp.bfloat16)
    b_expand_grad = jnp.sum(expanded_grad.astype(jnp.float32), axis=(0, 1))
    w_expand_grad = jnp.einsum(
        "csd,csf->df", second_rows, expanded_grad, preferred_element_type=jnp.float32
    )
    second_terms = jnp.einsum(
        "csf,df->csd", expanded_grad, we_all, preferred_element_type=jnp.float32
    )
    second_grad = lax.psum_scatter(
        second_terms.astype(jnp.bfloat16), "tp", scatter_dimension=1, tiled=True
    ).astype(jnp.float32)
    second_gain_grad = jnp.sum(second_grad * normed_two, axis=(0, 1))
    second_shift_grad = jnp.sum(second_grad, axis=(0, 1))
    middle_grad = grad_wide + norm_back(second_grad, normed_two, inverse_two, gain_two)
    branch_grad = middle_grad.astype(jnp.bfloat16)
    b_out_grad = jnp.sum(branch_grad.astype(jnp.float32), axis=(0, 1))
    b_reduce_grad = jnp.sum(grad_wide, axis=(0, 1))
    branch_rows = lax.all_gather(branch_grad, "tp", axis=1, tiled=True)
    w_out_grad = jnp.einsum(
        "cse,csd->ed", context_flat, branch_rows, preferred_element_type=jnp.float32
    )
    context_grad = jnp.einsum(
        "csd,ed->cse", branch_rows, wo_all, preferred_element_type=jnp.float32
    ).astype(jnp.bfloat16)
    query_grad, key_grad, value_grad = lax.map(
        attend_back,
        (query_heads, key_heads, value_heads, lengths, log_total, context_grad.reshape(head_shape)),
    )
    query_grad = query_grad.reshape(per_group, seq_len, -1)
    key_grad = key_grad.reshape(per_group, seq_len, -1)
    value_grad = value_grad.reshape(per_group, seq_len, -1)
    w_query_grad = (
        jnp.einsum("csd,cse->de", first_rows, query_grad, preferred_element_type=jnp.float32)
        * q_factor
    )
    b_query_grad = jnp.sum(query_grad.astype(jnp.float32), axis=(0, 1)) * q_factor
    w_key_grad = jnp.einsum("csd,cse->de", first_rows, key_grad, preferred_element_type=jnp.float32)
    w_value_grad = jnp.einsum(
        "csd,cse->de", first_rows, value_grad, preferred_element_type=jnp.float32
    )
    b_value_grad = jnp.sum(value_grad.astype(jnp.float32), axis=(0, 1))
    first_terms = (
        jnp.einsum("cse,de->csd", query_grad, wq_all, preferred_element_type=jnp.float32) * q_factor
        + jnp.einsum("cse,de->csd", key_grad, wk_all, preferred_element_type=jnp.float32)
        + jnp.einsum("cse,de->csd", value_grad, wv_all, preferred_element_type=jnp.float32)
    )
    first_grad = lax.psum_scatter(
        first_terms.astype(jnp.bfloat16), "tp", scatter_dimension=1, tiled=True
    ).astype(jnp.float32)
    first_gain_grad = jnp.sum(first_grad * normed_one, axis=(0, 1))
    first_shift_grad = jnp.sum(first_grad, axis=(0, 1))
    frames_grad = (middle_grad + norm_back(first_grad, normed_one, inverse_one, gain_one)).astype(
        jnp.bfloat16
    )
    inward_grads = (
        lax.psum_scatter(
            w_query_grad.astype(jnp.bfloat16), "fsdp", scatter_dimension=0, tiled=True
        ).astype(jnp.float32),
        lax.psum_scatter(
            w_key_grad.astype(jnp.bfloat16), "fsdp", scatter_dimension=0, tiled=True
        ).astype(jnp.float32),
        lax.psum_scatter(
            w_value_grad.astype(jnp.bfloat16), "fsdp", scatter_dimension=0, tiled=True
        ).astype(jnp.float32),
        lax.psum_scatter(
            b_query_grad.astype(jnp.bfloat16), "fsdp", scatter_dimension=0, tiled=True
        ).astype(jnp.float32),
        lax.psum_scatter(
            b_value_grad.astype(jnp.bfloat16), "fsdp", scatter_dimension=0, tiled=True
        ).astype(jnp.float32),
        lax.psum_scatter(
            w_expand_grad.astype(jnp.bfloat16), "fsdp", scatter_dimension=0, tiled=True
        ).astype(jnp.float32),
        lax.psum_scatter(
            b_expand_grad.astype(jnp.bfloat16), "fsdp", scatter_dimension=0, tiled=True
        ).astype(jnp.float32),
    )
    outward_grads = (
        lax.psum_scatter(
            w_out_grad.astype(jnp.bfloat16), "fsdp", scatter_dimension=1, tiled=True
        ).astype(jnp.float32),
        lax.psum_scatter(
            w_reduce_grad.astype(jnp.bfloat16), "fsdp", scatter_dimension=1, tiled=True
        ).astype(jnp.float32),
    )
    small_grads = (
        lax.psum_scatter(first_gain_grad, ("fsdp", "tp"), scatter_dimension=0, tiled=True),
        lax.psum_scatter(first_shift_grad, ("fsdp", "tp"), scatter_dimension=0, tiled=True),
        lax.psum_scatter(second_gain_grad, ("fsdp", "tp"), scatter_dimension=0, tiled=True),
        lax.psum_scatter(second_shift_grad, ("fsdp", "tp"), scatter_dimension=0, tiled=True),
        lax.psum_scatter(b_out_grad, ("fsdp", "tp"), scatter_dimension=0, tiled=True),
        lax.psum_scatter(b_reduce_grad, ("fsdp", "tp"), scatter_dimension=0, tiled=True),
    )
    return (
        out_frames,
        frames_grad,
        inward_grads[0],
        inward_grads[1],
        inward_grads[2],
        inward_grads[3],
        inward_grads[4],
        outward_grads[0],
        small_grads[4],
        inward_grads[5],
        inward_grads[6],
        outward_grads[1],
        small_grads[5],
        small_grads[0],
        small_grads[1],
        small_grads[2],
        small_grads[3],
    )


VMEM_LIMIT = 60 << 20
PAD = 128
COSTS = {'project': 3.0, 'attend': 3.0, 'merge_heads': 3.0, 'feed': 3.0, 'weight_grad': 3.0, 'head_grad': 0.02, 'branch_back': 3.0, 'out_weight_grad': 0.02, 'first_back': 0.02, 'frames_back': 0.02, 'attend_back': (8.0, 0.02)}


def kernel_params():
    return pltpu.CompilerParams(vmem_limit_bytes=VMEM_LIMIT)


def cost(flops, moved, scale):
    return pl.CostEstimate(flops=int(scale * flops), bytes_accessed=int(min(1.0, scale) * moved), transcendentals=0)


def lanes(rows):
    return -(-rows // PAD) * PAD


def row_pieces(rows, size):
    return [(start, min(size, rows - start)) for start in range(0, rows, size)]


def whole(shape, fixed=None):
    index = fixed if fixed is not None else (0,) * len(shape)
    return pl.BlockSpec(shape, lambda *_: index)


def normalise(rows):
    row_mean = jnp.mean(rows, axis=-1, keepdims=True)
    centred = rows - row_mean
    inverse = lax.rsqrt(jnp.mean(centred * centred, axis=-1, keepdims=True) + EPSILON)
    return centred * inverse, inverse


def dot_nn(left, right):
    return jnp.dot(left, right, preferred_element_type=jnp.float32)


def dot_nt(left, right):
    return lax.dot_general(left, right, (((1,), (1,)), ((), ())), preferred_element_type=jnp.float32)


def dot_tn(left, right):
    return lax.dot_general(left, right, (((0,), (0,)), ((), ())), preferred_element_type=jnp.float32)


def project_kernel(
    heads, scal_ref, frames_ref, gain_ref, shift_ref, weight_ref, bq_ref, bv_ref,
    first_ref, q_ref, k_ref, v_ref,
):
    rows, width = frames_ref.shape
    cols = heads * HD
    length, start = scal_ref[0], scal_ref[1]
    q_factor = HD ** (-0.5)
    pieces = row_pieces(rows, 256)

    def norm(piece):
        normed, _ = normalise(frames_ref[piece[0] : piece[0] + piece[1], :].astype(jnp.float32))
        first = (normed * gain_ref[...] + shift_ref[...]).astype(jnp.bfloat16)
        first_ref[piece[0] : piece[0] + piece[1], :] = first
        return first

    def split(block, offset, filler, lane):
        if offset + PAD <= block.shape[1]:
            part = block[:, offset : offset + PAD]
        else:
            back = block.shape[1] - PAD
            part = pltpu.roll(block[:, back:], PAD - (offset - back), 1)
        return jnp.where(lane < HD, part, filler).astype(jnp.bfloat16)

    def finish(piece, out):
        lane = lax.broadcasted_iota(jnp.int32, (piece[1], PAD), 1)
        position = lax.broadcasted_iota(jnp.int32, (piece[1], PAD), 0) + (start + piece[0])
        one = jnp.where(lane == HD, 1.0, 0.0)
        hide = jnp.where((lane == HD) & (position >= length), HIDDEN, 0.0)
        queries = (out[:, :cols] + bq_ref[...]) * q_factor
        keys = out[:, cols : 2 * cols]
        values = out[:, 2 * cols :] + bv_ref[...]
        for head in range(heads):
            where = (head, slice(piece[0], piece[0] + piece[1]), slice(None))
            q_ref[where] = split(queries, head * HD, one, lane)
            k_ref[where] = split(keys, head * HD, hide, lane)
            v_ref[where] = split(values, head * HD, 0.0, lane)

    first = norm(pieces[0])
    for number, piece in enumerate(pieces):
        out = dot_nn(first, weight_ref[...])
        if number + 1 < len(pieces):
            first = norm(pieces[number + 1])
        finish(piece, out)


def project(scalars, frames, gain, shift, weights, bias_q, bias_v, heads):
    rows, width = frames.shape
    cols = heads * HD
    head_out = jax.ShapeDtypeStruct((heads, rows, PAD), jnp.bfloat16)
    return pl.pallas_call(
        functools.partial(project_kernel, heads),
        out_shape=(jax.ShapeDtypeStruct((rows, width), jnp.bfloat16), head_out, head_out, head_out),
        grid_spec=pltpu.PrefetchScalarGridSpec(
            num_scalar_prefetch=1,
            grid=(1,),
            in_specs=[
                whole((rows, width)), whole((1, width)), whole((1, width)),
                whole((width, 3 * cols)), whole((1, cols)), whole((1, cols)),
            ],
            out_specs=(whole((rows, width)),) + (whole((heads, rows, PAD)),) * 3,
        ),
        compiler_params=kernel_params(),
        cost_estimate=cost(2 * rows * width * 3 * cols, 4 * rows * width + 6 * width * cols, COSTS["project"]),
        name="project",
    )(scalars, frames, gain, shift, weights, bias_q, bias_v)


def attend_kernel(q_ref, ko_ref, kt_ref, vo_ref, vt_ref, out_ref, log_ref):
    per_step, rows, _ = q_ref.shape
    half = -(-rows // 256) * 128
    pieces = [(head, start, size) for head in range(per_step) for start, size in row_pieces(rows, half)]
    keys = [jnp.concatenate([ko_ref[h], kt_ref[h]], axis=0) for h in range(per_step)]
    values = [jnp.concatenate([vo_ref[h], vt_ref[h]], axis=0).T[:HD] for h in range(per_step)]

    def scores(piece):
        head, start, size = piece
        return dot_nt(keys[head], q_ref[head, start : start + size, :])

    def finish(piece, score):
        head, start, size = piece
        top = jnp.max(score, axis=0, keepdims=True)
        raised = jnp.exp(score - top)
        total = jnp.sum(raised, axis=0, keepdims=True)
        context = dot_nn(values[head], raised.astype(jnp.bfloat16)) / total
        out_ref[head, :, start : start + size] = context.astype(jnp.bfloat16)
        log_ref[head, :, start : start + size] = top + jnp.log(total)

    if out_ref.shape[2] > rows:
        out_ref[:, :, rows:] = jnp.zeros((per_step, HD, out_ref.shape[2] - rows), jnp.bfloat16)
    current = scores(pieces[0])
    for number, piece in enumerate(pieces):
        coming = scores(pieces[number + 1]) if number + 1 < len(pieces) else None
        finish(piece, current)
        current = coming


def attend_rows(queries, keys_own, keys_far, values_own, values_far):
    heads, rows, _ = queries.shape
    per_step = 4 if heads % 4 == 0 else 1
    spec = pl.BlockSpec((per_step, rows, PAD), lambda h: (h, 0, 0))
    return pl.pallas_call(
        attend_kernel,
        out_shape=(
            jax.ShapeDtypeStruct((heads, HD, lanes(rows)), jnp.bfloat16),
            jax.ShapeDtypeStruct((heads, 1, rows), jnp.float32),
        ),
        grid=(heads // per_step,),
        in_specs=[spec] * 5,
        out_specs=(
            pl.BlockSpec((per_step, HD, lanes(rows)), lambda h: (h, 0, 0)),
            pl.BlockSpec((per_step, 1, rows), lambda h: (h, 0, 0)),
        ),
        compiler_params=kernel_params(),
        cost_estimate=cost(heads * 2 * rows * 2 * rows * 2 * 400, heads * rows * PAD * 12, COSTS["attend"]),
        name="attend",
    )(queries, keys_own, keys_far, values_own, values_far)


def attend_back_kernel(
    qo_ref, qt_ref, ko_ref, kt_ref, vo_ref, vt_ref, go_ref, gt_ref, lo_ref, lt_ref,
    own_ref, far_ref, dq_ref,
):
    rows = qo_ref.shape[1]
    cols = own_ref.shape[1] // 3
    keys = jnp.concatenate([ko_ref[0], kt_ref[0]], axis=0)
    values = jnp.concatenate([vo_ref[0], vt_ref[0]], axis=0)
    keys_turned = keys.T[:HD]
    pieces = [(side, start, size) for side in range(2) for start, size in row_pieces(rows, 256)]
    sides = ((qo_ref, go_ref, lo_ref), (qt_ref, gt_ref, lt_ref))

    def query(piece):
        side, start, size = piece
        return sides[side][0][0, start : start + size, :]

    def upstream(piece):
        side, start, size = piece
        return sides[side][1][0, :, start : start + size]

    def begin(piece):
        score = dot_nt(keys, query(piece))
        padded = jnp.concatenate(
            [upstream(piece), jnp.zeros((PAD - HD, piece[2]), jnp.bfloat16)], axis=0
        )
        return score, dot_nn(values, padded)

    def middle(piece, score, weight_grad):
        side, start, size = piece
        probs = jnp.exp(score - sides[side][2][0, :, start : start + size])
        tilted = probs * weight_grad
        inner = jnp.sum(tilted, axis=0, keepdims=True)
        return probs.astype(jnp.bfloat16), (tilted - probs * inner).astype(jnp.bfloat16)

    total_k = total_v = None
    current = begin(pieces[0])
    for number, piece in enumerate(pieces):
        coming = begin(pieces[number + 1]) if number + 1 < len(pieces) else None
        weights, score_grad = middle(piece, *current)
        value_part = dot_nt(weights, upstream(piece))
        key_part = dot_nn(score_grad, query(piece))
        query_grad = dot_nn(keys_turned, score_grad)
        side, start, size = piece
        dq_ref[side * rows + start : side * rows + start + size, :] = query_grad.T.astype(jnp.bfloat16)
        total_v = value_part if total_v is None else total_v + value_part
        total_k = key_part if total_k is None else total_k + key_part
        current = coming
    key_grad = total_k[:, :HD].astype(jnp.bfloat16)
    value_grad = total_v.astype(jnp.bfloat16)
    for head in range(cols // HD):

        @pl.when(pl.program_id(0) == head)
        def _(head=head):
            for part, grad in enumerate((dq_ref[...], key_grad, value_grad)):
                take = slice(part * cols + head * HD, part * cols + (head + 1) * HD)
                own_ref[:, take] = grad[:rows]
                far_ref[:, take] = grad[rows:]


def attend_back_rows(queries, keys, values, upstream, logs, start, heads):
    rows = queries[0].shape[1]
    spec = pl.BlockSpec((1, rows, PAD), lambda h: (h + start, 0, 0))
    turned = pl.BlockSpec((1, HD, lanes(rows)), lambda h: (h + start, 0, 0))
    line = pl.BlockSpec((1, 1, rows), lambda h: (h + start, 0, 0))
    packed = (rows, 3 * heads * HD)
    return pl.pallas_call(
        attend_back_kernel,
        out_shape=(jax.ShapeDtypeStruct(packed, jnp.bfloat16),) * 2,
        grid=(heads,),
        in_specs=[spec] * 6 + [turned] * 2 + [line] * 2,
        out_specs=(whole(packed),) * 2,
        scratch_shapes=[pltpu.VMEM((2 * rows, HD), jnp.bfloat16)],
        compiler_params=kernel_params(),
        cost_estimate=cost(heads * 4 * rows * rows * 2 * 900, heads * rows * PAD * 24, COSTS["attend_back"][start > 0]),
        name="attend_back",
    )(*queries, *keys, *values, *upstream, *logs)


def merge_kernel(
    co_ref, ct_ref, wo_ref, wt_ref, frames_ref, bias_ref, gain_ref, shift_ref, middle_ref, second_ref,
):
    rows = frames_ref.shape[0]
    own, far = co_ref[:, :rows].T, ct_ref[:, :rows].T
    pieces = row_pieces(rows, 256)

    def branch(piece):
        take = slice(piece[0], piece[0] + piece[1])
        return dot_nt(own[take], wo_ref[...]) + dot_nt(far[take], wt_ref[...])

    def finish(piece, part):
        take = slice(piece[0], piece[0] + piece[1])
        middle = frames_ref[take, :].astype(jnp.float32) + part + bias_ref[...]
        middle_ref[take, :] = middle
        normed, _ = normalise(middle)
        second_ref[take, :] = (normed * gain_ref[...] + shift_ref[...]).astype(jnp.bfloat16)

    current = branch(pieces[0])
    for number, piece in enumerate(pieces):
        coming = branch(pieces[number + 1]) if number + 1 < len(pieces) else None
        finish(piece, current)
        current = coming


def merge_heads(context_own, context_far, pack, frames, bias, gain, shift):
    rows, width = frames.shape
    cols = context_own.shape[0]
    return pl.pallas_call(
        merge_kernel,
        out_shape=(
            jax.ShapeDtypeStruct((rows, width), jnp.float32),
            jax.ShapeDtypeStruct((rows, width), jnp.bfloat16),
        ),
        grid=(1,),
        in_specs=[
            whole((cols, lanes(rows))), whole((cols, lanes(rows))), whole((width, cols), (0, 3)),
            whole((width, cols), (0, 4)), whole((rows, width)), whole((1, width)), whole((1, width)), whole((1, width)),
        ],
        out_specs=(whole((rows, width)),) * 2,
        compiler_params=kernel_params(),
        cost_estimate=cost(4 * rows * width * cols, 10 * rows * width + 4 * width * cols, COSTS["merge_heads"]),
        name="merge_heads",
    )(context_own, context_far, pack, pack, frames, bias, gain, shift)


def feed_kernel(
    grads_too, second_ref, grad_ref, expand_ref, reduce_ref, bias_ref, *refs,
):
    if grads_too:
        far_ref, hid_ref, back_ref, bsum_ref, out_ref, terms_ref, dred_ref, out_acc, terms_acc, hidden_ref = refs
    else:
        hidden_ref, back_ref, bsum_ref, out_ref, terms_ref, out_acc, terms_acc = refs
    step = pl.program_id(0)
    rows = second_ref.shape[0]
    pieces = row_pieces(rows, 376 if rows % 376 == 0 else 256)
    expand, reduce = expand_ref[...], reduce_ref[...]

    def begin(piece):
        take = slice(piece[0], piece[0] + piece[1])
        return dot_nn(second_ref[take, :], expand), dot_nn(grad_ref[take, :], reduce)

    @pl.when(step == 0)
    def _():
        out_acc[...] = jnp.zeros_like(out_acc)
        terms_acc[...] = jnp.zeros_like(terms_acc)

    sums = None
    current = begin(pieces[0])
    for number, piece in enumerate(pieces):
        coming = begin(pieces[number + 1]) if number + 1 < len(pieces) else None
        take = slice(piece[0], piece[0] + piece[1])
        raw, upstream = current
        raw = raw + bias_ref[...]
        below = 0.5 + 0.5 * lax.erf(raw * 0.7071067811865476)
        density = jnp.exp(raw * raw * -0.5) * 0.3989422804014327
        hidden = (raw * below).astype(jnp.bfloat16)
        back = (upstream * (below + raw * density)).astype(jnp.bfloat16)
        hidden_ref[take, :] = hidden
        back_ref[take, :] = back
        part = jnp.sum(back.astype(jnp.float32), axis=0, keepdims=True)
        sums = part if sums is None else sums + part
        terms_acc[take, :] += dot_nt(back, expand)
        out_acc[take, :] += dot_nt(hidden, reduce)
        current = coming
    bsum_ref[...] = sums
    if grads_too:
        total = dot_tn(far_ref[...], hid_ref[...]) + dot_tn(grad_ref[...], hidden_ref[...])
        dred_ref[...] = total.astype(jnp.bfloat16)

    @pl.when(step == pl.num_programs(0) - 1)
    def _():
        out_ref[...] = out_acc[...].astype(jnp.bfloat16)
        terms_ref[...] = terms_acc[...].astype(jnp.bfloat16)


def feed(second, grads, pack, bias, units, far=None):
    rows, width = second.shape
    block = 512 if units % 512 == 0 else units
    steps = units // block
    wide = pl.BlockSpec((rows, block), lambda j: (0, j))
    weights = [
        pl.BlockSpec((width, block), lambda j: (0, j)),
        pl.BlockSpec((width, block), lambda j: (0, j + steps)),
    ]
    line = pl.BlockSpec((1, block), lambda j: (0, j))
    hidden = jax.ShapeDtypeStruct((rows, units), jnp.bfloat16)
    full = jax.ShapeDtypeStruct((rows, width), jnp.bfloat16)
    outs = [hidden, jax.ShapeDtypeStruct((1, units), jnp.float32), full, full]
    out_specs = [wide, line, whole((rows, width)), whole((rows, width))]
    scratch = [pltpu.VMEM((rows, width), jnp.float32)] * 2
    in_specs = [whole((rows, width)), whole((rows, width)), *weights, line]
    if far is None:
        outs, out_specs = [hidden] + outs, [wide] + out_specs
    else:
        outs = outs + [jax.ShapeDtypeStruct((width, units), jnp.bfloat16)]
        out_specs = out_specs + [weights[0]]
        in_specs = in_specs + [whole((rows, width)), wide]
        scratch = scratch + [pltpu.VMEM((rows, block), jnp.bfloat16)]
    flops = (8 if far is None else 12) * rows * width * units
    return pl.pallas_call(
        functools.partial(feed_kernel, far is not None),
        out_shape=tuple(outs),
        grid=(steps,),
        in_specs=in_specs,
        out_specs=tuple(out_specs),
        scratch_shapes=scratch,
        compiler_params=kernel_params(),
        cost_estimate=cost(flops, 8 * rows * (units + width) + 4 * width * units, COSTS["feed"]),
        name="feed" if far is None else "feed_last",
    )(second, grads, pack, pack, bias, *(far or ()))


def head_grad_kernel(count, lo_ref, lt_ref, *refs):
    out_ref = refs[2 * count]
    offset = 0
    for own_ref, far_ref in zip(refs[:count], refs[count : 2 * count]):
        wide = own_ref.shape[1]
        total = dot_tn(lo_ref[...], own_ref[...]) + dot_tn(lt_ref[...], far_ref[...])
        lane = lax.broadcasted_iota(jnp.int32, (1, wide), 1)
        total = total * jnp.where(lane < wide // 3, HD ** (-0.5), 1.0)
        out_ref[:, offset : offset + wide] = total.astype(jnp.bfloat16)
        offset += wide


def head_grad(lefts, own, far):
    rows, width = lefts[0].shape
    units = sum(pack.shape[1] for pack in own)
    block = 256 if width % 256 == 0 else width
    left = pl.BlockSpec((rows, block), lambda j: (0, j))
    return pl.pallas_call(
        functools.partial(head_grad_kernel, len(own)),
        out_shape=jax.ShapeDtypeStruct((width, units), jnp.bfloat16),
        grid=(width // block,),
        in_specs=[left] * 2 + [whole(pack.shape) for pack in (*own, *far)],
        out_specs=pl.BlockSpec((block, units), lambda j: (j, 0)),
        compiler_params=kernel_params(),
        cost_estimate=cost(4 * rows * width * units, 4 * rows * (width + units) + 2 * width * units, COSTS["head_grad"]),
        name="head_grad",
    )(*lefts, *own, *far)


def branch_kernel(
    own_ref, far_ref, middle_ref, grad_ref, gain_ref, wo_ref, wt_ref,
    mgrad_ref, branch_ref, go_ref, gt_ref, sums_ref,
):
    rows, width = middle_ref.shape
    pieces = row_pieces(rows, 256)

    def step_back(piece):
        take = slice(piece[0], piece[0] + piece[1])
        second_grad = own_ref[take, :].astype(jnp.float32) + far_ref[take, :].astype(jnp.float32)
        normed, inverse = normalise(middle_ref[take, :])
        wide = grad_ref[take, :].astype(jnp.float32)
        moved = second_grad * normed
        tilted = second_grad * gain_ref[...]
        mgrad = wide + inverse * (
            tilted
            - jnp.mean(tilted, axis=-1, keepdims=True)
            - normed * jnp.mean(tilted * normed, axis=-1, keepdims=True)
        )
        branch = mgrad.astype(jnp.bfloat16)
        mgrad_ref[take, :] = mgrad
        branch_ref[take, :] = branch
        sums = [
            jnp.sum(moved, axis=0, keepdims=True),
            jnp.sum(second_grad, axis=0, keepdims=True),
            jnp.sum(branch.astype(jnp.float32), axis=0, keepdims=True),
            jnp.sum(wide, axis=0, keepdims=True),
        ]
        return branch, sums

    def finish(piece, branch):
        take = slice(piece[0], piece[0] + piece[1])
        go_ref[:, take] = dot_nn(branch, wo_ref[...]).astype(jnp.bfloat16).T
        gt_ref[:, take] = dot_nn(branch, wt_ref[...]).astype(jnp.bfloat16).T

    totals = None
    branch, sums = step_back(pieces[0])
    totals = sums
    for number, piece in enumerate(pieces):
        now = branch
        if number + 1 < len(pieces):
            branch, sums = step_back(pieces[number + 1])
            totals = [a + b for a, b in zip(totals, sums)]
        finish(piece, now)
    if go_ref.shape[1] > rows:
        blank = jnp.zeros((go_ref.shape[0], go_ref.shape[1] - rows), jnp.bfloat16)
        go_ref[:, rows:] = blank
        gt_ref[:, rows:] = blank
    for index, line in enumerate(totals):
        sums_ref[index : index + 1, :] = line


def branch_back(own, far, middle, grads, gain, pack, cols):
    rows, width = middle.shape
    full = whole((rows, width))
    return pl.pallas_call(
        branch_kernel,
        out_shape=(
            jax.ShapeDtypeStruct((rows, width), jnp.float32),
            jax.ShapeDtypeStruct((rows, width), jnp.bfloat16),
            jax.ShapeDtypeStruct((cols, lanes(rows)), jnp.bfloat16),
            jax.ShapeDtypeStruct((cols, lanes(rows)), jnp.bfloat16),
            jax.ShapeDtypeStruct((4, width), jnp.float32),
        ),
        grid=(1,),
        in_specs=[
            full, full, full, full, whole((1, width)), whole((width, cols), (0, 3)), whole((width, cols), (0, 4))
        ],
        out_specs=(full, full, whole((cols, lanes(rows))), whole((cols, lanes(rows))), whole((4, width))),
        compiler_params=kernel_params(),
        cost_estimate=cost(4 * rows * width * cols, 18 * rows * width, COSTS["branch_back"]),
        name="branch_back",
    )(own, far, middle, grads, gain, pack, pack)


def side_grad_kernel(
    so_ref, st_ref, bo_ref, bt_ref, branch_ref, co_ref, ct_ref, out_ref
):
    step = pl.program_id(0)
    last = pl.num_programs(0) - 1

    @pl.when(step < last - 1)
    def _():
        total = dot_tn(so_ref[...], bo_ref[...]) + dot_tn(st_ref[...], bt_ref[...])
        out_ref[...] = total.astype(jnp.bfloat16)

    @pl.when(step == last - 1)
    def _():
        out_ref[...] = dot_tn(branch_ref[...], co_ref[:, : branch_ref.shape[0]].T).astype(jnp.bfloat16)

    @pl.when(step == last)
    def _():
        out_ref[...] = dot_tn(branch_ref[...], ct_ref[:, : branch_ref.shape[0]].T).astype(jnp.bfloat16)


def side_grads(second, back, branch, contexts):
    rows, width = branch.shape
    units, cols = back[0].shape[1], contexts[0].shape[0]
    steps = units // cols
    part = pl.BlockSpec((rows, cols), lambda j: (0, jnp.minimum(j, steps - 1)))
    return pl.pallas_call(
        side_grad_kernel,
        out_shape=jax.ShapeDtypeStruct((width, units + 2 * cols), jnp.bfloat16),
        grid=(steps + 2,),
        in_specs=[whole((rows, width))] * 2 + [part] * 2
        + [whole((rows, width))] + [whole((cols, lanes(rows)))] * 2,
        out_specs=pl.BlockSpec((width, cols), lambda j: (0, j)),
        compiler_params=kernel_params(),
        cost_estimate=cost(4 * rows * width * (units + cols), 4 * rows * (width + units), COSTS["weight_grad"]),
        name="side_grads",
    )(*second, *back, branch, *contexts)


def first_kernel(count, *refs):
    packs, (weight_ref, frames_ref, terms_ref, sums_ref, bias_ref, pack_ref) = refs[:count], refs[count:]
    rows, width = frames_ref.shape
    cols = pack_ref.shape[1] // 3
    q_factor = HD ** (-0.5)
    pieces = row_pieces(rows, 256)
    offset = 0
    for ref in packs:
        wide = ref.shape[1] // 3
        for part in range(3):
            place = part * cols + offset
            pack_ref[:, place : place + wide] = ref[:, part * wide : (part + 1) * wide]
        offset += wide

    def begin(piece):
        take = slice(piece[0], piece[0] + piece[1])
        return dot_nt(pack_ref[take, :cols], weight_ref[:, :cols]) * q_factor + dot_nt(
            pack_ref[take, cols:], weight_ref[:, cols:]
        )

    totals = None
    current = begin(pieces[0])
    for number, piece in enumerate(pieces):
        coming = begin(pieces[number + 1]) if number + 1 < len(pieces) else None
        take = slice(piece[0], piece[0] + piece[1])
        terms_ref[take, :] = current.astype(jnp.bfloat16)
        normed, _ = normalise(frames_ref[take, :].astype(jnp.float32))
        sums = [
            jnp.sum(current * normed, axis=0, keepdims=True),
            jnp.sum(current, axis=0, keepdims=True),
            jnp.sum(pack_ref[take, :].astype(jnp.float32), axis=0, keepdims=True),
        ]
        totals = sums if totals is None else [a + b for a, b in zip(totals, sums)]
        current = coming
    sums_ref[0:1, :] = totals[0]
    sums_ref[1:2, :] = totals[1]
    bias_ref[...] = totals[2]


def first_back(packs, weights, frames):
    rows, width = frames.shape
    wide = sum(pack.shape[1] for pack in packs)
    return pl.pallas_call(
        functools.partial(first_kernel, len(packs)),
        out_shape=(
            jax.ShapeDtypeStruct((rows, width), jnp.bfloat16),
            jax.ShapeDtypeStruct((2, width), jnp.float32),
            jax.ShapeDtypeStruct((1, wide), jnp.float32),
        ),
        grid=(1,),
        in_specs=[whole(pack.shape) for pack in packs] + [whole((width, wide)), whole((rows, width))],
        out_specs=(whole((rows, width)), whole((2, width)), whole((1, wide))),
        scratch_shapes=[pltpu.VMEM((rows, wide), jnp.bfloat16)],
        compiler_params=kernel_params(),
        cost_estimate=cost(2 * rows * width * wide, 2 * (rows + width) * wide + 4 * rows * width, COSTS["first_back"]),
        name="first_back",
    )(*packs, weights, frames)


def frames_kernel(frames_ref, own_ref, far_ref, mgrad_ref, gain_ref, out_ref):
    normed, inverse = normalise(frames_ref[...].astype(jnp.float32))
    tilted = (own_ref[...].astype(jnp.float32) + far_ref[...].astype(jnp.float32)) * gain_ref[...]
    out_ref[...] = (
        mgrad_ref[...]
        + inverse
        * (
            tilted
            - jnp.mean(tilted, axis=-1, keepdims=True)
            - normed * jnp.mean(tilted * normed, axis=-1, keepdims=True)
        )
    ).astype(jnp.bfloat16)


def frames_back(frames, own, far, mgrad, gain):
    rows, width = frames.shape
    block = 376 if rows % 376 == 0 else rows
    spec = pl.BlockSpec((block, width), lambda i: (i, 0))
    return pl.pallas_call(
        frames_kernel,
        out_shape=jax.ShapeDtypeStruct((rows, width), jnp.bfloat16),
        grid=(rows // block,),
        in_specs=[spec] * 4 + [whole((1, width))],
        out_specs=spec,
        compiler_params=kernel_params(),
        cost_estimate=cost(20 * rows * width, 12 * rows * width, COSTS["frames_back"]),
        name="frames_back",
    )(frames, own, far, mgrad, gain)


def swap_tp(piece):
    return lax.ppermute(piece, "tp", [(0, 1), (1, 0)])


def tie(*values):
    return lax.optimization_barrier(values)


def gather_steps(vector, other, fsdp):
    index = lax.axis_index("fsdp")
    side = lax.axis_index("tp")
    held = jnp.where(side == 0, jnp.stack([vector, other]), jnp.stack([other, vector]))
    bit = 1
    while bit < fsdp:
        other = lax.ppermute(held, "fsdp", [(i, i ^ bit) for i in range(fsdp)])
        low = (index & bit) == 0
        held = jnp.where(low, jnp.concatenate([held, other]), jnp.concatenate([other, held]))
        bit *= 2
    return held


def halving_order(fsdp):
    return [bit for bit in (1, 2, 8, 4, 16, 32, 64, 128) if bit < fsdp]


def halve(held, bit, left, fsdp, last=False):
    index = lax.axis_index("fsdp")
    mine = (index // bit) % 2
    parts = held if isinstance(held, list) else [held]
    outer = 2 ** sorted(left, reverse=True).index(bit)
    views = [part.reshape(outer, 2, -1, part.shape[-1]) for part in parts]

    def chosen(which):
        return jnp.concatenate(
            [lax.dynamic_index_in_dim(view, which, 1, keepdims=False) for view in views], axis=-1
        )

    other = lax.ppermute(chosen(1 - mine), "fsdp", [(i, i ^ bit) for i in range(fsdp)])
    total = chosen(mine).astype(jnp.float32) + other.astype(jnp.float32)
    return (total if last else total.astype(jnp.bfloat16)).reshape(-1, total.shape[-1])


def per_device_pair(
    frames, out_grad, clip_lengths, clip_order, w_query, w_key, w_value, b_query, b_value,
    w_out, b_out, w_expand, b_expand, w_reduce, b_reduce,
    first_gain, first_shift, second_gain, second_shift, *, fsdp,
):
    side = lax.axis_index("tp")
    slot = lax.axis_index("fsdp")
    clip_count = clip_order.shape[0]
    every_clip = jnp.arange(clip_count, dtype=jnp.int32)
    clip_id = jnp.sum(jnp.where(every_clip == slot, clip_order, 0))
    length = jnp.sum(jnp.where(every_clip == clip_id, clip_lengths, 0))
    frames, out_grad = frames[0], out_grad[0]
    rows, width = frames.shape
    cols = w_query.shape[1]
    heads = cols // HD
    units = w_expand.shape[1]
    q_factor = HD ** (-0.5)
    scal_own = jnp.stack([length, side * rows]).astype(jnp.int32)
    scal_far = jnp.stack([length, (1 - side) * rows]).astype(jnp.int32)

    wide_six = [first_gain, first_shift, second_gain, second_shift, b_out, b_reduce]
    small_own = jnp.concatenate(wide_six + [b_query, b_value, b_expand])
    out_turned = w_out.T
    small_far, out_other = swap_tp(small_own), swap_tp(out_turned)
    pack_one = lax.all_gather(
        jnp.concatenate([w_query, w_key, w_value, out_turned, out_other], axis=1),
        "fsdp", axis=0, tiled=True,
    )
    pack_two = lax.all_gather(
        jnp.concatenate([w_expand, w_reduce.T], axis=1), "fsdp", axis=0, tiled=True
    )
    sent_frames, small_far, out_other = tie(frames, small_far, out_other)
    frames_far = swap_tp(sent_frames)
    sent_grads, frames_far = tie(out_grad, frames_far)
    grads_far = swap_tp(sent_grads)
    small = gather_steps(small_own, small_far, fsdp)
    lot = first_gain.shape[0]
    whole_six = small[:, : 6 * lot].astype(jnp.float32).reshape(2 * fsdp, 6, lot)
    whole_six = whole_six.transpose(1, 0, 2).reshape(6, 1, width)
    gain_one, shift_one, gain_two, shift_two, out_bias, reduce_bias = [whole_six[i] for i in range(6)]
    mine = lax.dynamic_index_in_dim(
        small[:, 6 * lot :].astype(jnp.float32).reshape(fsdp, 2, -1), side, axis=1, keepdims=False
    )
    part = b_query.shape[0]
    bias_q = mine[:, :part].reshape(1, -1)
    bias_v = mine[:, part : 2 * part].reshape(1, -1)
    bias_e = mine[:, 2 * part :].reshape(1, -1)

    first_own, q_own, k_own, v_own = project(
        scal_own, frames, gain_one, shift_one, pack_one, bias_q, bias_v, heads
    )
    first_far, q_far, k_far, v_far = project(
        scal_far, frames_far, gain_one, shift_one, pack_one, bias_q, bias_v, heads
    )
    context_send, log_far = attend_rows(q_far, k_own, k_far, v_own, v_far)
    context_send, q_own = tie(context_send, q_own)
    context_far = swap_tp(context_send.reshape(cols, -1))
    context_own, log_own = attend_rows(q_own, k_own, k_far, v_own, v_far)
    context_own = context_own.reshape(cols, -1)
    middle, second_own = merge_heads(
        context_own, context_far, pack_one, frames, out_bias, gain_two, shift_two
    )

    second_far = swap_tp(second_own)
    hid_far, back_far, bsum_far, out_send, terms_send = feed(
        second_far, grads_far, pack_two, bias_e, units
    )
    terms_send, second_own = tie(terms_send, second_own)
    terms_far = swap_tp(terms_send)
    back_own, bsum_own, out_own, terms_own, d_reduce = feed(
        second_own, out_grad, pack_two, bias_e, units, (grads_far, hid_far)
    )
    g_reduce = lax.psum_scatter(d_reduce, "fsdp", scatter_dimension=0, tiled=True)
    mgrad, branch, up_own, up_send, sums_two = branch_back(
        terms_own, terms_far, middle, out_grad, gain_two, pack_one, cols
    )
    up_send, second_own = tie(up_send, second_own)
    up_far = swap_tp(up_send)
    d_side = side_grads(
        (second_own, second_far), (back_own, back_far), branch, (context_own, context_far)
    )

    turned = (heads, HD, lanes(rows))
    up_far, out_send, d_side = tie(up_far, out_send, d_side)
    out_far = swap_tp(out_send)
    ups = (up_own.reshape(turned), up_far.reshape(turned))
    steps = halving_order(fsdp)
    firsts = (first_own, first_far)

    def back(q_first, start, count):
        return attend_back_rows(
            (q_first, q_far), (k_own, k_far), (v_own, v_far), ups, (log_own, log_far), start, count
        )

    many = (heads + 1) // 2
    own_a, far_a = back(q_own, 0, many)
    own_a, d_side = tie(own_a, d_side)
    g_side = lax.psum_scatter(d_side, "fsdp", scatter_dimension=0, tiled=True)
    d_heads = head_grad(firsts, [own_a], [far_a])
    held_a = halve(d_heads, steps[0], steps, fsdp)
    held_a, q_own = tie(held_a, q_own)
    own_b, far_b = back(q_own, many, heads - many)
    far_b, out_far = tie(far_b, out_far)
    held_a = halve(held_a, steps[1], steps[1:], fsdp)
    held_a, far_b = tie(held_a, far_b)
    first_send, sums_far, bias_far = first_back([far_a, far_b], pack_one, frames_far)
    first_send, far_b = tie(first_send, far_b)
    first_recv = swap_tp(first_send)
    held_b = head_grad(firsts, [own_b], [far_b])
    held_b, own_b = tie(held_b, own_b)
    first_keep, sums_own, bias_own = first_back([own_a, own_b], pack_one, frames)
    held_a = halve(held_a, steps[2], steps[2:], fsdp, len(steps) == 3)
    sums_one = sums_own + sums_far
    bias_sum = bias_own + bias_far
    wide_sums = jnp.concatenate([sums_one, sums_two])
    wide_sums = wide_sums.reshape(6, fsdp, 2, lot).transpose(1, 2, 0, 3).reshape(fsdp, 12 * lot)
    tall = jnp.concatenate(
        [
            wide_sums,
            (bias_sum[:, :cols] * q_factor).reshape(fsdp, -1),
            bias_sum[:, 2 * cols :].reshape(fsdp, -1),
            (bsum_own + bsum_far).reshape(fsdp, -1),
        ],
        axis=1,
    )
    wide = held_b.shape[1]
    extra = -(-tall.shape[1] // (8 * wide)) * 8
    tall = jnp.pad(tall, ((0, 0), (0, extra * wide - tall.shape[1]))).astype(jnp.bfloat16)
    lots = width // fsdp
    held_b = jnp.concatenate(
        [held_b.reshape(fsdp, lots, wide), tall.reshape(fsdp, extra, wide)], axis=1
    ).reshape(-1, wide)
    held_b = halve(held_b, steps[0], steps, fsdp)
    held_b = halve(held_b, steps[1], steps[1:], fsdp)
    out_frames = (
        middle + out_own.astype(jnp.float32) + out_far.astype(jnp.float32) + reduce_bias
    ).astype(jnp.bfloat16)
    for place in range(2, len(steps)):
        last = place + 1 == len(steps)
        if place > 2:
            held_a, held_b = tie(held_a, held_b)
            held_a = halve(held_a, steps[place], steps[place:], fsdp, last)
        if last:
            held_b, first_keep, out_frames = tie(held_b, first_keep, out_frames)
            frames_grad = frames_back(frames, first_keep, first_recv, mgrad, gain_one)
            held_b, frames_grad, g_side = tie(held_b, frames_grad, g_side)
        held_b = halve(held_b, steps[place], steps[place:], fsdp, last)
    held_b, small_sum = held_b[:lots], held_b[lots:].reshape(-1)
    g_expand, g_out = g_side[:, :units], g_side[:, units:]
    some = many * HD

    def joined(kind):
        rest = cols - some
        return jnp.concatenate(
            [held_a[:, kind * some : (kind + 1) * some], held_b[:, kind * rest : (kind + 1) * rest]], axis=1
        )

    g_query, g_key, g_value = joined(0), joined(1), joined(2)

    six = small_sum[: 12 * lot].reshape(2, 6 * lot)
    keep = lax.dynamic_index_in_dim(six, side, 0, keepdims=False)
    send = lax.dynamic_index_in_dim(six, 1 - side, 0, keepdims=False)
    six = (keep + swap_tp(send)).reshape(6, lot)
    rest = small_sum[12 * lot :]
    g_bq, g_bv = rest[:part], rest[part : 2 * part]
    g_be = rest[2 * part : 2 * part + b_expand.shape[0]]
    g_out_sum = g_out[:, :cols].astype(jnp.float32) + swap_tp(g_out[:, cols:]).astype(jnp.float32)
    return (
        out_frames[None],
        frames_grad[None],
        g_query,
        g_key,
        g_value,
        g_bq,
        g_bv,
        g_out_sum.T,
        six[4],
        g_expand.astype(jnp.float32),
        g_be,
        g_reduce.T.astype(jnp.float32),
        six[5],
        six[0],
        six[1],
        six[2],
        six[3],
    )


def solution(mesh):
    fsdp = mesh.shape["fsdp"]
    if mesh.shape["tp"] == 2 and fsdp & (fsdp - 1) == 0:

        def body(*args):
            return per_device_pair(*args, fsdp=fsdp) if args[0].shape[0] == 1 else per_device(*args)
    else:
        body = per_device
    return jax.shard_map(
        body,
        mesh=mesh,
        in_specs=(
            P("fsdp", "tp", None),
            P("fsdp", "tp", None),
            P(),
            P(),
            P("fsdp", "tp"),
            P("fsdp", "tp"),
            P("fsdp", "tp"),
            P(("tp", "fsdp")),
            P(("tp", "fsdp")),
            P("tp", "fsdp"),
            P(("fsdp", "tp")),
            P("fsdp", "tp"),
            P(("tp", "fsdp")),
            P("tp", "fsdp"),
            P(("fsdp", "tp")),
            P(("fsdp", "tp")),
            P(("fsdp", "tp")),
            P(("fsdp", "tp")),
            P(("fsdp", "tp")),
        ),
        out_specs=(
            P("fsdp", "tp", None),
            P("fsdp", "tp", None),
            P("fsdp", "tp"),
            P("fsdp", "tp"),
            P("fsdp", "tp"),
            P(("tp", "fsdp")),
            P(("tp", "fsdp")),
            P("tp", "fsdp"),
            P(("fsdp", "tp")),
            P("fsdp", "tp"),
            P(("tp", "fsdp")),
            P("tp", "fsdp"),
            P(("fsdp", "tp")),
            P(("fsdp", "tp")),
            P(("fsdp", "tp")),
            P(("fsdp", "tp")),
            P(("fsdp", "tp")),
        ),
        check_vma=False,
    )
```
